256 devices in a mesh: dom: 64 (over y, z, core), rep: 4 (over x).
Axes of the slice: x: 4, y: 4, z: 8, core: 2. Of those that a mesh axis runs over, the one named last changes fastest.
Arguments:
- inflow_pressure: float32 [32, 262144], P('rep', 'dom'), may hold values from -6 to 6
- inflow_mask: int32 [262144], P('dom'), may hold values 0 or 1
- seg_ends: int32 [2, 458752], P(None, 'dom'), may hold values from 0 to 4095, as said below
- live_counts: int32 [64], P('dom'), may hold values from 3072 to 6144, as said below
- shown_blocks: int32 [512], P('dom'), may hold values from 0 to 31, as said below
- radius: float32 [458752], P('dom'), may hold values from 3 to 6
- seg_length: float32 [458752], P('dom'), may hold values from 20 to 100
Outputs:
- pressure: float32 [32, 262144], P('rep', 'dom')
- mean_pressure: float32 [262144], P('dom')
The draws below stay inside these ranges and needn't reach their ends.
Inputs may be any that keep to these rules, and one draw needn't show every extreme that they name: `seg_ends`: row 0 holds local node ids; for inner slots row 1 holds a local node id different from row 0, for junction slots a slot of the upper partition below 1024. `live_counts`: some partition has all inner slots live. `shown_blocks`: distinct within each partition.
All inputs are finite; a program needn't handle non-finite values. No bound on the sum of `inflow_mask` on one device may be relied on, other than what follows from the above.
Results may differ from the reference program's by a relative error of at most 0.0018.
Values may be sent and summed in bfloat16 or wider, within the bound.
A program may use at most 64 MiB of HBM per device.

```python
import math
import jax
import jax.numpy as jnp
from jax import lax

TILE_NODES = 128
BLOCKS_DEV = 32
SCENARIOS = 32
ITERATIONS = 3
NODES_DEV = 4096
SHOWN_BLOCKS = 8
JUNCTIONS = 1024
INNER_SEGS = 6144
SEGS_DEV = 7168
NODES = 262144
SEGMENTS = 458752


def draw_seg_ends(key, part):
    parts = SEGMENTS // SEGS_DEV
    heads = jax.random.randint(jax.random.fold_in(key, 11), (parts, SEGS_DEV), 0, NODES_DEV)
    near_offset = jax.random.randint(jax.random.fold_in(key, 12), (parts, INNER_SEGS), 1, 160)
    far_offset = jax.random.randint(jax.random.fold_in(key, 14), (parts, INNER_SEGS), 1, NODES_DEV)
    selector = jax.random.randint(jax.random.fold_in(key, 15), (parts, INNER_SEGS), 0, 8)
    offset = jnp.where(selector == 0, far_offset, near_offset)
    inner_tails = (heads[:, :INNER_SEGS] + offset) % NODES_DEV
    slots = jax.random.randint(jax.random.fold_in(key, 13), (parts, JUNCTIONS), 0, JUNCTIONS)
    tails = jnp.concatenate([inner_tails, slots], axis=1)
    return jnp.stack([heads, tails]).reshape(2, SEGMENTS).astype(jnp.int32)


def draw_live_counts(key, part):
    parts = SEGMENTS // SEGS_DEV
    counts = jax.random.randint(jax.random.fold_in(key, 21), (parts,), INNER_SEGS // 2, INNER_SEGS + 1)
    full = jax.random.randint(jax.random.fold_in(key, 22), (), 0, parts)
    counts = jnp.where(jnp.arange(parts) == full, INNER_SEGS, counts)
    return counts.astype(jnp.int32)


def draw_shown_blocks(key, part):
    parts = SEGMENTS // SEGS_DEV
    keys = jax.random.split(jax.random.fold_in(key, 31), parts)

    def pick(single):
        return jax.random.permutation(single, BLOCKS_DEV)[:SHOWN_BLOCKS]
    return jax.vmap(pick)(keys).reshape(-1).astype(jnp.int32)


def plant(array, rng, least, high):
    index_at = [jax.random.randint(jax.random.fold_in(rng, axis), (), 0, length) for axis, length in enumerate(array.shape)]
    longest = array.shape.index(max(array.shape))
    next_to = index_at[:longest] + [(index_at[longest] + 1) % array.shape[longest]] + index_at[longest + 1:]
    return array.at[tuple(index_at)].set(least).at[tuple(next_to)].set(high)


def shard_levels(rng, shape, pieces, least, largest):
    level = 1.0
    for dim, shards_of in pieces:
        draws = jax.random.uniform(jax.random.fold_in(jax.random.fold_in(rng, 6), dim), (shards_of,), jnp.float32, least / len(pieces), largest / len(pieces))
        level = level * jnp.repeat(jnp.exp(draws), shape[dim] // shards_of).reshape((-1,) + (1,) * (len(shape) - 1 - dim))
    return level


def centred(own_key, dims, spread, limit, cuts=(), held_as=jnp.bfloat16):
    drawn = jax.random.normal(own_key, dims, jnp.float32) * spread
    if len(cuts) > 0:
        drawn = shard_levels(own_key, dims, cuts, -0.22, 0.18) * drawn
    return jnp.clip(drawn, min=-limit, max=limit).astype(held_as)


def setup_inputs(seed: int = 0) -> dict:
    seeds = jax.random.split(jax.random.key(seed), 8)
    inflow_pressure = centred(seeds[0], (SCENARIOS, NODES), 1.0, 6.0, ((0, 4), (1, 64)), jnp.float32)
    inflow_mask = plant((jax.random.randint(seeds[1], (NODES,), 0, 16) < 1).astype(jnp.int32), jax.random.fold_in(seeds[1], 1), 0, 1)
    seg_ends = draw_seg_ends(jax.random.fold_in(seeds[7], 71), 0)
    live_counts = draw_live_counts(jax.random.fold_in(seeds[7], 71), 0)
    shown_blocks = draw_shown_blocks(jax.random.fold_in(seeds[7], 71), 0)
    radius = jnp.clip(jnp.exp(math.log(6.0) - 0.6931472 * jax.random.uniform(seeds[5], (SEGMENTS,), jnp.float32) ** shard_levels(seeds[5], (SEGMENTS,), ((0, 64),), -0.2, 0.2)), 3.0, 6.0)
    seg_length = jnp.clip(jnp.exp(math.log(100.0) - 1.609438 * jax.random.uniform(seeds[6], (SEGMENTS,), jnp.float32) ** shard_levels(seeds[6], (SEGMENTS,), ((0, 64),), -0.2, 0.2)), 20.0, 100.0)
    return {"inflow_pressure": inflow_pressure, "inflow_mask": inflow_mask, "seg_ends": seg_ends, "live_counts": live_counts, "shown_blocks": shown_blocks, "radius": radius, "seg_length": seg_length}


leak_rate = 0.05
inflow_weight = 20.0

def conductance(radius, seg_length):
    diameter = 2.0 * radius
    viscous = 220.0 * jnp.exp(-1.3 * diameter) + 3.2 - 2.44 * jnp.exp(-0.06 * diameter ** 0.645)
    return (diameter / 8.0) ** 4 * (50.0 / seg_length) / viscous

def block_inverses(head, tail, weight, degree, first, count):
    group = math.gcd(count, 32)
    same = head // TILE_NODES == tail // TILE_NODES
    weight = jnp.where(same, weight, 0.0)
    row = head % TILE_NODES
    column = tail % TILE_NODES
    owner = head // TILE_NODES
    diag_tiles = degree.reshape(-1, TILE_NODES)
    unit = jnp.eye(TILE_NODES, dtype=jnp.float32)

    def one_group(start):
        local = owner - start
        inside = (local >= 0) & (local < group)
        safe = jnp.where(inside, local, 0).astype(jnp.int32)
        taken = jnp.where(inside, weight, 0.0)
        flat_one = (safe * TILE_NODES + row) * TILE_NODES + column
        flat_two = (safe * TILE_NODES + column) * TILE_NODES + row
        tiles = jnp.zeros(group * TILE_NODES * TILE_NODES, jnp.float32)
        tiles = tiles.at[flat_one].add(-taken).at[flat_two].add(-taken)
        tiles = tiles.reshape(group, TILE_NODES, TILE_NODES)
        diagonal = lax.dynamic_slice_in_dim(diag_tiles, start, group, 0)
        tiles = tiles + diagonal[:, :, None] * unit
        factor = jnp.linalg.cholesky(tiles)
        inverse = jax.scipy.linalg.cho_solve((factor, True), jnp.broadcast_to(unit, tiles.shape))
        return inverse.astype(jnp.bfloat16)
    starts = (first + jnp.arange(count // group, dtype=jnp.int32) * group).astype(jnp.int32)
    return lax.map(one_group, starts).reshape(count, TILE_NODES, TILE_NODES)

def reference(inflow_pressure, inflow_mask, seg_ends, live_counts, shown_blocks, radius, seg_length):
    parts = live_counts.shape[0]
    nodes = parts * NODES_DEV
    cond = conductance(radius, seg_length).reshape(parts, SEGS_DEV)
    ends = seg_ends.reshape(2, parts, SEGS_DEV)
    position = jnp.arange(SEGS_DEV, dtype=jnp.int32)
    index = jnp.arange(parts, dtype=jnp.int32)
    live = jnp.where(position[None, :] < INNER_SEGS, position[None, :] < live_counts[:, None], (index < parts - 1)[:, None])
    cond = jnp.where(live, cond, 0.0)
    offsets = (index * NODES_DEV)[:, None]
    inner_head = ends[0, :, :INNER_SEGS]
    inner_tail = ends[1, :, :INNER_SEGS]
    inner_cond = cond[:, :INNER_SEGS]
    junc_cond = cond[:, INNER_SEGS:]
    junc_head = ends[0, :, INNER_SEGS:] + offsets
    slots = ends[1, :, INNER_SEGS:]
    upper_lists = jnp.roll(shown_blocks.reshape(parts, SHOWN_BLOCKS), -1, axis=0)
    upper_node = jnp.take_along_axis(upper_lists, slots // TILE_NODES, axis=1) * TILE_NODES + slots % TILE_NODES
    junc_tail = ((upper_node + offsets + NODES_DEV) % nodes).astype(jnp.int32)
    heads = jnp.concatenate([(inner_head + offsets).reshape(-1), junc_head.reshape(-1)]).astype(jnp.int32)
    tails = jnp.concatenate([(inner_tail + offsets).reshape(-1), junc_tail.reshape(-1)]).astype(jnp.int32)
    conds = jnp.concatenate([inner_cond.reshape(-1), junc_cond.reshape(-1)])
    extra = leak_rate + inflow_weight * inflow_mask.astype(jnp.float32)
    degree = jnp.zeros(nodes, jnp.float32).at[heads].add(conds).at[tails].add(conds) + extra

    def invert_part(items):
        return block_inverses(items[0], items[1], items[2], items[3], 0, BLOCKS_DEV)
    inverse = lax.map(invert_part, (inner_head, inner_tail, inner_cond, degree.reshape(parts, NODES_DEV)))
    inverse = inverse.reshape(-1, TILE_NODES, TILE_NODES).astype(jnp.float32)
    scen = inflow_pressure.shape[0]

    def operate(field):
        flow = conds * (field[:, heads] - field[:, tails])
        out = extra * field
        return out.at[:, heads].add(flow).at[:, tails].add(-flow)

    def precond(field):
        rounded = field.astype(jnp.bfloat16)
        rounded = lax.optimization_barrier(rounded).astype(jnp.float32)
        blocks = rounded.reshape(scen, -1, TILE_NODES)
        return jnp.einsum('bij,sbj->sbi', inverse, blocks).reshape(scen, nodes)
    rhs = inflow_weight * inflow_mask.astype(jnp.float32)[None, :] * inflow_pressure
    pressure = jnp.zeros_like(rhs)
    residual = rhs
    z_field = precond(residual)
    direction = z_field
    rz_now = jnp.sum(residual * z_field, axis=1)
    for step in range(ITERATIONS):
        image = operate(direction)
        alpha = rz_now / jnp.sum(direction * image, axis=1)
        pressure = pressure + alpha[:, None] * direction
        residual = residual - alpha[:, None] * image
        if step + 1 < ITERATIONS:
            z_field = precond(residual)
            rz_next = jnp.sum(residual * z_field, axis=1)
            direction = z_field + (rz_next / rz_now)[:, None] * direction
            rz_now = rz_next
    mean_pressure = jnp.sum(pressure, axis=0) / SCENARIOS
    return (pressure, mean_pressure)
```

```python
import functools

import jax
import jax.numpy as jnp
from jax import lax
from jax.experimental import pallas as pl
from jax.experimental.pallas import tpu as pltpu
from jax.sharding import PartitionSpec as P

MESH = pl.DeviceIdType.MESH
F32 = jnp.float32
BF16 = jnp.bfloat16
I32 = jnp.int32

TILE = 128
BLOCKS = 32
NODES = 4096
SCEN_ALL = 32
JUNC = 1024
INNER = 6144
SEGS = 7168
SHOWN = 8
CHUNKS = 80
PANEL = 16
GROUP = 16

leak_rate = 0.05
inflow_weight = 20.0


def dot_nt(a, b):
    return lax.dot_general(a, b, (((1,), (1,)), ((), ())), preferred_element_type=F32)


def dot_nn(a, b):
    return lax.dot_general(a, b, (((1,), (0,)), ((), ())), preferred_element_type=F32)


def dot_tn(a, b):
    return lax.dot_general(a, b, (((0,), (0,)), ((), ())), preferred_element_type=F32)


def parts2(x):
    hi = x.astype(BF16).astype(F32)
    return hi, x - hi


def parts3(x):
    hi = x.astype(BF16).astype(F32)
    rest = x - hi
    mid = rest.astype(BF16).astype(F32)
    return hi, mid, rest - mid


def one_hot_rows(row, count):
    ids = lax.broadcasted_iota(I32, (count, row.shape[1]), 0)
    return ids == row


def spread(mask, value):
    return jnp.where(mask, value, 0.0).astype(BF16)


def conductance(radius, seg_length):
    diameter = 2.0 * radius
    power = jnp.exp(0.645 * jnp.log(diameter))
    viscous = 220.0 * jnp.exp(-1.3 * diameter) + 3.2 - 2.44 * jnp.exp(-0.06 * power)
    scaled = diameter * 0.125
    scaled = scaled * scaled
    return scaled * scaled * (50.0 / seg_length) / viscous


def head_kernel(parts, ends, radius, length, live, cond_out, arrived, sent, landed, send_sem, recv_sem):
    place = lax.axis_index("dom")
    upper = lax.rem(place + 1, parts)
    lower = lax.rem(place + parts - 1, parts)
    barrier = pltpu.get_barrier_semaphore()
    for other in (upper, lower):
        pl.semaphore_signal(barrier, inc=1, device_id={"dom": other}, device_id_type=MESH)
    cond = conductance(radius[...], length[...])
    position = lax.broadcasted_iota(I32, (1, SEGS), 1)
    limit = jnp.where(position < INNER, jnp.full((1, SEGS), live[0], I32), jnp.full((1, SEGS), (parts - 1 - place) * SEGS, I32))
    cond = jnp.where(position < limit, cond, 0.0)
    cond_out[...] = cond
    slot = ends[1:2, INNER:]
    junc = cond[:, INNER:]
    owner = one_hot_rows(slot >> 7, SHOWN)
    stack = jnp.concatenate([jnp.where(owner, part, 0.0) for part in parts3(junc)], axis=0).astype(BF16)
    lanes = spread(one_hot_rows(slot & 127, TILE), 1.0)
    sums = dot_nt(stack, lanes)
    sent[...] = sums[0:8] + sums[8:16] + sums[16:24]
    pl.semaphore_wait(barrier, 2)
    copy = pltpu.make_async_remote_copy(
        src_ref=sent, dst_ref=landed, send_sem=send_sem, recv_sem=recv_sem, device_id={"dom": upper}, device_id_type=MESH
    )
    copy.start()
    copy.wait()
    arrived[...] = landed[...]


def setup_kernel(
    ends, cond, mask, shown, arrived, inverse, degree_out, table, rank, degree, sums, packed, counts, counts_smem, sem
):
    degree[...] = jnp.zeros_like(degree)
    sums[...] = jnp.zeros_like(sums)
    width = 256
    before = lax.broadcasted_iota(I32, (width, width), 0) < lax.broadcasted_iota(I32, (width, width), 1)
    before = jnp.where(before, 1.0, 0.0).astype(BF16)

    def add_degree(node, value):
        owner = one_hot_rows(node >> 7, BLOCKS)
        stack = jnp.concatenate([jnp.where(owner, part, 0.0) for part in parts3(value)], axis=0).astype(BF16)
        lanes = spread(one_hot_rows(node & 127, TILE), 1.0)
        degree[...] += dot_nt(stack, lanes)

    def scan(step, carry):
        cols = pl.ds(pl.multiple_of(step * width, width), width)
        head = ends[0:1, cols]
        tail = ends[1:2, cols]
        value = cond[:, cols]
        add_degree(head, value)
        add_degree(tail, value)
        bucket = jnp.where((head >> 7) == (tail >> 7), head >> 7, -1)
        member = one_hot_rows(bucket, BLOCKS)
        ahead = dot_nn(spread(member, 1.0), before)
        rank[:, cols] = jnp.sum(jnp.where(member, ahead + carry, 0.0), axis=0, keepdims=True)
        return carry + jnp.sum(jnp.where(member, 1.0, 0.0), axis=1, keepdims=True)

    total = lax.fori_loop(0, INNER // width, scan, jnp.zeros((BLOCKS, 1), F32))
    add_degree(ends[0:1, INNER:], cond[:, INNER:])
    deg = degree[0:32, :] + degree[32:64, :] + degree[64:96, :]
    block_id = lax.broadcasted_iota(I32, (BLOCKS, TILE), 0)
    for j in range(SHOWN):
        deg = deg + jnp.where(block_id == shown[j], arrived[j : j + 1, :], 0.0)
    deg = deg + (leak_rate + inflow_weight * mask[...].astype(F32))
    degree_out[...] = deg

    chunks = jnp.floor((jnp.broadcast_to(total, (BLOCKS, TILE)) + 127.0) * (1.0 / 128.0))
    below = lax.broadcasted_iota(I32, (BLOCKS, BLOCKS), 1) < lax.broadcasted_iota(I32, (BLOCKS, BLOCKS), 0)
    start = dot_nn(jnp.where(below, 1.0, 0.0).astype(BF16), chunks.astype(BF16))
    counts[0:32, :] = start.astype(I32)
    counts[32:64, :] = chunks.astype(I32)
    to_scalar = pltpu.make_async_copy(counts, counts_smem, sem)
    to_scalar.start()
    start_column = start[:, 0:1]
    wide = 512

    def compact(step, carry):
        cols = pl.ds(pl.multiple_of(step * wide, wide), wide)
        head = ends[0:1, cols]
        tail = ends[1:2, cols]
        inside = (head >> 7) == (tail >> 7)
        bucket = jnp.where(inside, head >> 7, -1)
        base = jnp.sum(jnp.where(one_hot_rows(bucket, BLOCKS), start_column, 0.0), axis=0, keepdims=True)
        order = rank[:, cols].astype(I32)
        chunk = jnp.where(inside, base.astype(I32) + (order >> 7), -1)
        at_chunk = one_hot_rows(chunk, CHUNKS)
        values = ((head & 127).astype(F32), (tail & 127).astype(F32)) + parts3(cond[:, cols])
        stack = jnp.concatenate([spread(at_chunk, value) for value in values], axis=0)
        lanes = spread(one_hot_rows(order & 127, TILE), 1.0)
        sums[...] += dot_nt(stack, lanes)
        return carry

    lax.fori_loop(0, INNER // wide, compact, 0)
    packed[...] = sums[...]
    to_scalar.wait()

    row_id = lax.broadcasted_iota(I32, (TILE, TILE), 0)
    lane_id = lax.broadcasted_iota(I32, (TILE, TILE), 1)

    def fill(block, carry):
        first = counts_smem[block, 0]
        count = counts_smem[block + BLOCKS, 0]

        def add_chunk(index, acc):
            row = first + index
            head = packed[pl.ds(row, 1), :].astype(I32)
            tail = packed[pl.ds(row + CHUNKS, 1), :].astype(I32)
            at_head = row_id == head
            at_tail = row_id == tail
            left = jnp.concatenate([spread(at_head, 1.0), spread(at_tail, 1.0)], axis=1)
            for k in range(3):
                value = packed[pl.ds(row + (2 + k) * CHUNKS, 1), :]
                right = jnp.concatenate([spread(at_tail, value), spread(at_head, value)], axis=1)
                acc = acc + dot_nt(left, right)
            return acc

        acc = lax.fori_loop(0, count, add_chunk, jnp.zeros((TILE, TILE), F32))
        table[block] = jnp.where(row_id == lane_id, degree_out[pl.ds(block, 1), :], -acc)
        return carry

    lax.fori_loop(0, BLOCKS, fill, 0)

    lane16 = lax.broadcasted_iota(I32, (PANEL, TILE), 1)
    row16 = lax.broadcasted_iota(I32, (PANEL, TILE), 0)

    def panel(index, carry):
        base = pl.multiple_of(index * PANEL, PANEL)
        rows = pl.ds(base, PANEL)
        in_panel = (lane_id >= base) & (lane_id < base + PANEL)

        def group(number, inner):
            blocks = [number * GROUP + i for i in range(GROUP)]
            turned = [pltpu.roll(table[b, rows, :], TILE - base, 1) for b in blocks]
            for t in range(PANEL):
                for i in range(GROUP):
                    x = turned[i]
                    pivot = 1.0 / x[t : t + 1, t : t + 1]
                    row = jnp.where(lane16[0:1] == t, pivot, x[t : t + 1, :] * pivot)
                    rest = jnp.where(lane16 == t, 0.0, x) - x[:, t : t + 1] * row
                    turned[i] = jnp.where(row16 == t, row, rest)
            for i, b in enumerate(blocks):
                old = table[b, rows, :]
                new = pltpu.roll(turned[i], base, 1)
                old = jnp.where(lane16 < base, -old, old)
                oh, om, ol = [part.astype(BF16) for part in parts3(old)]
                nh, nm, nl = [part.astype(BF16) for part in parts3(new)]
                left = jnp.concatenate([oh, oh, om, oh, ol, om], axis=0)
                right = jnp.concatenate([nh, nm, nh, nl, nh, nm], axis=0)
                update = dot_tn(left, right)
                table[b] = jnp.where(in_panel, 0.0, table[b]) - update
                table[b, rows, :] = new
            return inner

        lax.fori_loop(0, BLOCKS // GROUP, group, 0)
        return carry

    lax.fori_loop(0, TILE // PANEL, panel, 0)

    def finish(block, carry):
        inverse[block] = table[block].astype(BF16)
        return carry

    lax.fori_loop(0, BLOCKS, finish, 0)


def solve_kernel(
    sizes, inflow, mask, ends, cond, degree, inverse, shown, pressure, mean,
    table, owner8, cond8, basis, images, residual, pair, upper_pair, out, back_out, gathered, fwd_out, fwd_in, back_src, back_in,
    one_buf, two_buf, rep_buf,
    fwd_send, fwd_recv, back_send, back_recv, one_send, one_recv, two_send, two_recv, rep_send, rep_recv,
):
    parts, depth_z, planes, reps = sizes
    place = lax.axis_index("dom")
    mine = lax.axis_index("rep")
    upper = lax.rem(place + 1, parts)
    lower = lax.rem(place + parts - 1, parts)
    core = lax.rem(place, 2)
    column = lax.rem(place // 2, depth_z)
    line = place // (2 * depth_z)
    seat = line * 2 + core

    def plane_place(other):
        return ((other // 2) * depth_z + column) * 2 + lax.rem(other, 2)

    def column_place(other):
        return (line * depth_z + other) * 2 + core

    barrier = pltpu.get_barrier_semaphore()
    partners = [{"dom": upper}, {"dom": lower}]
    partners += [{"dom": plane_place(lax.rem(seat + o, planes))} for o in range(1, planes)]
    partners += [{"dom": column_place(lax.rem(column + o, depth_z))} for o in range(1, depth_z)]
    partners += [{"rep": lax.rem(mine + o, reps)} for o in range(1, reps)]
    for partner in partners:
        pl.semaphore_signal(barrier, inc=1, device_id=partner, device_id_type=MESH)

    wide = 256

    def make(step, carry):
        cols = pl.ds(pl.multiple_of(step * wide, wide), wide)
        value = jnp.broadcast_to(cond[:, cols], (8, wide))
        cond8[:, cols] = value
        for side in range(2):
            node = ends[side : side + 1, cols]
            into = pl.ds(pl.multiple_of(side * SEGS + step * wide, wide), wide)
            table[:, into] = spread(one_hot_rows(node & 127, TILE), 1.0)
            owner8[:, into] = jnp.broadcast_to(node >> 7, (8, wide))
        return carry

    lax.fori_loop(0, SEGS // wide, make, 0)

    def split_into(target, value):
        hi, lo = parts2(value)
        target[:, 0:TILE] = hi.astype(BF16)
        target[:, TILE:] = lo.astype(BF16)

    def gather(source, cols, blocks):
        lanes = table[:, cols]
        full = dot_nn(source[...], jnp.concatenate([lanes, lanes], axis=0))
        owner = owner8[:, cols]
        result = jnp.zeros((8, wide), F32)
        for b in range(blocks):
            result = jnp.where(owner == b, full[8 * b : 8 * b + 8, :], result)
        return result

    def scatter(value, cols, blocks):
        owner = owner8[:, cols]
        hi, lo = parts2(value)
        left = [jnp.concatenate([jnp.where(owner == b, part, 0.0) for b in range(blocks)], axis=0).astype(BF16) for part in (hi, lo)]
        lanes = table[:, cols]
        return dot_nt(jnp.concatenate(left, axis=1), jnp.concatenate([lanes, lanes], axis=1))

    def head_cols(step):
        return pl.ds(pl.multiple_of(step * wide, wide), wide)

    def tail_cols(step):
        return pl.ds(pl.multiple_of(SEGS + step * wide, wide), wide)

    def precondition(k):
        for b in range(BLOCKS):
            field = residual[8 * b : 8 * b + 8, :].astype(BF16)
            basis[k, 8 * b : 8 * b + 8, :] = dot_nn(field, inverse[b])

    for b in range(BLOCKS):
        weight = inflow_weight * mask[b : b + 1, :].astype(F32)
        residual[8 * b : 8 * b + 8, :] = weight * inflow[:, TILE * b : TILE * b + TILE]
    precondition(0)

    lane = lax.broadcasted_iota(I32, (8, TILE), 1)
    moments = jnp.zeros((8, TILE), F32)

    def total_of(k, other):
        acc = jnp.zeros((8, TILE), F32)
        for b in range(BLOCKS):
            acc = acc + basis[k, 8 * b : 8 * b + 8, :] * other(b)
        return jnp.sum(acc, axis=1, keepdims=True)

    def right_side(b):
        weight = inflow_weight * mask[b : b + 1, :].astype(F32)
        return weight * inflow[:, TILE * b : TILE * b + TILE]

    junc_first = INNER // wide
    junc_steps = JUNC // wide
    for k in range(3):
        split_into(pair, basis[k])
        for j in range(SHOWN):
            wanted = jnp.broadcast_to(shown[j : j + 1, :], (8, TILE))
            tile = jnp.zeros((8, TILE), F32)
            for b in range(BLOCKS):
                tile = jnp.where(wanted == b, basis[k, 8 * b : 8 * b + 8, :], tile)
            fwd_out[k, 8 * j : 8 * j + 8, :] = tile
        if k == 0:
            pl.semaphore_wait(barrier, len(partners))
        forward = pltpu.make_async_remote_copy(
            src_ref=fwd_out.at[k], dst_ref=fwd_in.at[k], send_sem=fwd_send.at[k], recv_sem=fwd_recv.at[k],
            device_id={"dom": lower}, device_id_type=MESH,
        )
        forward.start()
        moments = jnp.where(lane == k, total_of(k, right_side), moments)
        if k < 2:
            back_out[...] = jnp.zeros_like(back_out)
            for step in range(junc_steps):
                cols = head_cols(junc_first + step)
                value = gather(pair, cols, BLOCKS)
                gathered[:, step * wide : step * wide + wide] = value
                back_out[...] += scatter(cond8[:, cols] * value, tail_cols(junc_first + step), SHOWN)
            back_src[k] = back_out[...]
            backward = pltpu.make_async_remote_copy(
                src_ref=back_src.at[k], dst_ref=back_in.at[k], send_sem=back_send.at[k], recv_sem=back_recv.at[k],
                device_id={"dom": upper}, device_id_type=MESH,
            )
            backward.start()
            out[...] = jnp.zeros_like(out)

            def inner(step, carry):
                hcols, tcols = head_cols(step), tail_cols(step)
                value = cond8[:, hcols]
                at_head = gather(pair, hcols, BLOCKS)
                at_tail = gather(pair, tcols, BLOCKS)
                out[...] += scatter(value * at_tail, hcols, BLOCKS) + scatter(value * at_head, tcols, BLOCKS)
                return carry

            lax.fori_loop(0, INNER // wide, inner, 0)
            forward.wait()
            split_into(upper_pair, fwd_in[k])
            for step in range(junc_steps):
                hcols, tcols = head_cols(junc_first + step), tail_cols(junc_first + step)
                value = gather(upper_pair, tcols, SHOWN)
                out[...] += scatter(cond8[:, hcols] * value, hcols, BLOCKS)
            backward.wait()
            for b in range(BLOCKS):
                acc = out[8 * b : 8 * b + 8, :]
                for j in range(SHOWN):
                    acc = acc + jnp.where(jnp.broadcast_to(shown[j : j + 1, :], (8, TILE)) == b, back_in[k, 8 * j : 8 * j + 8, :], 0.0)
                image = degree[b : b + 1, :] * basis[k, 8 * b : 8 * b + 8, :] - acc
                images[k, 8 * b : 8 * b + 8, :] = image
                residual[8 * b : 8 * b + 8, :] = residual[8 * b : 8 * b + 8, :] - image
            precondition(k + 1)
            moments = jnp.where(lane == 3 + k, total_of(k, lambda b: images[k, 8 * b : 8 * b + 8, :]), moments)
            moments = jnp.where(lane == 6 + k, total_of(k + 1, lambda b: images[k, 8 * b : 8 * b + 8, :]), moments)
        else:
            def quadratic(step, carry):
                hcols, tcols = head_cols(step), tail_cols(step)
                return carry + cond8[:, hcols] * gather(pair, hcols, BLOCKS) * gather(pair, tcols, BLOCKS)

            crossed = lax.fori_loop(0, INNER // wide, quadratic, jnp.zeros((8, wide), F32))
            forward.wait()
            split_into(upper_pair, fwd_in[k])
            for step in range(junc_steps):
                hcols, tcols = head_cols(junc_first + step), tail_cols(junc_first + step)
                crossed = crossed + cond8[:, hcols] * gather(pair, hcols, BLOCKS) * gather(upper_pair, tcols, SHOWN)
            square = total_of(2, lambda b: degree[b : b + 1, :] * basis[2, 8 * b : 8 * b + 8, :])
            square = square - 2.0 * jnp.sum(crossed, axis=1, keepdims=True)
            moments = jnp.where(lane == 5, square, moments)
            moments = jnp.where(lane == 8, total_of(2, lambda b: images[0, 8 * b : 8 * b + 8, :]), moments)

    def exchange(buffer, send, recv, index, count, target):
        copies = []
        for o in range(1, count):
            other = lax.rem(index + o, count)
            copies.append(pltpu.make_async_remote_copy(
                src_ref=buffer.at[index], dst_ref=buffer.at[index], send_sem=send.at[o], recv_sem=recv.at[o],
                device_id=target(other), device_id_type=MESH,
            ))
        for copy in copies:
            copy.start()
        for copy in copies:
            copy.wait()
        acc = buffer[0]
        for o in range(1, count):
            acc = acc + buffer[o]
        return acc

    one_buf[seat] = moments
    moments = exchange(one_buf, one_send, one_recv, seat, planes, lambda other: {"dom": plane_place(other)})
    two_buf[column] = moments
    moments = exchange(two_buf, two_send, two_recv, column, depth_z, lambda other: {"dom": column_place(other)})

    def entry(index):
        return jnp.broadcast_to(moments[:, index : index + 1], (8, TILE))

    b0, b1, b2, g00, g11, g22, g01, g12, g02 = [entry(i) for i in range(9)]

    def safe_inverse(value, scale):
        good = value > 1e-6 * scale
        return jnp.where(good, 1.0 / jnp.where(good, value, 1.0), 0.0)

    i0 = safe_inverse(g00, g00)
    l10 = g01 * i0
    l20 = g02 * i0
    i1 = safe_inverse(g11 - l10 * g01, g11)
    c12 = g12 - l20 * g01
    l21 = c12 * i1
    i2 = safe_inverse(g22 - l20 * g02 - l21 * c12, g22)
    w1 = b1 - l10 * b0
    w2 = b2 - l20 * b0 - l21 * w1
    y2 = w2 * i2
    y1 = w1 * i1 - l21 * y2
    y0 = b0 * i0 - l10 * y1 - l20 * y2
    for b in range(BLOCKS):
        rows = slice(8 * b, 8 * b + 8)
        value = y0 * basis[0, rows, :] + y1 * basis[1, rows, :] + y2 * basis[2, rows, :]
        pressure[:, TILE * b : TILE * b + TILE] = value
        rep_buf[mine, b : b + 1, :] = jnp.sum(value, axis=0, keepdims=True)
    total = exchange(rep_buf, rep_send, rep_recv, mine, reps, lambda other: {"rep": other})
    mean[...] = total * (1.0 / SCEN_ALL)


def vmem(count):
    return [pl.BlockSpec(memory_space=pltpu.VMEM)] * count


def smem(count):
    return [pl.BlockSpec(memory_space=pltpu.SMEM)] * count


def per_device(sizes, inflow, mask, ends, live, shown, radius, length):
    parts, depth_z, planes, reps = sizes
    mask = mask.reshape(BLOCKS, TILE)
    dma = pltpu.SemaphoreType.DMA
    cond, arrived = pl.pallas_call(
        functools.partial(head_kernel, parts),
        out_shape=(jax.ShapeDtypeStruct((1, SEGS), F32), jax.ShapeDtypeStruct((SHOWN, TILE), F32)),
        in_specs=vmem(3) + smem(1),
        out_specs=tuple(vmem(2)),
        scratch_shapes=[pltpu.VMEM((SHOWN, TILE), F32), pltpu.VMEM((SHOWN, TILE), F32), dma, dma],
        compiler_params=pltpu.CompilerParams(collective_id=0, has_side_effects=True),
        name="conductances",
    )(ends, radius.reshape(1, SEGS), length.reshape(1, SEGS), live)
    inverse, degree = pl.pallas_call(
        setup_kernel,
        out_shape=(jax.ShapeDtypeStruct((BLOCKS, TILE, TILE), BF16), jax.ShapeDtypeStruct((BLOCKS, TILE), F32)),
        in_specs=vmem(3) + smem(1) + vmem(1),
        out_specs=tuple(vmem(2)),
        scratch_shapes=[
            pltpu.VMEM((BLOCKS, TILE, TILE), F32),
            pltpu.VMEM((1, INNER), F32),
            pltpu.VMEM((96, TILE), F32),
            pltpu.VMEM((5 * CHUNKS, TILE), F32),
            pltpu.VMEM((5 * CHUNKS, TILE), F32),
            pltpu.VMEM((64, TILE), I32),
            pltpu.SMEM((64, TILE), I32),
            dma,
        ],
        name="inverses",
    )(ends, cond, mask, shown, arrived)
    rows = 8 * BLOCKS
    back = 8 * SHOWN
    pressure, mean = pl.pallas_call(
        functools.partial(solve_kernel, sizes),
        out_shape=(jax.ShapeDtypeStruct((8, NODES), F32), jax.ShapeDtypeStruct((BLOCKS, TILE), F32)),
        in_specs=vmem(7),
        out_specs=tuple(vmem(2)),
        scratch_shapes=[
            pltpu.VMEM((TILE, 2 * SEGS), BF16),
            pltpu.VMEM((8, 2 * SEGS), I32),
            pltpu.VMEM((8, SEGS), F32),
            pltpu.VMEM((3, rows, TILE), F32),
            pltpu.VMEM((2, rows, TILE), F32),
            pltpu.VMEM((rows, TILE), F32),
            pltpu.VMEM((rows, 2 * TILE), BF16),
            pltpu.VMEM((back, 2 * TILE), BF16),
            pltpu.VMEM((rows, TILE), F32),
            pltpu.VMEM((back, TILE), F32),
            pltpu.VMEM((8, JUNC), F32),
            pltpu.VMEM((3, back, TILE), F32),
            pltpu.VMEM((3, back, TILE), F32),
            pltpu.VMEM((2, back, TILE), F32),
            pltpu.VMEM((2, back, TILE), F32),
            pltpu.VMEM((planes, 8, TILE), F32),
            pltpu.VMEM((depth_z, 8, TILE), F32),
            pltpu.VMEM((reps, BLOCKS, TILE), F32),
            dma((3,)), dma((3,)), dma((2,)), dma((2,)),
            dma((planes,)), dma((planes,)), dma((depth_z,)), dma((depth_z,)), dma((reps,)), dma((reps,)),
        ],
        compiler_params=pltpu.CompilerParams(collective_id=1, has_side_effects=True),
        name="gradients",
    )(inflow, mask, ends, cond, degree, inverse, jnp.broadcast_to(shown[:, None], (SHOWN, TILE)))
    return pressure, mean.reshape(NODES)


def solution(mesh):
    in_specs = (P("rep", "dom"), P("dom"), P(None, "dom"), P("dom"), P("dom"), P("dom"), P("dom"))
    out_specs = (P("rep", "dom"), P("dom"))
    parts, reps = mesh.shape["dom"], mesh.shape["rep"]
    depth_z = 8 if parts == 64 else parts // 4
    sizes = (parts, depth_z, parts // depth_z, reps)
    return jax.shard_map(
        functools.partial(per_device, sizes), mesh=mesh, in_specs=in_specs, out_specs=out_specs, check_vma=False
    )
```

```python
import functools

import jax
import jax.numpy as jnp
from jax import lax
from jax.experimental import pallas as pl
from jax.experimental.pallas import tpu as pltpu
from jax.sharding import PartitionSpec as P

MESH = pl.DeviceIdType.MESH
F32 = jnp.float32
BF16 = jnp.bfloat16
I32 = jnp.int32

TILE = 128
BLOCKS = 32
NODES = 4096
SCEN_ALL = 32
JUNC = 1024
INNER = 6144
SEGS = 7168
SHOWN = 8
CHUNKS = 80
PANEL = 32
FOUR = 4
UNROLL = 4

leak_rate = 0.05
inflow_weight = 20.0


def dot_nt(a, b):
    return lax.dot_general(a, b, (((1,), (1,)), ((), ())), preferred_element_type=F32)


def dot_nn(a, b):
    return lax.dot_general(a, b, (((1,), (0,)), ((), ())), preferred_element_type=F32)


def dot_tn(a, b):
    return lax.dot_general(a, b, (((0,), (0,)), ((), ())), preferred_element_type=F32)


def parts2(x):
    hi = x.astype(BF16).astype(F32)
    return hi, x - hi


def parts3(x):
    hi = x.astype(BF16).astype(F32)
    rest = x - hi
    mid = rest.astype(BF16).astype(F32)
    return hi, mid, rest - mid


def one_hot_rows(row, count):
    ids = lax.broadcasted_iota(I32, (count, row.shape[1]), 0)
    return ids == row


def spread(mask, value):
    return jnp.where(mask, value, 0.0).astype(BF16)


def conductance(radius, seg_length):
    diameter = 2.0 * radius
    power = jnp.exp(0.645 * jnp.log(diameter))
    viscous = 220.0 * jnp.exp(-1.3 * diameter) + 3.2 - 2.44 * jnp.exp(-0.06 * power)
    scaled = diameter * 0.125
    scaled = scaled * scaled
    return scaled * scaled * (50.0 / seg_length) / viscous


def head_kernel(parts, ends, radius, length, live, cond_out, arrived, sent, landed, send_sem, recv_sem):
    place = lax.axis_index("dom")
    upper = lax.rem(place + 1, parts)
    lower = lax.rem(place + parts - 1, parts)
    barrier = pltpu.get_barrier_semaphore()
    for other in (upper, lower):
        pl.semaphore_signal(barrier, inc=1, device_id={"dom": other}, device_id_type=MESH)
    cond = conductance(radius[...], length[...])
    position = lax.broadcasted_iota(I32, (1, SEGS), 1)
    limit = jnp.where(position < INNER, jnp.full((1, SEGS), live[0], I32), jnp.full((1, SEGS), (parts - 1 - place) * SEGS, I32))
    cond = jnp.where(position < limit, cond, 0.0)
    cond_out[...] = cond
    slot = ends[1:2, INNER:]
    junc = cond[:, INNER:]
    owner = one_hot_rows(slot >> 7, SHOWN)
    stack = jnp.concatenate([jnp.where(owner, part, 0.0) for part in parts3(junc)], axis=0).astype(BF16)
    lanes = spread(one_hot_rows(slot & 127, TILE), 1.0)
    sums = dot_nt(stack, lanes)
    sent[...] = sums[0:8] + sums[8:16] + sums[16:24]
    pl.semaphore_wait(barrier, 2)
    copy = pltpu.make_async_remote_copy(
        src_ref=sent, dst_ref=landed, send_sem=send_sem, recv_sem=recv_sem, device_id={"dom": upper}, device_id_type=MESH
    )
    copy.start()
    copy.wait()
    arrived[...] = landed[...]


def setup_kernel(
    ends, cond, mask, shown, arrived, inverse, degree_out, table, rank, degree, sums, packed, counts, counts_smem, sem
):
    degree[...] = jnp.zeros_like(degree)
    sums[...] = jnp.zeros_like(sums)
    width = 256
    before = lax.broadcasted_iota(I32, (width, width), 0) < lax.broadcasted_iota(I32, (width, width), 1)
    before = jnp.where(before, 1.0, 0.0).astype(BF16)

    def add_degree(node, value):
        owner = one_hot_rows(node >> 7, BLOCKS)
        stack = jnp.concatenate([jnp.where(owner, part, 0.0) for part in parts3(value)], axis=0).astype(BF16)
        lanes = spread(one_hot_rows(node & 127, TILE), 1.0)
        degree[...] += dot_nt(stack, lanes)

    def scan(step, carry):
        cols = pl.ds(pl.multiple_of(step * width, width), width)
        head = ends[0:1, cols]
        tail = ends[1:2, cols]
        value = cond[:, cols]
        add_degree(head, value)
        add_degree(tail, value)
        bucket = jnp.where((head >> 7) == (tail >> 7), head >> 7, -1)
        member = one_hot_rows(bucket, BLOCKS)
        ahead = dot_nn(spread(member, 1.0), before)
        rank[:, cols] = jnp.sum(jnp.where(member, ahead + carry, 0.0), axis=0, keepdims=True)
        return carry + jnp.sum(jnp.where(member, 1.0, 0.0), axis=1, keepdims=True)

    total = lax.fori_loop(0, INNER // width, scan, jnp.zeros((BLOCKS, 1), F32))
    add_degree(ends[0:1, INNER:], cond[:, INNER:])
    deg = degree[0:32, :] + degree[32:64, :] + degree[64:96, :]
    block_id = lax.broadcasted_iota(I32, (BLOCKS, TILE), 0)
    for j in range(SHOWN):
        deg = deg + jnp.where(block_id == shown[j], arrived[j : j + 1, :], 0.0)
    deg = deg + (leak_rate + inflow_weight * mask[...].astype(F32))
    degree_out[...] = deg

    chunks = jnp.floor((jnp.broadcast_to(total, (BLOCKS, TILE)) + 127.0) * (1.0 / 128.0))
    below = lax.broadcasted_iota(I32, (BLOCKS, BLOCKS), 1) < lax.broadcasted_iota(I32, (BLOCKS, BLOCKS), 0)
    start = dot_nn(jnp.where(below, 1.0, 0.0).astype(BF16), chunks.astype(BF16))
    counts[0:32, :] = start.astype(I32)
    counts[32:64, :] = chunks.astype(I32)
    to_scalar = pltpu.make_async_copy(counts, counts_smem, sem)
    to_scalar.start()
    start_column = start[:, 0:1]
    wide = 512

    def compact(step, carry):
        cols = pl.ds(pl.multiple_of(step * wide, wide), wide)
        head = ends[0:1, cols]
        tail = ends[1:2, cols]
        inside = (head >> 7) == (tail >> 7)
        bucket = jnp.where(inside, head >> 7, -1)
        base = jnp.sum(jnp.where(one_hot_rows(bucket, BLOCKS), start_column, 0.0), axis=0, keepdims=True)
        order = rank[:, cols].astype(I32)
        chunk = jnp.where(inside, base.astype(I32) + (order >> 7), -1)
        at_chunk = one_hot_rows(chunk, CHUNKS)
        values = ((head & 127).astype(F32), (tail & 127).astype(F32)) + parts3(cond[:, cols])
        stack = jnp.concatenate([spread(at_chunk, value) for value in values], axis=0)
        lanes = spread(one_hot_rows(order & 127, TILE), 1.0)
        sums[...] += dot_nt(stack, lanes)
        return carry

    lax.fori_loop(0, INNER // wide, compact, 0)
    packed[...] = sums[...]
    to_scalar.wait()

    row_id = lax.broadcasted_iota(I32, (TILE, TILE), 0)
    lane_id = lax.broadcasted_iota(I32, (TILE, TILE), 1)

    def fill(block, carry):
        first = counts_smem[block, 0]
        count = counts_smem[block + BLOCKS, 0]

        def add_chunk(index, acc):
            row = first + index
            head = packed[pl.ds(row, 1), :].astype(I32)
            tail = packed[pl.ds(row + CHUNKS, 1), :].astype(I32)
            at_head = row_id == head
            at_tail = row_id == tail
            left = jnp.concatenate([spread(at_head, 1.0), spread(at_tail, 1.0)], axis=1)
            for k in range(3):
                value = packed[pl.ds(row + (2 + k) * CHUNKS, 1), :]
                right = jnp.concatenate([spread(at_tail, value), spread(at_head, value)], axis=1)
                acc = acc + dot_nt(left, right)
            return acc

        acc = lax.fori_loop(0, count, add_chunk, jnp.zeros((TILE, TILE), F32))
        table[block] = jnp.where(row_id == lane_id, degree_out[pl.ds(block, 1), :], -acc)
        return carry

    lax.fori_loop(0, BLOCKS, fill, 0)

    panel_lane = lax.broadcasted_iota(I32, (PANEL, TILE), 1)
    panel_row = lax.broadcasted_iota(I32, (PANEL, TILE), 0)
    own_lane = panel_lane & (PANEL - 1)
    own_block = (row_id // PANEL) == (lane_id // PANEL)

    def panel(index, carry):
        base = pl.multiple_of(index * PANEL, PANEL)
        rows = pl.ds(base, PANEL)
        olds = [table[b, rows, :] for b in range(BLOCKS)]
        small = []
        for g in range(BLOCKS // FOUR):
            joined = jnp.zeros((PANEL, TILE), F32)
            for i in range(FOUR):
                turned = pltpu.roll(olds[g * FOUR + i], lax.rem(PANEL * i + TILE - base, TILE), 1)
                joined = jnp.where((panel_lane // PANEL) == i, turned, joined)
            small.append(joined)
        for t in range(PANEL):
            source = (panel_lane // PANEL) * PANEL + t
            at_lane = own_lane == t
            for g in range(BLOCKS // FOUR):
                x = small[g]
                column = jnp.take_along_axis(x, source, axis=1, mode="promise_in_bounds")
                pivot = 1.0 / column[t : t + 1, :]
                row = jnp.where(at_lane[0:1], pivot, x[t : t + 1, :] * pivot)
                rest = jnp.where(at_lane, 0.0, x) - column * row
                small[g] = jnp.where(panel_row == t, row, rest)
        unit = jnp.where(panel_lane == panel_row + base, 1.0, 0.0)
        in_panel = (panel_lane >= base) & (panel_lane < base + PANEL)
        keep = ((lane_id >= base) & (lane_id < base + PANEL)) | ((row_id >= base) & (row_id < base + PANEL))
        zero = jnp.zeros((PANEL, TILE), BF16)
        for g in range(BLOCKS // FOUR):
            diagonal = jnp.where(own_block, jnp.concatenate([small[g]] * FOUR, axis=0), 0.0)
            members = [jnp.where(in_panel, unit, olds[g * FOUR + i]) for i in range(FOUR)]
            stack = jnp.concatenate(members, axis=0)
            dh, dm, dl = [part.astype(BF16) for part in parts3(diagonal)]
            sh, sm, sl = [part.astype(BF16) for part in parts3(stack)]
            fresh = dot_nn(jnp.concatenate([dh, dm], axis=1), jnp.concatenate([sh, sm], axis=0))
            fresh = fresh + dot_nn(jnp.concatenate([dh, dm], axis=1), jnp.concatenate([sm, sh], axis=0))
            fresh = fresh + dot_nn(jnp.concatenate([dh, dl], axis=1), jnp.concatenate([sl, sh], axis=0))
            turned = jnp.where(row_id < base + PANEL, -stack.T, stack.T)
            th, tm, tl = [part.astype(BF16) for part in parts3(turned)]
            fh, fm, fl = [part.astype(BF16) for part in parts3(fresh)]

            def across(value):
                lines = []
                for i in range(FOUR):
                    cells = [zero] * FOUR
                    cells[i] = value[PANEL * i : PANEL * i + PANEL, :]
                    lines.append(jnp.concatenate(cells, axis=1))
                return jnp.concatenate(lines, axis=0)

            ah, am, al = across(fh), across(fm), across(fl)
            update = dot_nn(jnp.concatenate([th, tm], axis=1), jnp.concatenate([ah, am], axis=0))
            update = update + dot_nn(jnp.concatenate([th, tm], axis=1), jnp.concatenate([am, ah], axis=0))
            update = update + dot_nn(jnp.concatenate([th, tl], axis=1), jnp.concatenate([al, ah], axis=0))
            for i in range(FOUR):
                b = g * FOUR + i
                table[b] = jnp.where(keep, 0.0, table[b]) - update[:, TILE * i : TILE * i + TILE]
        return carry

    lax.fori_loop(0, TILE // PANEL, panel, 0)

    def finish(block, carry):
        inverse[block] = table[block].astype(BF16)
        return carry

    lax.fori_loop(0, BLOCKS, finish, 0)


def solve_kernel(
    sizes, inflow, mask, ends, cond, degree, inverse, shown, pressure, mean,
    table, owner8, cond8, basis, images, residual, pair, upper_pair, out, back_out, fwd_out, fwd_in, back_src, back_in,
    one_buf, two_buf, rep_buf,
    fwd_send, fwd_recv, back_send, back_recv, one_send, one_recv, two_send, two_recv, rep_send, rep_recv,
):
    parts, depth_z, planes, reps = sizes
    place = lax.axis_index("dom")
    mine = lax.axis_index("rep")
    upper = lax.rem(place + 1, parts)
    lower = lax.rem(place + parts - 1, parts)
    core = lax.rem(place, 2)
    column = lax.rem(place // 2, depth_z)
    line = place // (2 * depth_z)
    seat = line * 2 + core

    def plane_place(other):
        return ((other // 2) * depth_z + column) * 2 + lax.rem(other, 2)

    def column_place(other):
        return (line * depth_z + other) * 2 + core

    barrier = pltpu.get_barrier_semaphore()
    partners = [{"dom": upper}, {"dom": lower}]
    partners += [{"dom": plane_place(lax.rem(seat + o, planes))} for o in range(1, planes)]
    partners += [{"dom": column_place(lax.rem(column + o, depth_z))} for o in range(1, depth_z)]
    partners += [{"rep": lax.rem(mine + o, reps)} for o in range(1, reps)]
    for partner in partners:
        pl.semaphore_signal(barrier, inc=1, device_id=partner, device_id_type=MESH)

    wide = 256

    def make(step, carry):
        cols = pl.ds(pl.multiple_of(step * wide, wide), wide)
        value = jnp.broadcast_to(cond[:, cols], (8, wide))
        cond8[:, cols] = value
        for side in range(2):
            node = ends[side : side + 1, cols]
            into = pl.ds(pl.multiple_of(side * SEGS + step * wide, wide), wide)
            table[:, into] = spread(one_hot_rows(node & 255, 256), 1.0)
            owner8[:, into] = jnp.broadcast_to(node >> 8, (8, wide))
        return carry

    lax.fori_loop(0, SEGS // wide, make, 0)

    def split_into(target, tile, pairs):
        rows = 8 * pairs
        for q in range(0, pairs, 2):
            highs, lows = [], []
            for half in range(2):
                parts = [parts2(tile(2 * (q + i) + half)) for i in range(2)]
                highs.append(jnp.concatenate([part[0] for part in parts], axis=0))
                lows.append(jnp.concatenate([part[1] for part in parts], axis=0))
            target[8 * q : 8 * q + 16, :] = jnp.concatenate(highs, axis=1).astype(BF16)
            target[rows + 8 * q : rows + 8 * q + 16, :] = jnp.concatenate(lows, axis=1).astype(BF16)

    def gather(source, cols, pairs):
        full = dot_nn(source[...], table[:, cols])
        owner = owner8[:, cols]
        result = jnp.zeros((8, wide), F32)
        for q in range(pairs):
            value = full[8 * q : 8 * q + 8, :] + full[8 * (q + pairs) : 8 * (q + pairs) + 8, :]
            result = jnp.where(owner == q, value, result)
        return result

    def scatter(values, cols, pairs):
        left, right = [], []
        for value, at in zip(values, cols):
            owner = owner8[:, at]
            left.append(jnp.concatenate([jnp.where(owner == q, part, 0.0) for part in parts2(value) for q in range(pairs)], axis=0).astype(BF16))
            right.append(table[:, at])
        return dot_nt(jnp.concatenate(left, axis=1), jnp.concatenate(right, axis=1))

    def tile_of(source, b, pairs):
        rows, lanes = 8 * (b // 2), slice(TILE * (b % 2), TILE * (b % 2) + TILE)
        return source[rows : rows + 8, lanes] + source[8 * pairs + rows : 8 * pairs + rows + 8, lanes]

    pairs_all = BLOCKS // 2
    pairs_shown = SHOWN // 2

    def head_cols(step):
        return pl.ds(pl.multiple_of(step * wide, wide), wide)

    def tail_cols(step):
        return pl.ds(pl.multiple_of(SEGS + step * wide, wide), wide)

    def precondition(k):
        for b in range(BLOCKS):
            field = residual[8 * b : 8 * b + 8, :].astype(BF16)
            basis[k, 8 * b : 8 * b + 8, :] = dot_nn(field, inverse[b])

    for b in range(BLOCKS):
        weight = inflow_weight * mask[b : b + 1, :].astype(F32)
        residual[8 * b : 8 * b + 8, :] = weight * inflow[:, TILE * b : TILE * b + TILE]
    precondition(0)

    lane = lax.broadcasted_iota(I32, (8, TILE), 1)
    moments = jnp.zeros((8, TILE), F32)

    def total_of(k, other):
        acc = jnp.zeros((8, TILE), F32)
        for b in range(BLOCKS):
            acc = acc + basis[k, 8 * b : 8 * b + 8, :] * other(b)
        return jnp.sum(acc, axis=1, keepdims=True)

    def right_side(b):
        weight = inflow_weight * mask[b : b + 1, :].astype(F32)
        return weight * inflow[:, TILE * b : TILE * b + TILE]

    junc_first = INNER // wide
    junc_steps = JUNC // wide
    for k in range(3):
        split_into(pair, lambda b: basis[k, 8 * b : 8 * b + 8, :], pairs_all)
        for j in range(SHOWN):
            wanted = jnp.broadcast_to(shown[j : j + 1, :], (8, TILE))
            tile = jnp.zeros((8, TILE), F32)
            for b in range(BLOCKS):
                tile = jnp.where(wanted == b, basis[k, 8 * b : 8 * b + 8, :], tile)
            fwd_out[k, 8 * j : 8 * j + 8, :] = tile
        if k == 0:
            pl.semaphore_wait(barrier, len(partners))
        forward = pltpu.make_async_remote_copy(
            src_ref=fwd_out.at[k], dst_ref=fwd_in.at[k], send_sem=fwd_send.at[k], recv_sem=fwd_recv.at[k],
            device_id={"dom": lower}, device_id_type=MESH,
        )
        forward.start()
        moments = jnp.where(lane == k, total_of(k, right_side), moments)
        if k < 2:
            hcols = [head_cols(junc_first + step) for step in range(junc_steps)]
            tcols = [tail_cols(junc_first + step) for step in range(junc_steps)]
            back_out[...] = scatter([cond8[:, at] * gather(pair, at, pairs_all) for at in hcols], tcols, pairs_shown)
            for j in range(SHOWN):
                back_src[k, 8 * j : 8 * j + 8, :] = tile_of(back_out, j, pairs_shown)
            backward = pltpu.make_async_remote_copy(
                src_ref=back_src.at[k], dst_ref=back_in.at[k], send_sem=back_send.at[k], recv_sem=back_recv.at[k],
                device_id={"dom": upper}, device_id_type=MESH,
            )
            backward.start()
            out[...] = jnp.zeros_like(out)

            def inner(step, carry):
                values, cols = [], []
                for i in range(UNROLL):
                    h, t = head_cols(UNROLL * step + i), tail_cols(UNROLL * step + i)
                    weight = cond8[:, h]
                    values += [weight * gather(pair, t, pairs_all), weight * gather(pair, h, pairs_all)]
                    cols += [h, t]
                out[...] += scatter(values, cols, pairs_all)
                return carry

            lax.fori_loop(0, INNER // wide // UNROLL, inner, 0)
            forward.wait()
            split_into(upper_pair, lambda j: fwd_in[k, 8 * j : 8 * j + 8, :], pairs_shown)
            out[...] += scatter([cond8[:, h] * gather(upper_pair, t, pairs_shown) for h, t in zip(hcols, tcols)], hcols, pairs_all)
            backward.wait()
            for b in range(BLOCKS):
                acc = tile_of(out, b, pairs_all)
                for j in range(SHOWN):
                    acc = acc + jnp.where(jnp.broadcast_to(shown[j : j + 1, :], (8, TILE)) == b, back_in[k, 8 * j : 8 * j + 8, :], 0.0)
                image = degree[b : b + 1, :] * basis[k, 8 * b : 8 * b + 8, :] - acc
                images[k, 8 * b : 8 * b + 8, :] = image
                residual[8 * b : 8 * b + 8, :] = residual[8 * b : 8 * b + 8, :] - image
            precondition(k + 1)
            moments = jnp.where(lane == 3 + k, total_of(k, lambda b: images[k, 8 * b : 8 * b + 8, :]), moments)
            moments = jnp.where(lane == 6 + k, total_of(k + 1, lambda b: images[k, 8 * b : 8 * b + 8, :]), moments)
        else:
            def quadratic(step, carry):
                for i in range(UNROLL):
                    h, t = head_cols(UNROLL * step + i), tail_cols(UNROLL * step + i)
                    carry = carry + cond8[:, h] * gather(pair, h, pairs_all) * gather(pair, t, pairs_all)
                return carry

            crossed = lax.fori_loop(0, INNER // wide // UNROLL, quadratic, jnp.zeros((8, wide), F32))
            ahead = [cond8[:, head_cols(junc_first + step)] * gather(pair, head_cols(junc_first + step), pairs_all) for step in range(junc_steps)]
            forward.wait()
            split_into(upper_pair, lambda j: fwd_in[k, 8 * j : 8 * j + 8, :], pairs_shown)
            for step in range(junc_steps):
                crossed = crossed + ahead[step] * gather(upper_pair, tail_cols(junc_first + step), pairs_shown)
            square = total_of(2, lambda b: degree[b : b + 1, :] * basis[2, 8 * b : 8 * b + 8, :])
            square = square - 2.0 * jnp.sum(crossed, axis=1, keepdims=True)
            moments = jnp.where(lane == 5, square, moments)
            moments = jnp.where(lane == 8, total_of(2, lambda b: images[0, 8 * b : 8 * b + 8, :]), moments)

    def exchange(buffer, send, recv, index, count, target):
        copies = []
        for o in range(1, count):
            other = lax.rem(index + o, count)
            copies.append(pltpu.make_async_remote_copy(
                src_ref=buffer.at[index], dst_ref=buffer.at[index], send_sem=send.at[o], recv_sem=recv.at[o],
                device_id=target(other), device_id_type=MESH,
            ))
        for copy in copies:
            copy.start()
        for copy in copies:
            copy.wait()
        acc = buffer[0]
        for o in range(1, count):
            acc = acc + buffer[o]
        return acc

    one_buf[seat] = moments
    moments = exchange(one_buf, one_send, one_recv, seat, planes, lambda other: {"dom": plane_place(other)})
    two_buf[column] = moments
    moments = exchange(two_buf, two_send, two_recv, column, depth_z, lambda other: {"dom": column_place(other)})

    def entry(index):
        return jnp.broadcast_to(moments[:, index : index + 1], (8, TILE))

    b0, b1, b2, g00, g11, g22, g01, g12, g02 = [entry(i) for i in range(9)]

    def safe_inverse(value, scale):
        good = value > 1e-6 * scale
        return jnp.where(good, 1.0 / jnp.where(good, value, 1.0), 0.0)

    i0 = safe_inverse(g00, g00)
    l10 = g01 * i0
    l20 = g02 * i0
    i1 = safe_inverse(g11 - l10 * g01, g11)
    c12 = g12 - l20 * g01
    l21 = c12 * i1
    i2 = safe_inverse(g22 - l20 * g02 - l21 * c12, g22)
    w1 = b1 - l10 * b0
    w2 = b2 - l20 * b0 - l21 * w1
    y2 = w2 * i2
    y1 = w1 * i1 - l21 * y2
    y0 = b0 * i0 - l10 * y1 - l20 * y2
    for b in range(BLOCKS):
        rows = slice(8 * b, 8 * b + 8)
        value = y0 * basis[0, rows, :] + y1 * basis[1, rows, :] + y2 * basis[2, rows, :]
        pressure[:, TILE * b : TILE * b + TILE] = value
        rep_buf[mine, b : b + 1, :] = jnp.sum(value, axis=0, keepdims=True)
    total = exchange(rep_buf, rep_send, rep_recv, mine, reps, lambda other: {"rep": other})
    mean[...] = total * (1.0 / SCEN_ALL)


def vmem(count):
    return [pl.BlockSpec(memory_space=pltpu.VMEM)] * count


def smem(count):
    return [pl.BlockSpec(memory_space=pltpu.SMEM)] * count


def per_device(sizes, inflow, mask, ends, live, shown, radius, length):
    parts, depth_z, planes, reps = sizes
    mask = mask.reshape(BLOCKS, TILE)
    dma = pltpu.SemaphoreType.DMA
    cond, arrived = pl.pallas_call(
        functools.partial(head_kernel, parts),
        out_shape=(jax.ShapeDtypeStruct((1, SEGS), F32), jax.ShapeDtypeStruct((SHOWN, TILE), F32)),
        in_specs=vmem(3) + smem(1),
        out_specs=tuple(vmem(2)),
        scratch_shapes=[pltpu.VMEM((SHOWN, TILE), F32), pltpu.VMEM((SHOWN, TILE), F32), dma, dma],
        compiler_params=pltpu.CompilerParams(collective_id=0, has_side_effects=True),
        name="conductances",
    )(ends, radius.reshape(1, SEGS), length.reshape(1, SEGS), live)
    inverse, degree = pl.pallas_call(
        setup_kernel,
        out_shape=(jax.ShapeDtypeStruct((BLOCKS, TILE, TILE), BF16), jax.ShapeDtypeStruct((BLOCKS, TILE), F32)),
        in_specs=vmem(3) + smem(1) + vmem(1),
        out_specs=tuple(vmem(2)),
        scratch_shapes=[
            pltpu.VMEM((BLOCKS, TILE, TILE), F32),
            pltpu.VMEM((1, INNER), F32),
            pltpu.VMEM((96, TILE), F32),
            pltpu.VMEM((5 * CHUNKS, TILE), F32),
            pltpu.VMEM((5 * CHUNKS, TILE), F32),
            pltpu.VMEM((64, TILE), I32),
            pltpu.SMEM((64, TILE), I32),
            dma,
        ],
        name="inverses",
    )(ends, cond, mask, shown, arrived)
    rows = 8 * BLOCKS
    back = 8 * SHOWN
    pressure, mean = pl.pallas_call(
        functools.partial(solve_kernel, sizes),
        out_shape=(jax.ShapeDtypeStruct((8, NODES), F32), jax.ShapeDtypeStruct((BLOCKS, TILE), F32)),
        in_specs=vmem(7),
        out_specs=tuple(vmem(2)),
        scratch_shapes=[
            pltpu.VMEM((2 * TILE, 2 * SEGS), BF16),
            pltpu.VMEM((8, 2 * SEGS), I32),
            pltpu.VMEM((8, SEGS), F32),
            pltpu.VMEM((3, rows, TILE), F32),
            pltpu.VMEM((2, rows, TILE), F32),
            pltpu.VMEM((rows, TILE), F32),
            pltpu.VMEM((rows, 2 * TILE), BF16),
            pltpu.VMEM((back, 2 * TILE), BF16),
            pltpu.VMEM((rows, 2 * TILE), F32),
            pltpu.VMEM((back, 2 * TILE), F32),
            pltpu.VMEM((3, back, TILE), F32),
            pltpu.VMEM((3, back, TILE), F32),
            pltpu.VMEM((2, back, TILE), F32),
            pltpu.VMEM((2, back, TILE), F32),
            pltpu.VMEM((planes, 8, TILE), F32),
            pltpu.VMEM((depth_z, 8, TILE), F32),
            pltpu.VMEM((reps, BLOCKS, TILE), F32),
            dma((3,)), dma((3,)), dma((2,)), dma((2,)),
            dma((planes,)), dma((planes,)), dma((depth_z,)), dma((depth_z,)), dma((reps,)), dma((reps,)),
        ],
        compiler_params=pltpu.CompilerParams(collective_id=1, has_side_effects=True),
        name="gradients",
    )(inflow, mask, ends, cond, degree, inverse, jnp.broadcast_to(shown[:, None], (SHOWN, TILE)))
    return pressure, mean.reshape(NODES)


def solution(mesh):
    in_specs = (P("rep", "dom"), P("dom"), P(None, "dom"), P("dom"), P("dom"), P("dom"), P("dom"))
    out_specs = (P("rep", "dom"), P("dom"))
    parts, reps = mesh.shape["dom"], mesh.shape["rep"]
    depth_z = 8 if parts == 64 else parts // 4
    sizes = (parts, depth_z, parts // depth_z, reps)
    return jax.shard_map(
        functools.partial(per_device, sizes), mesh=mesh, in_specs=in_specs, out_specs=out_specs, check_vma=False
    )
```

```python
import functools

import jax
import jax.numpy as jnp
from jax import lax
from jax.experimental import pallas as pl
from jax.experimental.pallas import tpu as pltpu
from jax.sharding import PartitionSpec as P

MESH = pl.DeviceIdType.MESH
F32 = jnp.float32
BF16 = jnp.bfloat16
I32 = jnp.int32

TILE = 128
BLOCKS = 32
NODES = 4096
SCEN_ALL = 32
JUNC = 1024
INNER = 6144
SEGS = 7168
SHOWN = 8
CHUNKS = 80
PANEL = 32
FOUR = 4
UNROLL = 4
SCANS = 2

leak_rate = 0.05
inflow_weight = 20.0


def dot_nt(a, b):
    return lax.dot_general(a, b, (((1,), (1,)), ((), ())), preferred_element_type=F32)


def dot_nn(a, b):
    return lax.dot_general(a, b, (((1,), (0,)), ((), ())), preferred_element_type=F32)


def dot_tn(a, b):
    return lax.dot_general(a, b, (((0,), (0,)), ((), ())), preferred_element_type=F32)


def parts2(x):
    hi = x.astype(BF16).astype(F32)
    return hi, x - hi


def parts3(x):
    hi = x.astype(BF16).astype(F32)
    rest = x - hi
    mid = rest.astype(BF16).astype(F32)
    return hi, mid, rest - mid


def one_hot_rows(row, count):
    ids = lax.broadcasted_iota(I32, (count, row.shape[1]), 0)
    return ids == row


def spread(mask, value):
    return jnp.where(mask, value, 0.0).astype(BF16)


def conductance(radius, seg_length):
    diameter = 2.0 * radius
    power = jnp.exp(0.645 * jnp.log(diameter))
    viscous = 220.0 * jnp.exp(-1.3 * diameter) + 3.2 - 2.44 * jnp.exp(-0.06 * power)
    scaled = diameter * 0.125
    scaled = scaled * scaled
    return scaled * scaled * (50.0 / seg_length) / viscous


def head_kernel(parts, ends, radius, length, live, cond_out, arrived, sent, landed, send_sem, recv_sem):
    place = lax.axis_index("dom")
    upper = lax.rem(place + 1, parts)
    lower = lax.rem(place + parts - 1, parts)
    barrier = pltpu.get_barrier_semaphore()
    for other in (upper, lower):
        pl.semaphore_signal(barrier, inc=1, device_id={"dom": other}, device_id_type=MESH)
    cond = conductance(radius[...], length[...])
    position = lax.broadcasted_iota(I32, (1, SEGS), 1)
    limit = jnp.where(position < INNER, jnp.full((1, SEGS), live[0], I32), jnp.full((1, SEGS), (parts - 1 - place) * SEGS, I32))
    cond = jnp.where(position < limit, cond, 0.0)
    high, low = parts2(cond)
    cond = high + low.astype(BF16).astype(F32)
    cond_out[...] = cond
    slot = ends[1:2, INNER:]
    junc = cond[:, INNER:]
    owner = one_hot_rows(slot >> 7, SHOWN)
    stack = jnp.concatenate([jnp.where(owner, part, 0.0) for part in parts2(junc)], axis=0).astype(BF16)
    lanes = spread(one_hot_rows(slot & 127, TILE), 1.0)
    sums = dot_nt(stack, lanes)
    sent[...] = sums[0:8] + sums[8:16]
    pl.semaphore_wait(barrier, 2)
    copy = pltpu.make_async_remote_copy(
        src_ref=sent, dst_ref=landed, send_sem=send_sem, recv_sem=recv_sem, device_id={"dom": upper}, device_id_type=MESH
    )
    copy.start()
    copy.wait()
    arrived[...] = landed[...]


def setup_kernel(
    ends, cond, mask, shown, arrived, inverse, degree_out, table, rank, degree, sums, packed, counts, old_rows, turned_rows, small, counts_smem, sem
):
    degree[...] = jnp.zeros_like(degree)
    sums[...] = jnp.zeros_like(sums)
    width = 256
    before = lax.broadcasted_iota(I32, (width, width), 0) < lax.broadcasted_iota(I32, (width, width), 1)
    before = jnp.where(before, 1.0, 0.0).astype(BF16)

    def add_degree(nodes, values):
        stacks, lanes = [], []
        for node, value in zip(nodes, values):
            owner = one_hot_rows(node >> 7, BLOCKS)
            stacks.append(jnp.concatenate([jnp.where(owner, part, 0.0) for part in parts2(value)], axis=0).astype(BF16))
            lanes.append(spread(one_hot_rows(node & 127, TILE), 1.0))
        degree[...] += dot_nt(jnp.concatenate(stacks, axis=1), jnp.concatenate(lanes, axis=1))

    def scan(step, carry):
        nodes, values = [], []
        for i in range(SCANS):
            cols = pl.ds(pl.multiple_of((SCANS * step + i) * width, width), width)
            head = ends[0:1, cols]
            tail = ends[1:2, cols]
            value = cond[:, cols]
            nodes += [head, tail]
            values += [value, value]
            bucket = jnp.where((head >> 7) == (tail >> 7), head >> 7, -1)
            member = one_hot_rows(bucket, BLOCKS)
            ahead = dot_nn(spread(member, 1.0), before)
            rank[:, cols] = jnp.sum(jnp.where(member, ahead + carry, 0.0), axis=0, keepdims=True)
            carry = carry + jnp.sum(jnp.where(member, 1.0, 0.0), axis=1, keepdims=True)
        add_degree(nodes, values)
        return carry

    total = lax.fori_loop(0, INNER // width // SCANS, scan, jnp.zeros((BLOCKS, 1), F32))
    add_degree([ends[0:1, INNER:]], [cond[:, INNER:]])
    deg = degree[0:32, :] + degree[32:64, :]
    block_id = lax.broadcasted_iota(I32, (BLOCKS, TILE), 0)
    for j in range(SHOWN):
        deg = deg + jnp.where(block_id == shown[j], arrived[j : j + 1, :], 0.0)
    deg = deg + (leak_rate + inflow_weight * mask[...].astype(F32))
    degree_out[...] = deg

    chunks = jnp.floor((jnp.broadcast_to(total, (BLOCKS, TILE)) + 127.0) * (1.0 / 128.0))
    below = lax.broadcasted_iota(I32, (BLOCKS, BLOCKS), 1) < lax.broadcasted_iota(I32, (BLOCKS, BLOCKS), 0)
    start = dot_nn(jnp.where(below, 1.0, 0.0).astype(BF16), chunks.astype(BF16))
    counts[0:32, :] = start.astype(I32)
    counts[32:64, :] = chunks.astype(I32)
    to_scalar = pltpu.make_async_copy(counts, counts_smem, sem)
    to_scalar.start()
    start_column = start[:, 0:1]
    wide = 512

    def compact(step, carry):
        cols = pl.ds(pl.multiple_of(step * wide, wide), wide)
        head = ends[0:1, cols]
        tail = ends[1:2, cols]
        inside = (head >> 7) == (tail >> 7)
        bucket = jnp.where(inside, head >> 7, -1)
        base = jnp.sum(jnp.where(one_hot_rows(bucket, BLOCKS), start_column, 0.0), axis=0, keepdims=True)
        order = rank[:, cols].astype(I32)
        chunk = jnp.where(inside, base.astype(I32) + (order >> 7), -1)
        at_chunk = one_hot_rows(chunk, CHUNKS)
        values = ((head & 127).astype(F32), (tail & 127).astype(F32)) + parts2(cond[:, cols])
        stack = jnp.concatenate([spread(at_chunk, value) for value in values], axis=0)
        lanes = spread(one_hot_rows(order & 127, TILE), 1.0)
        sums[...] += dot_nt(stack, lanes)
        return carry

    lax.fori_loop(0, INNER // wide, compact, 0)
    packed[...] = sums[...]
    to_scalar.wait()

    row_id = lax.broadcasted_iota(I32, (TILE, TILE), 0)
    lane_id = lax.broadcasted_iota(I32, (TILE, TILE), 1)

    def chunk_of(row, live):
        head = packed[pl.ds(row, 1), :].astype(I32)
        tail = packed[pl.ds(row + CHUNKS, 1), :].astype(I32)
        at_head = row_id == head
        at_tail = row_id == tail
        left = jnp.concatenate([spread(at_head, 1.0), spread(at_tail, 1.0)], axis=1)
        right = []
        for k in range(2):
            value = packed[pl.ds(row + (2 + k) * CHUNKS, 1), :] * live
            right.append(jnp.concatenate([spread(at_tail, value), spread(at_head, value)], axis=1))
        both = dot_nt(left, jnp.concatenate(right, axis=0))
        return both[:, 0:TILE] + both[:, TILE:]

    def fill(step, carry):
        filled = []
        for i in range(FOUR):
            block = step * FOUR + i
            live = jnp.where(counts_smem[block + BLOCKS, 0] > 0, 1.0, 0.0)
            off = chunk_of(counts_smem[block, 0], live)
            filled.append(jnp.where(row_id == lane_id, degree_out[pl.ds(block, 1), :], -off))
        for i in range(FOUR):
            table[pl.ds(pl.multiple_of((step * FOUR + i) * TILE, TILE), TILE), :] = filled[i]
        return carry

    lax.fori_loop(0, BLOCKS // FOUR, fill, 0)

    def refill(block, carry):
        rows = pl.ds(pl.multiple_of(block * TILE, TILE), TILE)

        def more(index, inner):
            table[rows, :] = table[rows, :] - chunk_of(counts_smem[block, 0] + index, 1.0)
            return inner

        lax.fori_loop(1, counts_smem[block + BLOCKS, 0], more, 0)
        return carry

    lax.fori_loop(0, BLOCKS, refill, 0)

    panel_lane = lax.broadcasted_iota(I32, (PANEL, TILE), 1)
    panel_row = lax.broadcasted_iota(I32, (PANEL, TILE), 0)
    own_block = (row_id // PANEL) == (lane_id // PANEL)
    lane_block = panel_lane & (PANEL - 1)
    lane_group = panel_lane // PANEL

    def replicated(x, group):
        return jnp.take_along_axis(x, lane_block + group * PANEL, axis=1, mode="promise_in_bounds")

    def panel(index, carry):
        base = pl.multiple_of(index * PANEL, PANEL)
        for b in range(BLOCKS):
            old_rows[b * PANEL : (b + 1) * PANEL, :] = table[pl.ds(b * TILE + base, PANEL), :]
        for i in range(8):
            lines = [old_rows[pl.ds(8 * h + i, BLOCKS, stride=PANEL), :] for h in range(4)]
            turned_rows[i] = jnp.concatenate(lines, axis=0).T
        state = [turned_rows[i, pl.ds(base, PANEL), :] for i in range(8)]
        for first in range(0, PANEL, 4):
            coming = [replicated(state[(first + d) % 8], (first + d) // 8) for d in range(4)]
            for d in range(4):
                t = first + d
                at_row = panel_row == t
                now = coming[d]
                pivot = 1.0 / now[t : t + 1, :]
                new = jnp.where(at_row, pivot, now * pivot)
                for e in range(d + 1, 4):
                    x = coming[e]
                    coming[e] = jnp.where(at_row, 0.0, x) - x[t : t + 1, :] * new
                for i in range(8):
                    x = state[i]
                    rest = jnp.where(at_row, 0.0, x) - x[t : t + 1, :] * new
                    state[i] = jnp.where(lane_group == t // 8, new, rest) if i == t % 8 else rest
        for i in range(8):
            back = jnp.concatenate([state[i]] * 4, axis=0).T
            for h in range(4):
                small[pl.ds(8 * h + i, BLOCKS, stride=PANEL), :] = back[PANEL * h : PANEL * h + PANEL, :]
        unit = jnp.where(panel_lane == panel_row + base, 1.0, 0.0)
        in_panel = (panel_lane >= base) & (panel_lane < base + PANEL)
        keep = ((lane_id >= base) & (lane_id < base + PANEL)) | ((row_id >= base) & (row_id < base + PANEL))
        zero = jnp.zeros((PANEL, TILE), BF16)
        for g in range(BLOCKS // FOUR):
            span = slice(TILE * g, TILE * g + TILE)
            diagonal = jnp.where(own_block, small[span, :], 0.0)
            members = [jnp.where(in_panel, unit, old_rows[TILE * g + PANEL * i : TILE * g + PANEL * i + PANEL, :]) for i in range(FOUR)]
            stack = jnp.concatenate(members, axis=0)
            dh, dm = [part.astype(BF16) for part in parts2(diagonal)]
            sh, sm = [part.astype(BF16) for part in parts2(stack)]
            left = jnp.concatenate([dh, dm], axis=1)
            fresh = dot_nn(left, jnp.concatenate([sh, sm], axis=0)) + dot_nn(left, jnp.concatenate([sm, sh], axis=0))
            turned = stack.T
            turned = jnp.where(row_id < base + PANEL, -turned, turned)
            th, tm = [part.astype(BF16) for part in parts2(turned)]
            fh, fm = [part.astype(BF16) for part in parts2(fresh)]

            def across(value):
                lines = []
                for i in range(FOUR):
                    cells = [zero] * FOUR
                    cells[i] = value[PANEL * i : PANEL * i + PANEL, :]
                    lines.append(jnp.concatenate(cells, axis=1))
                return jnp.concatenate(lines, axis=0)

            ah, am = across(fh), across(fm)
            left = jnp.concatenate([th, tm], axis=1)
            update = dot_nn(left, jnp.concatenate([ah, am], axis=0)) + dot_nn(left, jnp.concatenate([am, ah], axis=0))
            for i in range(FOUR):
                rows = slice((g * FOUR + i) * TILE, (g * FOUR + i + 1) * TILE)
                table[rows, :] = jnp.where(keep, 0.0, table[rows, :]) - update[:, TILE * i : TILE * i + TILE]
        return carry

    lax.fori_loop(0, TILE // PANEL, panel, 0)

    def finish(block, carry):
        inverse[block] = table[pl.ds(pl.multiple_of(block * TILE, TILE), TILE), :].astype(BF16)
        return carry

    lax.fori_loop(0, BLOCKS, finish, 0)


def solve_kernel(
    sizes, inflow, mask, ends, cond, degree, inverse, shown, pressure, mean,
    table, owner8, cond8, basis, images, residual, pair, upper_pair, out, back_out, fwd_out, fwd_in, back_src, back_in,
    one_buf, two_buf, rep_buf,
    fwd_send, fwd_recv, back_send, back_recv, one_send, one_recv, two_send, two_recv, rep_send, rep_recv,
):
    parts, depth_z, planes, reps = sizes
    place = lax.axis_index("dom")
    mine = lax.axis_index("rep")
    upper = lax.rem(place + 1, parts)
    lower = lax.rem(place + parts - 1, parts)
    core = lax.rem(place, 2)
    column = lax.rem(place // 2, depth_z)
    line = place // (2 * depth_z)
    seat = line * 2 + core

    def plane_place(other):
        return ((other // 2) * depth_z + column) * 2 + lax.rem(other, 2)

    def column_place(other):
        return (line * depth_z + other) * 2 + core

    barrier = pltpu.get_barrier_semaphore()
    partners = [{"dom": upper}, {"dom": lower}]
    partners += [{"dom": plane_place(lax.rem(seat + o, planes))} for o in range(1, planes)]
    partners += [{"dom": column_place(lax.rem(column + o, depth_z))} for o in range(1, depth_z)]
    partners += [{"rep": lax.rem(mine + o, reps)} for o in range(1, reps)]
    for partner in partners:
        pl.semaphore_signal(barrier, inc=1, device_id=partner, device_id_type=MESH)

    wide = 256

    def make(step, carry):
        cols = pl.ds(pl.multiple_of(step * wide, wide), wide)
        value = jnp.broadcast_to(cond[:, cols], (8, wide))
        cond8[:, cols] = value
        for side in range(2):
            node = ends[side : side + 1, cols]
            into = pl.ds(pl.multiple_of(side * SEGS + step * wide, wide), wide)
            table[:, into] = spread(one_hot_rows(node & 255, 256), 1.0)
            owner8[:, into] = jnp.broadcast_to(node >> 8, (8, wide))
        return carry

    lax.fori_loop(0, SEGS // wide, make, 0)

    def split_into(target, tile, pairs):
        rows = 8 * pairs
        for q in range(0, pairs, 2):
            highs, lows = [], []
            for half in range(2):
                parts = [parts2(tile(2 * (q + i) + half)) for i in range(2)]
                highs.append(jnp.concatenate([part[0] for part in parts], axis=0))
                lows.append(jnp.concatenate([part[1] for part in parts], axis=0))
            target[8 * q : 8 * q + 16, :] = jnp.concatenate(highs, axis=1).astype(BF16)
            target[rows + 8 * q : rows + 8 * q + 16, :] = jnp.concatenate(lows, axis=1).astype(BF16)

    def gather(source, cols, pairs):
        full = dot_nn(source[...], table[:, cols])
        owner = owner8[:, cols]
        result = jnp.zeros((8, wide), F32)
        for q in range(pairs):
            value = full[8 * q : 8 * q + 8, :] + full[8 * (q + pairs) : 8 * (q + pairs) + 8, :]
            result = jnp.where(owner == q, value, result)
        return result

    def scatter(values, cols, pairs):
        left, right = [], []
        for value, at in zip(values, cols):
            owner = owner8[:, at]
            left.append(jnp.concatenate([jnp.where(owner == q, part, 0.0) for part in parts2(value) for q in range(pairs)], axis=0).astype(BF16))
            right.append(table[:, at])
        return dot_nt(jnp.concatenate(left, axis=1), jnp.concatenate(right, axis=1))

    def tile_of(source, b, pairs):
        rows, lanes = 8 * (b // 2), slice(TILE * (b % 2), TILE * (b % 2) + TILE)
        return source[rows : rows + 8, lanes] + source[8 * pairs + rows : 8 * pairs + rows + 8, lanes]

    pairs_all = BLOCKS // 2
    pairs_shown = SHOWN // 2

    def head_cols(step):
        return pl.ds(pl.multiple_of(step * wide, wide), wide)

    def tail_cols(step):
        return pl.ds(pl.multiple_of(SEGS + step * wide, wide), wide)

    def precondition(k):
        for b in range(BLOCKS):
            field = residual[8 * b : 8 * b + 8, :].astype(BF16)
            basis[k, 8 * b : 8 * b + 8, :] = dot_nn(field, inverse[b])

    for b in range(BLOCKS):
        weight = inflow_weight * mask[b : b + 1, :].astype(F32)
        residual[8 * b : 8 * b + 8, :] = weight * inflow[:, TILE * b : TILE * b + TILE]
    precondition(0)

    lane = lax.broadcasted_iota(I32, (8, TILE), 1)
    moments = jnp.zeros((8, TILE), F32)

    def total_of(k, other):
        acc = jnp.zeros((8, TILE), F32)
        for b in range(BLOCKS):
            acc = acc + basis[k, 8 * b : 8 * b + 8, :] * other(b)
        return jnp.sum(acc, axis=1, keepdims=True)

    def right_side(b):
        weight = inflow_weight * mask[b : b + 1, :].astype(F32)
        return weight * inflow[:, TILE * b : TILE * b + TILE]

    junc_first = INNER // wide
    junc_steps = JUNC // wide
    for k in range(3):
        split_into(pair, lambda b: basis[k, 8 * b : 8 * b + 8, :], pairs_all)
        for j in range(SHOWN):
            wanted = jnp.broadcast_to(shown[j : j + 1, :], (8, TILE))
            tile = jnp.zeros((8, TILE), F32)
            for b in range(BLOCKS):
                tile = jnp.where(wanted == b, basis[k, 8 * b : 8 * b + 8, :], tile)
            fwd_out[k, 8 * j : 8 * j + 8, :] = tile
        if k == 0:
            pl.semaphore_wait(barrier, len(partners))
        forward = pltpu.make_async_remote_copy(
            src_ref=fwd_out.at[k], dst_ref=fwd_in.at[k], send_sem=fwd_send.at[k], recv_sem=fwd_recv.at[k],
            device_id={"dom": lower}, device_id_type=MESH,
        )
        forward.start()
        moments = jnp.where(lane == k, total_of(k, right_side), moments)
        if k < 2:
            hcols = [head_cols(junc_first + step) for step in range(junc_steps)]
            tcols = [tail_cols(junc_first + step) for step in range(junc_steps)]
            back_out[...] = scatter([cond8[:, at] * gather(pair, at, pairs_all) for at in hcols], tcols, pairs_shown)
            for j in range(SHOWN):
                back_src[k, 8 * j : 8 * j + 8, :] = tile_of(back_out, j, pairs_shown)
            backward = pltpu.make_async_remote_copy(
                src_ref=back_src.at[k], dst_ref=back_in.at[k], send_sem=back_send.at[k], recv_sem=back_recv.at[k],
                device_id={"dom": upper}, device_id_type=MESH,
            )
            backward.start()
            out[...] = jnp.zeros_like(out)

            def inner(step, carry):
                values, cols = [], []
                for i in range(UNROLL):
                    h, t = head_cols(UNROLL * step + i), tail_cols(UNROLL * step + i)
                    weight = cond8[:, h]
                    values += [weight * gather(pair, t, pairs_all), weight * gather(pair, h, pairs_all)]
                    cols += [h, t]
                out[...] += scatter(values, cols, pairs_all)
                return carry

            lax.fori_loop(0, INNER // wide // UNROLL, inner, 0)
            forward.wait()
            split_into(upper_pair, lambda j: fwd_in[k, 8 * j : 8 * j + 8, :], pairs_shown)
            out[...] += scatter([cond8[:, h] * gather(upper_pair, t, pairs_shown) for h, t in zip(hcols, tcols)], hcols, pairs_all)
            backward.wait()
            for b in range(BLOCKS):
                acc = tile_of(out, b, pairs_all)
                for j in range(SHOWN):
                    acc = acc + jnp.where(jnp.broadcast_to(shown[j : j + 1, :], (8, TILE)) == b, back_in[k, 8 * j : 8 * j + 8, :], 0.0)
                image = degree[b : b + 1, :] * basis[k, 8 * b : 8 * b + 8, :] - acc
                images[k, 8 * b : 8 * b + 8, :] = image
                residual[8 * b : 8 * b + 8, :] = residual[8 * b : 8 * b + 8, :] - image
            precondition(k + 1)
            moments = jnp.where(lane == 3 + k, total_of(k, lambda b: images[k, 8 * b : 8 * b + 8, :]), moments)
            moments = jnp.where(lane == 6 + k, total_of(k + 1, lambda b: images[k, 8 * b : 8 * b + 8, :]), moments)
        else:
            def quadratic(step, carry):
                for i in range(UNROLL):
                    h, t = head_cols(UNROLL * step + i), tail_cols(UNROLL * step + i)
                    carry = carry + cond8[:, h] * gather(pair, h, pairs_all) * gather(pair, t, pairs_all)
                return carry

            crossed = lax.fori_loop(0, INNER // wide // UNROLL, quadratic, jnp.zeros((8, wide), F32))
            ahead = [cond8[:, head_cols(junc_first + step)] * gather(pair, head_cols(junc_first + step), pairs_all) for step in range(junc_steps)]
            forward.wait()
            split_into(upper_pair, lambda j: fwd_in[k, 8 * j : 8 * j + 8, :], pairs_shown)
            for step in range(junc_steps):
                crossed = crossed + ahead[step] * gather(upper_pair, tail_cols(junc_first + step), pairs_shown)
            square = total_of(2, lambda b: degree[b : b + 1, :] * basis[2, 8 * b : 8 * b + 8, :])
            square = square - 2.0 * jnp.sum(crossed, axis=1, keepdims=True)
            moments = jnp.where(lane == 5, square, moments)
            moments = jnp.where(lane == 8, total_of(2, lambda b: images[0, 8 * b : 8 * b + 8, :]), moments)

    def exchange(buffer, send, recv, index, count, target):
        copies = []
        for o in range(1, count):
            other = lax.rem(index + o, count)
            copies.append(pltpu.make_async_remote_copy(
                src_ref=buffer.at[index], dst_ref=buffer.at[index], send_sem=send.at[o], recv_sem=recv.at[o],
                device_id=target(other), device_id_type=MESH,
            ))
        for copy in copies:
            copy.start()
        for copy in copies:
            copy.wait()
        acc = buffer[0]
        for o in range(1, count):
            acc = acc + buffer[o]
        return acc

    one_buf[seat] = moments
    moments = exchange(one_buf, one_send, one_recv, seat, planes, lambda other: {"dom": plane_place(other)})
    two_buf[column] = moments
    moments = exchange(two_buf, two_send, two_recv, column, depth_z, lambda other: {"dom": column_place(other)})

    def entry(index):
        return jnp.broadcast_to(moments[:, index : index + 1], (8, TILE))

    b0, b1, b2, g00, g11, g22, g01, g12, g02 = [entry(i) for i in range(9)]

    def safe_inverse(value, scale):
        good = value > 1e-6 * scale
        return jnp.where(good, 1.0 / jnp.where(good, value, 1.0), 0.0)

    i0 = safe_inverse(g00, g00)
    l10 = g01 * i0
    l20 = g02 * i0
    i1 = safe_inverse(g11 - l10 * g01, g11)
    c12 = g12 - l20 * g01
    l21 = c12 * i1
    i2 = safe_inverse(g22 - l20 * g02 - l21 * c12, g22)
    w1 = b1 - l10 * b0
    w2 = b2 - l20 * b0 - l21 * w1
    y2 = w2 * i2
    y1 = w1 * i1 - l21 * y2
    y0 = b0 * i0 - l10 * y1 - l20 * y2
    for b in range(BLOCKS):
        rows = slice(8 * b, 8 * b + 8)
        value = y0 * basis[0, rows, :] + y1 * basis[1, rows, :] + y2 * basis[2, rows, :]
        pressure[:, TILE * b : TILE * b + TILE] = value
        rep_buf[mine, b : b + 1, :] = jnp.sum(value, axis=0, keepdims=True)
    total = exchange(rep_buf, rep_send, rep_recv, mine, reps, lambda other: {"rep": other})
    mean[...] = total * (1.0 / SCEN_ALL)


def vmem(count):
    return [pl.BlockSpec(memory_space=pltpu.VMEM)] * count


def smem(count):
    return [pl.BlockSpec(memory_space=pltpu.SMEM)] * count


def setup_call(ends, cond, mask, shown, arrived):
    return pl.pallas_call(
        setup_kernel,
        out_shape=(jax.ShapeDtypeStruct((BLOCKS, TILE, TILE), BF16), jax.ShapeDtypeStruct((BLOCKS, TILE), F32)),
        in_specs=vmem(3) + smem(1) + vmem(1),
        out_specs=tuple(vmem(2)),
        scratch_shapes=[
            pltpu.VMEM((NODES, TILE), F32),
            pltpu.VMEM((1, INNER), F32),
            pltpu.VMEM((64, TILE), F32),
            pltpu.VMEM((4 * CHUNKS, TILE), F32),
            pltpu.VMEM((4 * CHUNKS, TILE), F32),
            pltpu.VMEM((64, TILE), I32),
            pltpu.VMEM((BLOCKS * PANEL, TILE), F32),
            pltpu.VMEM((8, TILE, TILE), F32),
            pltpu.VMEM((BLOCKS * PANEL, TILE), F32),
            pltpu.SMEM((64, TILE), I32),
            pltpu.SemaphoreType.DMA,
        ],
        name="inverses",
    )(ends, cond, mask, shown, arrived)


def per_device(sizes, inflow, mask, ends, live, shown, radius, length):
    parts, depth_z, planes, reps = sizes
    mask = mask.reshape(BLOCKS, TILE)
    dma = pltpu.SemaphoreType.DMA
    cond, arrived = pl.pallas_call(
        functools.partial(head_kernel, parts),
        out_shape=(jax.ShapeDtypeStruct((1, SEGS), F32), jax.ShapeDtypeStruct((SHOWN, TILE), F32)),
        in_specs=vmem(3) + smem(1),
        out_specs=tuple(vmem(2)),
        scratch_shapes=[pltpu.VMEM((SHOWN, TILE), F32), pltpu.VMEM((SHOWN, TILE), F32), dma, dma],
        compiler_params=pltpu.CompilerParams(collective_id=0, has_side_effects=True),
        name="conductances",
    )(ends, radius.reshape(1, SEGS), length.reshape(1, SEGS), live)
    inverse, degree = setup_call(ends, cond, mask, shown, arrived)
    rows = 8 * BLOCKS
    back = 8 * SHOWN
    pressure, mean = pl.pallas_call(
        functools.partial(solve_kernel, sizes),
        out_shape=(jax.ShapeDtypeStruct((8, NODES), F32), jax.ShapeDtypeStruct((BLOCKS, TILE), F32)),
        in_specs=vmem(7),
        out_specs=tuple(vmem(2)),
        scratch_shapes=[
            pltpu.VMEM((2 * TILE, 2 * SEGS), BF16),
            pltpu.VMEM((8, 2 * SEGS), I32),
            pltpu.VMEM((8, SEGS), F32),
            pltpu.VMEM((3, rows, TILE), F32),
            pltpu.VMEM((2, rows, TILE), F32),
            pltpu.VMEM((rows, TILE), F32),
            pltpu.VMEM((rows, 2 * TILE), BF16),
            pltpu.VMEM((back, 2 * TILE), BF16),
            pltpu.VMEM((rows, 2 * TILE), F32),
            pltpu.VMEM((back, 2 * TILE), F32),
            pltpu.VMEM((3, back, TILE), F32),
            pltpu.VMEM((3, back, TILE), F32),
            pltpu.VMEM((2, back, TILE), F32),
            pltpu.VMEM((2, back, TILE), F32),
            pltpu.VMEM((planes, 8, TILE), F32),
            pltpu.VMEM((depth_z, 8, TILE), F32),
            pltpu.VMEM((reps, BLOCKS, TILE), F32),
            dma((3,)), dma((3,)), dma((2,)), dma((2,)),
            dma((planes,)), dma((planes,)), dma((depth_z,)), dma((depth_z,)), dma((reps,)), dma((reps,)),
        ],
        compiler_params=pltpu.CompilerParams(collective_id=1, has_side_effects=True),
        name="gradients",
    )(inflow, mask, ends, cond, degree, inverse, jnp.broadcast_to(shown[:, None], (SHOWN, TILE)))
    return pressure, mean.reshape(NODES)


def solution(mesh):
    in_specs = (P("rep", "dom"), P("dom"), P(None, "dom"), P("dom"), P("dom"), P("dom"), P("dom"))
    out_specs = (P("rep", "dom"), P("dom"))
    parts, reps = mesh.shape["dom"], mesh.shape["rep"]
    depth_z = 8 if parts == 64 else parts // 4
    sizes = (parts, depth_z, parts // depth_z, reps)
    return jax.shard_map(
        functools.partial(per_device, sizes), mesh=mesh, in_specs=in_specs, out_specs=out_specs, check_vma=False
    )
```

```python
import functools

import jax
import jax.numpy as jnp
from jax import lax
from jax.experimental import pallas as pl
from jax.experimental.pallas import tpu as pltpu
from jax.sharding import PartitionSpec as P

MESH = pl.DeviceIdType.MESH
F32 = jnp.float32
BF16 = jnp.bfloat16
I32 = jnp.int32

TILE = 128
BLOCKS = 32
NODES = 4096
SCEN_ALL = 32
JUNC = 1024
INNER = 6144
SEGS = 7168
SHOWN = 8
CHUNKS = 80
PANEL = 32
PITCH = 40
FOUR = 4
UNROLL = 4
SCANS = 4

leak_rate = 0.05
inflow_weight = 20.0


def dot_nt(a, b):
    return lax.dot_general(a, b, (((1,), (1,)), ((), ())), preferred_element_type=F32)


def dot_nn(a, b):
    return lax.dot_general(a, b, (((1,), (0,)), ((), ())), preferred_element_type=F32)


def dot_tn(a, b):
    return lax.dot_general(a, b, (((0,), (0,)), ((), ())), preferred_element_type=F32)


def parts2(x):
    hi = x.astype(BF16).astype(F32)
    return hi, x - hi


def parts3(x):
    hi = x.astype(BF16).astype(F32)
    rest = x - hi
    mid = rest.astype(BF16).astype(F32)
    return hi, mid, rest - mid


def one_hot_rows(row, count):
    ids = lax.broadcasted_iota(I32, (count, row.shape[1]), 0)
    return ids == row


def one_hot_lanes(row, count):
    ids = lax.broadcasted_iota(I32, (count, row.shape[1]), 0).astype(F32).astype(BF16)
    return jnp.where(ids == row.astype(F32).astype(BF16), jnp.ones((), BF16), jnp.zeros((), BF16))


def spread(mask, value):
    return jnp.where(mask, value, 0.0).astype(BF16)


def conductance(radius, seg_length):
    diameter = 2.0 * radius
    power = jnp.exp(0.645 * jnp.log(diameter))
    viscous = 220.0 * jnp.exp(-1.3 * diameter) + 3.2 - 2.44 * jnp.exp(-0.06 * power)
    scaled = diameter * 0.125
    scaled = scaled * scaled
    return scaled * scaled * (50.0 / seg_length) / viscous


def head_kernel(parts, ends, radius, length, live, cond_out, arrived, sent, landed, send_sem, recv_sem):
    place = lax.axis_index("dom")
    upper = lax.rem(place + 1, parts)
    lower = lax.rem(place + parts - 1, parts)
    barrier = pltpu.get_barrier_semaphore()
    for other in (upper, lower):
        pl.semaphore_signal(barrier, inc=1, device_id={"dom": other}, device_id_type=MESH)
    cond = conductance(radius[...], length[...])
    position = lax.broadcasted_iota(I32, (1, SEGS), 1)
    limit = jnp.where(position < INNER, jnp.full((1, SEGS), live[0], I32), jnp.full((1, SEGS), (parts - 1 - place) * SEGS, I32))
    cond = jnp.where(position < limit, cond, 0.0)
    high, low = parts2(cond)
    cond = high + low.astype(BF16).astype(F32)
    cond_out[...] = cond
    slot = ends[1:2, INNER:]
    junc = cond[:, INNER:]
    owner = one_hot_rows(slot >> 7, SHOWN)
    stack = jnp.concatenate([jnp.where(owner, part, 0.0) for part in parts2(junc)], axis=0).astype(BF16)
    lanes = spread(one_hot_rows(slot & 127, TILE), 1.0)
    sums = dot_nt(stack, lanes)
    sent[...] = sums[0:8] + sums[8:16]
    pl.semaphore_wait(barrier, 2)
    copy = pltpu.make_async_remote_copy(
        src_ref=sent, dst_ref=landed, send_sem=send_sem, recv_sem=recv_sem, device_id={"dom": upper}, device_id_type=MESH
    )
    copy.start()
    copy.wait()
    arrived[...] = landed[...]


def setup_kernel(
    ends, cond, mask, shown, arrived, inverse, degree_out, table, rank, degree, sums, packed, counts, old_rows, turned_rows, small, counts_smem, sem
):
    degree[...] = jnp.zeros_like(degree)
    sums[...] = jnp.zeros_like(sums)
    width = 256
    before = lax.broadcasted_iota(I32, (width, width), 0) < lax.broadcasted_iota(I32, (width, width), 1)
    before = jnp.where(before, 1.0, 0.0).astype(BF16)

    def add_degree(nodes, values):
        stacks, lanes = [], []
        for node, value in zip(nodes, values):
            owner = one_hot_rows(node >> 7, BLOCKS)
            stacks.append(jnp.concatenate([jnp.where(owner, part, 0.0) for part in parts2(value)], axis=0).astype(BF16))
            lanes.append(spread(one_hot_rows(node & 127, TILE), 1.0))
        degree[...] += dot_nt(jnp.concatenate(stacks, axis=1), jnp.concatenate(lanes, axis=1))

    def scan(step, carry):
        nodes, values = [], []
        for i in range(SCANS):
            cols = pl.ds(pl.multiple_of((SCANS * step + i) * width, width), width)
            head = ends[0:1, cols]
            tail = ends[1:2, cols]
            value = cond[:, cols]
            nodes += [head, tail]
            values += [value, value]
            bucket = jnp.where((head >> 7) == (tail >> 7), head >> 7, -1)
            member = one_hot_rows(bucket, BLOCKS)
            ahead = dot_nn(spread(member, 1.0), before)
            rank[:, cols] = jnp.sum(jnp.where(member, ahead + carry, 0.0), axis=0, keepdims=True)
            carry = carry + jnp.sum(jnp.where(member, 1.0, 0.0), axis=1, keepdims=True)
        add_degree(nodes, values)
        return carry

    total = lax.fori_loop(0, INNER // width // SCANS, scan, jnp.zeros((BLOCKS, 1), F32))
    add_degree([ends[0:1, INNER:]], [cond[:, INNER:]])
    deg = degree[0:32, :] + degree[32:64, :]
    block_id = lax.broadcasted_iota(I32, (BLOCKS, TILE), 0)
    for j in range(SHOWN):
        deg = deg + jnp.where(block_id == shown[j], arrived[j : j + 1, :], 0.0)
    deg = deg + (leak_rate + inflow_weight * mask[...].astype(F32))
    degree_out[...] = deg

    chunks = jnp.floor((jnp.broadcast_to(total, (BLOCKS, TILE)) + 127.0) * (1.0 / 128.0))
    below = lax.broadcasted_iota(I32, (BLOCKS, BLOCKS), 1) < lax.broadcasted_iota(I32, (BLOCKS, BLOCKS), 0)
    start = dot_nn(jnp.where(below, 1.0, 0.0).astype(BF16), chunks.astype(BF16))
    counts[0:32, :] = start.astype(I32)
    counts[32:64, :] = chunks.astype(I32)
    to_scalar = pltpu.make_async_copy(counts, counts_smem, sem)
    to_scalar.start()
    start_column = start[:, 0:1]
    wide = 1024

    def compact(step, carry):
        cols = pl.ds(pl.multiple_of(step * wide, wide), wide)
        head = ends[0:1, cols]
        tail = ends[1:2, cols]
        inside = (head >> 7) == (tail >> 7)
        bucket = jnp.where(inside, head >> 7, -1)
        base = jnp.sum(jnp.where(one_hot_rows(bucket, BLOCKS), start_column, 0.0), axis=0, keepdims=True)
        order = rank[:, cols].astype(I32)
        chunk = jnp.where(inside, base.astype(I32) + (order >> 7), -1)
        at_chunk = one_hot_rows(chunk, CHUNKS)
        values = ((head & 127).astype(F32), (tail & 127).astype(F32)) + parts2(cond[:, cols])
        stack = jnp.concatenate([spread(at_chunk, value) for value in values], axis=0)
        lanes = spread(one_hot_rows(order & 127, TILE), 1.0)
        sums[...] += dot_nt(stack, lanes)
        return carry

    lax.fori_loop(0, INNER // wide, compact, 0)
    packed[...] = sums[...]
    to_scalar.wait()

    row_id = lax.broadcasted_iota(I32, (TILE, TILE), 0)
    lane_id = lax.broadcasted_iota(I32, (TILE, TILE), 1)

    def chunk_of(row, live):
        head = packed[pl.ds(row, 1), :].astype(I32)
        tail = packed[pl.ds(row + CHUNKS, 1), :].astype(I32)
        at_head = row_id == head
        at_tail = row_id == tail
        left = jnp.concatenate([spread(at_head, 1.0), spread(at_tail, 1.0)], axis=1)
        right = []
        for k in range(2):
            value = packed[pl.ds(row + (2 + k) * CHUNKS, 1), :] * live
            right.append(jnp.concatenate([spread(at_tail, value), spread(at_head, value)], axis=1))
        both = dot_nt(left, jnp.concatenate(right, axis=0))
        return both[:, 0:TILE] + both[:, TILE:]

    def fill(step, carry):
        filled = []
        for i in range(FOUR):
            block = step * FOUR + i
            live = jnp.where(counts_smem[block + BLOCKS, 0] > 0, 1.0, 0.0)
            off = chunk_of(counts_smem[block, 0], live)
            filled.append(jnp.where(row_id == lane_id, degree_out[pl.ds(block, 1), :], -off))
        for i in range(FOUR):
            table[pl.ds(pl.multiple_of((step * FOUR + i) * TILE, TILE), TILE), :] = filled[i]
        return carry

    lax.fori_loop(0, BLOCKS // FOUR, fill, 0)

    def refill(block, carry):
        rows = pl.ds(pl.multiple_of(block * TILE, TILE), TILE)

        def more(index, inner):
            table[rows, :] = table[rows, :] - chunk_of(counts_smem[block, 0] + index, 1.0)
            return inner

        lax.fori_loop(1, counts_smem[block + BLOCKS, 0], more, 0)
        return carry

    lax.fori_loop(0, BLOCKS, refill, 0)

    panel_lane = lax.broadcasted_iota(I32, (PANEL, TILE), 1)
    panel_row = lax.broadcasted_iota(I32, (PANEL, TILE), 0)
    own_block = (row_id // PANEL) == (lane_id // PANEL)
    lane_block = panel_lane & (PANEL - 1)
    lane_group = panel_lane // PANEL

    def replicated(x, group):
        return jnp.take_along_axis(x, lane_block + group * PANEL, axis=1, mode="promise_in_bounds")

    def panel(index, carry):
        base = pl.multiple_of(index * PANEL, PANEL)
        for b in range(BLOCKS):
            old_rows[b * PITCH : b * PITCH + PANEL, :] = table[pl.ds(b * TILE + base, PANEL), :]
        for i in range(8):
            lines = [old_rows[pl.ds(8 * h + i, BLOCKS, stride=PITCH), :] for h in range(4)]
            turned_rows[i] = jnp.concatenate(lines, axis=0).T
        state = [turned_rows[i, pl.ds(base, PANEL), :] for i in range(8)]
        for first in range(0, PANEL, 4):
            coming = [replicated(state[(first + d) % 8], (first + d) // 8) for d in range(4)]
            for d in range(4):
                t = first + d
                at_row = panel_row == t
                now = coming[d]
                pivot = 1.0 / now[t : t + 1, :]
                new = jnp.where(at_row, pivot, now * pivot)
                for e in range(d + 1, 4):
                    x = coming[e]
                    coming[e] = jnp.where(at_row, 0.0, x) - x[t : t + 1, :] * new
                for i in range(8):
                    x = state[i]
                    rest = jnp.where(at_row, 0.0, x) - x[t : t + 1, :] * new
                    state[i] = jnp.where(lane_group == t // 8, new, rest) if i == t % 8 else rest
        for i in range(8):
            back = jnp.concatenate([state[i]] * 4, axis=0).T
            for h in range(4):
                small[pl.ds(8 * h + i, BLOCKS, stride=PITCH), :] = back[PANEL * h : PANEL * h + PANEL, :]
        unit = jnp.where(panel_lane == panel_row + base, 1.0, 0.0)
        in_panel = (panel_lane >= base) & (panel_lane < base + PANEL)
        keep = ((lane_id >= base) & (lane_id < base + PANEL)) | ((row_id >= base) & (row_id < base + PANEL))
        for g in range(BLOCKS // FOUR):
            starts = [PITCH * (g * FOUR + i) for i in range(FOUR)]
            diagonal = jnp.where(own_block, jnp.concatenate([small[at : at + PANEL, :] for at in starts], axis=0), 0.0)
            members = [jnp.where(in_panel, unit, old_rows[at : at + PANEL, :]) for at in starts]
            stack = jnp.concatenate(members, axis=0)
            dh, dm = [part.astype(BF16) for part in parts2(diagonal)]
            sh, sm = [part.astype(BF16) for part in parts2(stack)]
            def crossed(high, low):
                return jnp.concatenate([jnp.concatenate([high, low], axis=1), jnp.concatenate([low, high], axis=1)], axis=0)

            fresh = dot_nn(jnp.concatenate([dh, dm], axis=1), crossed(sh, sm))
            fresh = fresh[:, 0:TILE] + fresh[:, TILE:]
            turned = stack.T
            turned = jnp.where(row_id < base + PANEL, -turned, turned)
            parts = [part.astype(BF16) for part in parts2(turned)]
            fh, fm = [part.astype(BF16) for part in parts2(fresh)]
            none = jnp.zeros((TILE, TILE), BF16)
            left = [jnp.concatenate([jnp.where((lane_id // PANEL) == i, part, none) for part in parts], axis=1) for i in range(FOUR)]
            update = dot_nn(jnp.concatenate(left, axis=0), crossed(fh, fm))
            update = update[:, 0:TILE] + update[:, TILE:]
            for i in range(FOUR):
                rows = slice((g * FOUR + i) * TILE, (g * FOUR + i + 1) * TILE)
                table[rows, :] = jnp.where(keep, 0.0, table[rows, :]) - update[TILE * i : TILE * i + TILE, :]
        return carry

    lax.fori_loop(0, TILE // PANEL, panel, 0)

    for block in range(BLOCKS):
        inverse[block] = table[block * TILE : (block + 1) * TILE, :].astype(BF16)


def solve_kernel(
    sizes, inflow, mask, ends, cond, degree, inverse, shown, pressure, mean,
    table, owner8, cond8, basis, images, residual, pair, upper_pair, out, back_out, fwd_out, fwd_in, back_src, back_in,
    one_buf, two_buf, rep_buf,
    fwd_send, fwd_recv, back_send, back_recv, one_send, one_recv, two_send, two_recv, rep_send, rep_recv,
):
    parts, depth_z, planes, reps = sizes
    place = lax.axis_index("dom")
    mine = lax.axis_index("rep")
    upper = lax.rem(place + 1, parts)
    lower = lax.rem(place + parts - 1, parts)
    core = lax.rem(place, 2)
    column = lax.rem(place // 2, depth_z)
    line = place // (2 * depth_z)
    seat = line * 2 + core

    def plane_place(other):
        return ((other // 2) * depth_z + column) * 2 + lax.rem(other, 2)

    def column_place(other):
        return (line * depth_z + other) * 2 + core

    barrier = pltpu.get_barrier_semaphore()
    partners = [{"dom": upper}, {"dom": lower}]
    partners += [{"dom": plane_place(lax.rem(seat + o, planes))} for o in range(1, planes)]
    partners += [{"dom": column_place(lax.rem(column + o, depth_z))} for o in range(1, depth_z)]
    partners += [{"rep": lax.rem(mine + o, reps)} for o in range(1, reps)]
    for partner in partners:
        pl.semaphore_signal(barrier, inc=1, device_id=partner, device_id_type=MESH)

    wide = 256

    def make(step, carry):
        cols = pl.ds(pl.multiple_of(step * wide, wide), wide)
        value = jnp.broadcast_to(cond[:, cols], (8, wide))
        cond8[:, cols] = value
        for side in range(2):
            node = ends[side : side + 1, cols]
            into = pl.ds(pl.multiple_of(side * SEGS + step * wide, wide), wide)
            table[:, into] = one_hot_lanes(node & 255, 256)
            owner8[:, into] = jnp.broadcast_to(node >> 8, (8, wide))
        return carry

    lax.fori_loop(0, SEGS // wide, make, 0)

    def split_into(target, tile, pairs):
        rows = 8 * pairs
        for q in range(0, pairs, 2):
            highs, lows = [], []
            for half in range(2):
                parts = [parts2(tile(2 * (q + i) + half)) for i in range(2)]
                highs.append(jnp.concatenate([part[0] for part in parts], axis=0))
                lows.append(jnp.concatenate([part[1] for part in parts], axis=0))
            target[8 * q : 8 * q + 16, :] = jnp.concatenate(highs, axis=1).astype(BF16)
            target[rows + 8 * q : rows + 8 * q + 16, :] = jnp.concatenate(lows, axis=1).astype(BF16)

    def gather(source, cols, pairs, both):
        full = dot_nn(source[...] if both else source[0 : 8 * pairs, :], table[:, cols])
        owner = owner8[:, cols]
        result = jnp.zeros((8, wide), F32)
        for q in range(pairs):
            value = full[8 * q : 8 * q + 8, :]
            if both:
                value = value + full[8 * (q + pairs) : 8 * (q + pairs) + 8, :]
            result = jnp.where(owner == q, value, result)
        return result

    def scatter(values, cols, pairs):
        left, right = [], []
        for value, at in zip(values, cols):
            owner = owner8[:, at]
            left.append(jnp.concatenate([jnp.where(owner == q, part, 0.0) for part in parts2(value) for q in range(pairs)], axis=0).astype(BF16))
            right.append(table[:, at])
        return dot_nt(jnp.concatenate(left, axis=1), jnp.concatenate(right, axis=1))

    def tile_of(source, b, pairs):
        rows, lanes = 8 * (b // 2), slice(TILE * (b % 2), TILE * (b % 2) + TILE)
        return source[rows : rows + 8, lanes] + source[8 * pairs + rows : 8 * pairs + rows + 8, lanes]

    pairs_all = BLOCKS // 2
    pairs_shown = SHOWN // 2

    def head_cols(step):
        return pl.ds(pl.multiple_of(step * wide, wide), wide)

    def tail_cols(step):
        return pl.ds(pl.multiple_of(SEGS + step * wide, wide), wide)

    def precondition(k):
        for b in range(BLOCKS):
            field = residual[8 * b : 8 * b + 8, :].astype(BF16)
            value = dot_nn(field, inverse[b])
            if k == 1:
                value = value.astype(BF16).astype(F32)
            basis[k, 8 * b : 8 * b + 8, :] = value

    for b in range(BLOCKS):
        weight = inflow_weight * mask[b : b + 1, :].astype(F32)
        residual[8 * b : 8 * b + 8, :] = weight * inflow[:, TILE * b : TILE * b + TILE]
    precondition(0)

    lane = lax.broadcasted_iota(I32, (8, TILE), 1)
    moments = jnp.zeros((8, TILE), F32)

    def total_of(k, other):
        acc = jnp.zeros((8, TILE), F32)
        for b in range(BLOCKS):
            acc = acc + basis[k, 8 * b : 8 * b + 8, :] * other(b)
        return jnp.sum(acc, axis=1, keepdims=True)

    def right_side(b):
        weight = inflow_weight * mask[b : b + 1, :].astype(F32)
        return weight * inflow[:, TILE * b : TILE * b + TILE]

    junc_first = INNER // wide
    junc_steps = JUNC // wide
    for k in range(3):
        split_into(pair, lambda b: basis[k, 8 * b : 8 * b + 8, :], pairs_all)
        for j in range(SHOWN):
            wanted = jnp.full((8, TILE), shown[j], I32)
            tile = jnp.zeros((8, TILE), F32)
            for b in range(BLOCKS):
                tile = jnp.where(wanted == b, basis[k, 8 * b : 8 * b + 8, :], tile)
            fwd_out[k, 8 * j : 8 * j + 8, :] = tile
        if k == 0:
            pl.semaphore_wait(barrier, len(partners))
        forward = pltpu.make_async_remote_copy(
            src_ref=fwd_out.at[k], dst_ref=fwd_in.at[k], send_sem=fwd_send.at[k], recv_sem=fwd_recv.at[k],
            device_id={"dom": lower}, device_id_type=MESH,
        )
        forward.start()
        moments = jnp.where(lane == k, total_of(k, right_side), moments)
        if k < 2:
            hcols = [head_cols(junc_first + step) for step in range(junc_steps)]
            tcols = [tail_cols(junc_first + step) for step in range(junc_steps)]
            back_out[...] = scatter([cond8[:, at] * gather(pair, at, pairs_all, k == 0) for at in hcols], tcols, pairs_shown)
            for j in range(SHOWN):
                back_src[k, 8 * j : 8 * j + 8, :] = tile_of(back_out, j, pairs_shown)
            backward = pltpu.make_async_remote_copy(
                src_ref=back_src.at[k], dst_ref=back_in.at[k], send_sem=back_send.at[k], recv_sem=back_recv.at[k],
                device_id={"dom": upper}, device_id_type=MESH,
            )
            backward.start()
            out[...] = jnp.zeros_like(out)

            def inner(step, carry):
                values, cols = [], []
                for i in range(UNROLL):
                    h, t = head_cols(UNROLL * step + i), tail_cols(UNROLL * step + i)
                    weight = cond8[:, h]
                    values += [weight * gather(pair, t, pairs_all, k == 0), weight * gather(pair, h, pairs_all, k == 0)]
                    cols += [h, t]
                out[...] += scatter(values, cols, pairs_all)
                return carry

            lax.fori_loop(0, INNER // wide // UNROLL, inner, 0)
            forward.wait()
            split_into(upper_pair, lambda j: fwd_in[k, 8 * j : 8 * j + 8, :], pairs_shown)
            out[...] += scatter([cond8[:, h] * gather(upper_pair, t, pairs_shown, k == 0) for h, t in zip(hcols, tcols)], hcols, pairs_all)
            backward.wait()
            for b in range(BLOCKS):
                acc = tile_of(out, b, pairs_all)
                for j in range(SHOWN):
                    acc = acc + jnp.where(jnp.full((8, TILE), shown[j], I32) == b, back_in[k, 8 * j : 8 * j + 8, :], 0.0)
                image = degree[b : b + 1, :] * basis[k, 8 * b : 8 * b + 8, :] - acc
                images[k, 8 * b : 8 * b + 8, :] = image
                residual[8 * b : 8 * b + 8, :] = residual[8 * b : 8 * b + 8, :] - image
            precondition(k + 1)
            moments = jnp.where(lane == 3 + k, total_of(k, lambda b: images[k, 8 * b : 8 * b + 8, :]), moments)
            moments = jnp.where(lane == 6 + k, total_of(k + 1, lambda b: images[k, 8 * b : 8 * b + 8, :]), moments)
        else:
            def quadratic(step, carry):
                for i in range(UNROLL):
                    h, t = head_cols(UNROLL * step + i), tail_cols(UNROLL * step + i)
                    carry = carry + cond8[:, h] * gather(pair, h, pairs_all, k == 0) * gather(pair, t, pairs_all, k == 0)
                return carry

            crossed = lax.fori_loop(0, INNER // wide // UNROLL, quadratic, jnp.zeros((8, wide), F32))
            ahead = [cond8[:, head_cols(junc_first + step)] * gather(pair, head_cols(junc_first + step), pairs_all, k == 0) for step in range(junc_steps)]
            forward.wait()
            split_into(upper_pair, lambda j: fwd_in[k, 8 * j : 8 * j + 8, :], pairs_shown)
            for step in range(junc_steps):
                crossed = crossed + ahead[step] * gather(upper_pair, tail_cols(junc_first + step), pairs_shown, k == 0)
            square = total_of(2, lambda b: degree[b : b + 1, :] * basis[2, 8 * b : 8 * b + 8, :])
            square = square - 2.0 * jnp.sum(crossed, axis=1, keepdims=True)
            moments = jnp.where(lane == 5, square, moments)
            moments = jnp.where(lane == 8, total_of(2, lambda b: images[0, 8 * b : 8 * b + 8, :]), moments)

    def exchange(buffer, send, recv, index, count, target):
        copies = []
        for o in range(1, count):
            other = lax.rem(index + o, count)
            copies.append(pltpu.make_async_remote_copy(
                src_ref=buffer.at[index], dst_ref=buffer.at[index], send_sem=send.at[o], recv_sem=recv.at[o],
                device_id=target(other), device_id_type=MESH,
            ))
        for copy in copies:
            copy.start()
        for copy in copies:
            copy.wait()
        acc = buffer[0]
        for o in range(1, count):
            acc = acc + buffer[o]
        return acc

    one_buf[seat] = moments
    moments = exchange(one_buf, one_send, one_recv, seat, planes, lambda other: {"dom": plane_place(other)})
    two_buf[column] = moments
    moments = exchange(two_buf, two_send, two_recv, column, depth_z, lambda other: {"dom": column_place(other)})

    def entry(index):
        return jnp.broadcast_to(moments[:, index : index + 1], (8, TILE))

    b0, b1, b2, g00, g11, g22, g01, g12, g02 = [entry(i) for i in range(9)]

    def safe_inverse(value, scale):
        good = value > 1e-6 * scale
        return jnp.where(good, 1.0 / jnp.where(good, value, 1.0), 0.0)

    i0 = safe_inverse(g00, g00)
    l10 = g01 * i0
    l20 = g02 * i0
    i1 = safe_inverse(g11 - l10 * g01, g11)
    c12 = g12 - l20 * g01
    l21 = c12 * i1
    i2 = safe_inverse(g22 - l20 * g02 - l21 * c12, g22)
    w1 = b1 - l10 * b0
    w2 = b2 - l20 * b0 - l21 * w1
    y2 = w2 * i2
    y1 = w1 * i1 - l21 * y2
    y0 = b0 * i0 - l10 * y1 - l20 * y2
    for b in range(BLOCKS):
        rows = slice(8 * b, 8 * b + 8)
        value = y0 * basis[0, rows, :] + y1 * basis[1, rows, :] + y2 * basis[2, rows, :]
        pressure[:, TILE * b : TILE * b + TILE] = value
        rep_buf[mine, b : b + 1, :] = jnp.sum(value, axis=0, keepdims=True)
    total = exchange(rep_buf, rep_send, rep_recv, mine, reps, lambda other: {"rep": other})
    mean[...] = total * (1.0 / SCEN_ALL)


def vmem(count):
    return [pl.BlockSpec(memory_space=pltpu.VMEM)] * count


def smem(count):
    return [pl.BlockSpec(memory_space=pltpu.SMEM)] * count


def setup_call(ends, cond, mask, shown, arrived):
    return pl.pallas_call(
        setup_kernel,
        out_shape=(jax.ShapeDtypeStruct((BLOCKS, TILE, TILE), BF16), jax.ShapeDtypeStruct((BLOCKS, TILE), F32)),
        in_specs=vmem(3) + smem(1) + vmem(1),
        out_specs=tuple(vmem(2)),
        scratch_shapes=[
            pltpu.VMEM((NODES, TILE), F32),
            pltpu.VMEM((1, INNER), F32),
            pltpu.VMEM((64, TILE), F32),
            pltpu.VMEM((4 * CHUNKS, TILE), F32),
            pltpu.VMEM((4 * CHUNKS, TILE), F32),
            pltpu.VMEM((64, TILE), I32),
            pltpu.VMEM((BLOCKS * PITCH, TILE), F32),
            pltpu.VMEM((8, TILE, TILE), F32),
            pltpu.VMEM((BLOCKS * PITCH, TILE), F32),
            pltpu.SMEM((64, TILE), I32),
            pltpu.SemaphoreType.DMA,
        ],
        name="inverses",
    )(ends, cond, mask, shown, arrived)


def per_device(sizes, inflow, mask, ends, live, shown, radius, length):
    parts, depth_z, planes, reps = sizes
    mask = mask.reshape(BLOCKS, TILE)
    dma = pltpu.SemaphoreType.DMA
    cond, arrived = pl.pallas_call(
        functools.partial(head_kernel, parts),
        out_shape=(jax.ShapeDtypeStruct((1, SEGS), F32), jax.ShapeDtypeStruct((SHOWN, TILE), F32)),
        in_specs=vmem(3) + smem(1),
        out_specs=tuple(vmem(2)),
        scratch_shapes=[pltpu.VMEM((SHOWN, TILE), F32), pltpu.VMEM((SHOWN, TILE), F32), dma, dma],
        compiler_params=pltpu.CompilerParams(collective_id=0, has_side_effects=True),
        name="conductances",
    )(ends, radius.reshape(1, SEGS), length.reshape(1, SEGS), live)
    inverse, degree = setup_call(ends, cond, mask, shown, arrived)
    rows = 8 * BLOCKS
    back = 8 * SHOWN
    pressure, mean = pl.pallas_call(
        functools.partial(solve_kernel, sizes),
        out_shape=(jax.ShapeDtypeStruct((8, NODES), F32), jax.ShapeDtypeStruct((BLOCKS, TILE), F32)),
        in_specs=vmem(6) + smem(1),
        out_specs=tuple(vmem(2)),
        scratch_shapes=[
            pltpu.VMEM((2 * TILE, 2 * SEGS), BF16),
            pltpu.VMEM((8, 2 * SEGS), I32),
            pltpu.VMEM((8, SEGS), F32),
            pltpu.VMEM((3, rows, TILE), F32),
            pltpu.VMEM((2, rows, TILE), F32),
            pltpu.VMEM((rows, TILE), F32),
            pltpu.VMEM((rows, 2 * TILE), BF16),
            pltpu.VMEM((back, 2 * TILE), BF16),
            pltpu.VMEM((rows, 2 * TILE), F32),
            pltpu.VMEM((back, 2 * TILE), F32),
            pltpu.VMEM((3, back, TILE), F32),
            pltpu.VMEM((3, back, TILE), F32),
            pltpu.VMEM((2, back, TILE), F32),
            pltpu.VMEM((2, back, TILE), F32),
            pltpu.VMEM((planes, 8, TILE), F32),
            pltpu.VMEM((depth_z, 8, TILE), F32),
            pltpu.VMEM((reps, BLOCKS, TILE), F32),
            dma((3,)), dma((3,)), dma((2,)), dma((2,)),
            dma((planes,)), dma((planes,)), dma((depth_z,)), dma((depth_z,)), dma((reps,)), dma((reps,)),
        ],
        compiler_params=pltpu.CompilerParams(collective_id=1, has_side_effects=True),
        name="gradients",
    )(inflow, mask, ends, cond, degree, inverse, shown)
    return pressure, mean.reshape(NODES)


def solution(mesh):
    in_specs = (P("rep", "dom"), P("dom"), P(None, "dom"), P("dom"), P("dom"), P("dom"), P("dom"))
    out_specs = (P("rep", "dom"), P("dom"))
    parts, reps = mesh.shape["dom"], mesh.shape["rep"]
    depth_z = 8 if parts == 64 else parts // 4
    sizes = (parts, depth_z, parts // depth_z, reps)
    return jax.shard_map(
        functools.partial(per_device, sizes), mesh=mesh, in_specs=in_specs, out_specs=out_specs, check_vma=False
    )
```

```python
import functools

import jax
import jax.numpy as jnp
from jax import lax
from jax.experimental import pallas as pl
from jax.experimental.pallas import tpu as pltpu
from jax.sharding import PartitionSpec as P

MESH = pl.DeviceIdType.MESH
F32 = jnp.float32
BF16 = jnp.bfloat16
I32 = jnp.int32

TILE = 128
BLOCKS = 32
NODES = 4096
SCEN_ALL = 32
JUNC = 1024
INNER = 6144
SEGS = 7168
SHOWN = 8
CHUNKS = 80
PANEL = 32
PITCH = 40
FOUR = 4
UNROLL = 8
SCANS = 4
FILLS = 8

leak_rate = 0.05
inflow_weight = 20.0


def dot_nt(a, b):
    return lax.dot_general(a, b, (((1,), (1,)), ((), ())), preferred_element_type=F32)


def dot_nn(a, b):
    return lax.dot_general(a, b, (((1,), (0,)), ((), ())), preferred_element_type=F32)


def dot_tn(a, b):
    return lax.dot_general(a, b, (((0,), (0,)), ((), ())), preferred_element_type=F32)


def parts2(x):
    hi = x.astype(BF16).astype(F32)
    return hi, x - hi


def parts3(x):
    hi = x.astype(BF16).astype(F32)
    rest = x - hi
    mid = rest.astype(BF16).astype(F32)
    return hi, mid, rest - mid


def one_hot_rows(row, count):
    ids = lax.broadcasted_iota(I32, (count, row.shape[1]), 0)
    return ids == row


def one_hot_lanes(row, count):
    ids = lax.broadcasted_iota(I32, (count, row.shape[1]), 0).astype(F32).astype(BF16)
    return jnp.where(ids == row.astype(F32).astype(BF16), jnp.ones((), BF16), jnp.zeros((), BF16))


def spread(mask, value):
    return jnp.where(mask, value, 0.0).astype(BF16)


def conductance(radius, seg_length):
    diameter = 2.0 * radius
    power = jnp.exp(0.645 * jnp.log(diameter))
    viscous = 220.0 * jnp.exp(-1.3 * diameter) + 3.2 - 2.44 * jnp.exp(-0.06 * power)
    scaled = diameter * 0.125
    scaled = scaled * scaled
    return scaled * scaled * (50.0 / seg_length) / viscous


def head_kernel(parts, ends, radius, length, live, cond_out, arrived, sent, landed, send_sem, recv_sem):
    place = lax.axis_index("dom")
    upper = lax.rem(place + 1, parts)
    lower = lax.rem(place + parts - 1, parts)
    barrier = pltpu.get_barrier_semaphore()
    for other in (upper, lower):
        pl.semaphore_signal(barrier, inc=1, device_id={"dom": other}, device_id_type=MESH)
    cond = conductance(radius[...], length[...])
    position = lax.broadcasted_iota(I32, (1, SEGS), 1)
    limit = jnp.where(position < INNER, jnp.full((1, SEGS), live[0], I32), jnp.full((1, SEGS), (parts - 1 - place) * SEGS, I32))
    cond = jnp.where(position < limit, cond, 0.0)
    high, low = parts2(cond)
    cond = high + low.astype(BF16).astype(F32)
    cond_out[...] = cond
    slot = ends[1:2, INNER:]
    junc = cond[:, INNER:]
    owner = one_hot_rows(slot >> 7, SHOWN)
    stack = jnp.concatenate([jnp.where(owner, part, 0.0) for part in parts2(junc)], axis=0).astype(BF16)
    lanes = spread(one_hot_rows(slot & 127, TILE), 1.0)
    sums = dot_nt(stack, lanes)
    sent[...] = sums[0:8] + sums[8:16]
    pl.semaphore_wait(barrier, 2)
    copy = pltpu.make_async_remote_copy(
        src_ref=sent, dst_ref=landed, send_sem=send_sem, recv_sem=recv_sem, device_id={"dom": upper}, device_id_type=MESH
    )
    copy.start()
    copy.wait()
    arrived[...] = landed[...]


def setup_kernel(
    ends, cond, mask, shown, arrived, inverse, degree_out, table, rank, degree, sums, packed, counts, old_rows, turned_rows, small, counts_smem, sem
):
    degree[...] = jnp.zeros_like(degree)
    sums[...] = jnp.zeros_like(sums)
    width = 256
    before = lax.broadcasted_iota(I32, (width, width), 0) < lax.broadcasted_iota(I32, (width, width), 1)
    before = jnp.where(before, 1.0, 0.0).astype(BF16)

    def add_degree(nodes, values):
        stacks, lanes = [], []
        for node, value in zip(nodes, values):
            owner = one_hot_rows(node >> 7, BLOCKS)
            stacks.append(jnp.concatenate([jnp.where(owner, part, 0.0) for part in parts2(value)], axis=0).astype(BF16))
            lanes.append(one_hot_lanes(node & 127, TILE))
        degree[...] += dot_nt(jnp.concatenate(stacks, axis=1), jnp.concatenate(lanes, axis=1))

    def scan(step, carry):
        nodes, values = [], []
        for i in range(SCANS):
            cols = pl.ds(pl.multiple_of((SCANS * step + i) * width, width), width)
            head = ends[0:1, cols]
            tail = ends[1:2, cols]
            value = cond[:, cols]
            nodes += [head, tail]
            values += [value, value]
            bucket = jnp.where((head >> 7) == (tail >> 7), head >> 7, -1)
            member = one_hot_rows(bucket, BLOCKS)
            ahead = dot_nn(spread(member, 1.0), before)
            rank[:, cols] = jnp.sum(jnp.where(member, ahead + carry, 0.0), axis=0, keepdims=True)
            carry = carry + jnp.sum(jnp.where(member, 1.0, 0.0), axis=1, keepdims=True)
        add_degree(nodes, values)
        return carry

    total = lax.fori_loop(0, INNER // width // SCANS, scan, jnp.zeros((BLOCKS, 1), F32))
    add_degree([ends[0:1, INNER:]], [cond[:, INNER:]])
    deg = degree[0:32, :] + degree[32:64, :]
    block_id = lax.broadcasted_iota(I32, (BLOCKS, TILE), 0)
    for j in range(SHOWN):
        deg = deg + jnp.where(block_id == shown[j], arrived[j : j + 1, :], 0.0)
    deg = deg + (leak_rate + inflow_weight * mask[...].astype(F32))
    degree_out[...] = deg

    chunks = jnp.floor((jnp.broadcast_to(total, (BLOCKS, TILE)) + 127.0) * (1.0 / 128.0))
    below = lax.broadcasted_iota(I32, (BLOCKS, BLOCKS), 1) < lax.broadcasted_iota(I32, (BLOCKS, BLOCKS), 0)
    start = dot_nn(jnp.where(below, 1.0, 0.0).astype(BF16), chunks.astype(BF16))
    counts[0:32, :] = start.astype(I32)
    counts[32:64, :] = chunks.astype(I32)
    counts[64:72, :] = jnp.broadcast_to(jnp.max(chunks, axis=0, keepdims=True), (8, TILE)).astype(I32)
    to_scalar = pltpu.make_async_copy(counts, counts_smem, sem)
    to_scalar.start()
    start_column = start[:, 0:1]
    wide = 1024

    def compact(step, carry):
        cols = pl.ds(pl.multiple_of(step * wide, wide), wide)
        head = ends[0:1, cols]
        tail = ends[1:2, cols]
        inside = (head >> 7) == (tail >> 7)
        bucket = jnp.where(inside, head >> 7, -1)
        base = jnp.sum(jnp.where(one_hot_rows(bucket, BLOCKS), start_column, 0.0), axis=0, keepdims=True)
        order = rank[:, cols].astype(I32)
        chunk = jnp.where(inside, base.astype(I32) + (order >> 7), -1)
        at_chunk = one_hot_rows(chunk, CHUNKS)
        values = ((head & 127).astype(F32), (tail & 127).astype(F32)) + parts2(cond[:, cols])
        stack = jnp.concatenate([spread(at_chunk, value) for value in values], axis=0)
        lanes = one_hot_lanes(order & 127, TILE)
        sums[...] += dot_nt(stack, lanes)
        return carry

    lax.fori_loop(0, INNER // wide, compact, 0)
    packed[...] = sums[...]
    to_scalar.wait()

    row_id = lax.broadcasted_iota(I32, (TILE, TILE), 0)
    lane_id = lax.broadcasted_iota(I32, (TILE, TILE), 1)

    def chunk_of(row, live):
        head = packed[pl.ds(row, 1), :].astype(I32)
        tail = packed[pl.ds(row + CHUNKS, 1), :].astype(I32)
        at_head = row_id == head
        at_tail = row_id == tail
        left = jnp.concatenate([spread(at_head, 1.0), spread(at_tail, 1.0)], axis=1)
        right = []
        for k in range(2):
            value = packed[pl.ds(row + (2 + k) * CHUNKS, 1), :] * live
            right.append(jnp.concatenate([spread(at_tail, value), spread(at_head, value)], axis=1))
        both = dot_nt(left, jnp.concatenate(right, axis=0))
        return both[:, 0:TILE] + both[:, TILE:]

    def fill(step, carry):
        filled = []
        for i in range(FILLS):
            block = step * FILLS + i
            live = jnp.where(counts_smem[block + BLOCKS, 0] > 0, 1.0, 0.0)
            off = chunk_of(counts_smem[block, 0], live)
            filled.append(jnp.where(row_id == lane_id, degree_out[pl.ds(block, 1), :], -off))
        for i in range(FILLS):
            table[pl.ds(pl.multiple_of((step * FILLS + i) * TILE, TILE), TILE), :] = filled[i]
        return carry

    lax.fori_loop(0, BLOCKS // FILLS, fill, 0)

    def refill(block, carry):
        rows = pl.ds(pl.multiple_of(block * TILE, TILE), TILE)

        def more(index, inner):
            table[rows, :] = table[rows, :] - chunk_of(counts_smem[block, 0] + index, 1.0)
            return inner

        lax.fori_loop(1, counts_smem[block + BLOCKS, 0], more, 0)
        return carry

    @pl.when(counts_smem[64, 0] > 1)
    def _():
        lax.fori_loop(0, BLOCKS, refill, 0)

    panel_lane = lax.broadcasted_iota(I32, (PANEL, TILE), 1)
    panel_row = lax.broadcasted_iota(I32, (PANEL, TILE), 0)
    own_block = (row_id // PANEL) == (lane_id // PANEL)
    lane_block = panel_lane & (PANEL - 1)
    lane_group = panel_lane // PANEL

    def replicated(x, group):
        return jnp.take_along_axis(x, lane_block + group * PANEL, axis=1, mode="promise_in_bounds")

    def panel(index, carry):
        base = pl.multiple_of(index * PANEL, PANEL)
        for b in range(BLOCKS):
            old_rows[b * PITCH : b * PITCH + PANEL, :] = table[pl.ds(b * TILE + base, PANEL), :]
        for i in range(8):
            lines = [old_rows[pl.ds(8 * h + i, BLOCKS, stride=PITCH), :] for h in range(4)]
            turned_rows[i] = jnp.concatenate(lines, axis=0).T
        state = [turned_rows[i, pl.ds(base, PANEL), :] for i in range(8)]
        for first in range(0, PANEL, 4):
            coming = [replicated(state[(first + d) % 8], (first + d) // 8) for d in range(4)]
            for d in range(4):
                t = first + d
                at_row = panel_row == t
                now = coming[d]
                pivot = 1.0 / now[t : t + 1, :]
                new = jnp.where(at_row, pivot, now * pivot)
                for e in range(d + 1, 4):
                    x = coming[e]
                    coming[e] = jnp.where(at_row, 0.0, x) - x[t : t + 1, :] * new
                for i in range(8):
                    x = state[i]
                    rest = jnp.where(at_row, 0.0, x) - x[t : t + 1, :] * new
                    state[i] = jnp.where(lane_group == t // 8, new, rest) if i == t % 8 else rest
        for i in range(8):
            back = jnp.concatenate([state[i]] * 4, axis=0).T
            for h in range(4):
                small[pl.ds(8 * h + i, BLOCKS, stride=PITCH), :] = back[PANEL * h : PANEL * h + PANEL, :]
        unit = jnp.where(panel_lane == panel_row + base, 1.0, 0.0)
        in_panel = (panel_lane >= base) & (panel_lane < base + PANEL)
        keep = ((lane_id >= base) & (lane_id < base + PANEL)) | ((row_id >= base) & (row_id < base + PANEL))
        for g in range(BLOCKS // FOUR):
            starts = [PITCH * (g * FOUR + i) for i in range(FOUR)]
            diagonal = jnp.where(own_block, jnp.concatenate([small[at : at + PANEL, :] for at in starts], axis=0), 0.0)
            members = [jnp.where(in_panel, unit, old_rows[at : at + PANEL, :]) for at in starts]
            stack = jnp.concatenate(members, axis=0)
            dh, dm = [part.astype(BF16) for part in parts2(diagonal)]
            sh, sm = [part.astype(BF16) for part in parts2(stack)]
            def crossed(high, low):
                return jnp.concatenate([jnp.concatenate([high, low], axis=1), jnp.concatenate([low, high], axis=1)], axis=0)

            fresh = dot_nn(jnp.concatenate([dh, dm], axis=1), crossed(sh, sm))
            fresh = fresh[:, 0:TILE] + fresh[:, TILE:]
            turned = stack.T
            turned = jnp.where(row_id < base + PANEL, -turned, turned)
            parts = [part.astype(BF16) for part in parts2(turned)]
            fh, fm = [part.astype(BF16) for part in parts2(fresh)]
            none = jnp.zeros((TILE, TILE), BF16)
            left = [jnp.concatenate([jnp.where((lane_id // PANEL) == i, part, none) for part in parts], axis=1) for i in range(FOUR)]
            update = dot_nn(jnp.concatenate(left, axis=0), crossed(fh, fm))
            update = update[:, 0:TILE] + update[:, TILE:]
            for i in range(FOUR):
                rows = slice((g * FOUR + i) * TILE, (g * FOUR + i + 1) * TILE)
                table[rows, :] = jnp.where(keep, 0.0, table[rows, :]) - update[TILE * i : TILE * i + TILE, :]
        return carry

    lax.fori_loop(0, TILE // PANEL, panel, 0)

    for block in range(BLOCKS):
        inverse[block] = table[block * TILE : (block + 1) * TILE, :].astype(BF16)


def solve_kernel(
    sizes, inflow, mask, ends, cond, degree, inverse, shown, pressure, mean,
    table, owner8, cond8, basis, images, residual, pair, upper_pair, out, back_out, fwd_out, fwd_in, back_src, back_in,
    one_buf, two_buf, rep_buf,
    fwd_send, fwd_recv, back_send, back_recv, one_send, one_recv, two_send, two_recv, rep_send, rep_recv,
):
    parts, depth_z, planes, reps = sizes
    place = lax.axis_index("dom")
    mine = lax.axis_index("rep")
    upper = lax.rem(place + 1, parts)
    lower = lax.rem(place + parts - 1, parts)
    core = lax.rem(place, 2)
    column = lax.rem(place // 2, depth_z)
    line = place // (2 * depth_z)
    seat = line * 2 + core

    def plane_place(other):
        return ((other // 2) * depth_z + column) * 2 + lax.rem(other, 2)

    def column_place(other):
        return (line * depth_z + other) * 2 + core

    barrier = pltpu.get_barrier_semaphore()
    partners = [{"dom": upper}, {"dom": lower}]
    partners += [{"dom": plane_place(lax.rem(seat + o, planes))} for o in range(1, planes)]
    partners += [{"dom": column_place(lax.rem(column + o, depth_z))} for o in range(1, depth_z)]
    partners += [{"rep": lax.rem(mine + o, reps)} for o in range(1, reps)]
    for partner in partners:
        pl.semaphore_signal(barrier, inc=1, device_id=partner, device_id_type=MESH)

    wide = 256

    def make(step, carry):
        cols = pl.ds(pl.multiple_of(step * wide, wide), wide)
        value = jnp.broadcast_to(cond[:, cols], (8, wide))
        cond8[:, cols] = value
        for side in range(2):
            node = ends[side : side + 1, cols]
            into = pl.ds(pl.multiple_of(side * SEGS + step * wide, wide), wide)
            table[:, into] = one_hot_lanes(node & 255, 256)
            owner8[:, into] = jnp.broadcast_to(node >> 8, (8, wide))
        return carry

    lax.fori_loop(0, SEGS // wide, make, 0, unroll=4)

    def split_into(target, tile, pairs):
        rows = 8 * pairs
        for q in range(0, pairs, 2):
            highs, lows = [], []
            for half in range(2):
                parts = [parts2(tile(2 * (q + i) + half)) for i in range(2)]
                highs.append(jnp.concatenate([part[0] for part in parts], axis=0))
                lows.append(jnp.concatenate([part[1] for part in parts], axis=0))
            target[8 * q : 8 * q + 16, :] = jnp.concatenate(highs, axis=1).astype(BF16)
            target[rows + 8 * q : rows + 8 * q + 16, :] = jnp.concatenate(lows, axis=1).astype(BF16)

    def gather(source, cols, pairs, both):
        full = dot_nn(source[...] if both else source[0 : 8 * pairs, :], table[:, cols])
        owner = owner8[:, cols]
        result = jnp.zeros((8, wide), F32)
        for q in range(pairs):
            value = full[8 * q : 8 * q + 8, :]
            if both:
                value = value + full[8 * (q + pairs) : 8 * (q + pairs) + 8, :]
            result = jnp.where(owner == q, value, result)
        return result

    def scatter(values, cols, pairs):
        left, right = [], []
        for value, at in zip(values, cols):
            owner = owner8[:, at]
            left.append(jnp.concatenate([jnp.where(owner == q, part, 0.0) for part in parts2(value) for q in range(pairs)], axis=0).astype(BF16))
            right.append(table[:, at])
        return dot_nt(jnp.concatenate(left, axis=1), jnp.concatenate(right, axis=1))

    def tile_of(source, b, pairs):
        rows, lanes = 8 * (b // 2), slice(TILE * (b % 2), TILE * (b % 2) + TILE)
        return source[rows : rows + 8, lanes] + source[8 * pairs + rows : 8 * pairs + rows + 8, lanes]

    pairs_all = BLOCKS // 2
    pairs_shown = SHOWN // 2

    def head_cols(step):
        return pl.ds(pl.multiple_of(step * wide, wide), wide)

    def tail_cols(step):
        return pl.ds(pl.multiple_of(SEGS + step * wide, wide), wide)

    def precondition(k):
        for b in range(BLOCKS):
            field = residual[8 * b : 8 * b + 8, :].astype(BF16)
            value = dot_nn(field, inverse[b])
            if k == 1:
                value = value.astype(BF16).astype(F32)
            basis[k, 8 * b : 8 * b + 8, :] = value

    for b in range(BLOCKS):
        weight = inflow_weight * mask[b : b + 1, :].astype(F32)
        residual[8 * b : 8 * b + 8, :] = weight * inflow[:, TILE * b : TILE * b + TILE]
    precondition(0)

    lane = lax.broadcasted_iota(I32, (8, TILE), 1)
    moments = jnp.zeros((8, TILE), F32)

    def total_of(k, other):
        accs = [jnp.zeros((8, TILE), F32)] * 4
        for b in range(BLOCKS):
            accs[b % 4] = accs[b % 4] + basis[k, 8 * b : 8 * b + 8, :] * other(b)
        return jnp.sum((accs[0] + accs[1]) + (accs[2] + accs[3]), axis=1, keepdims=True)

    def right_side(b):
        weight = inflow_weight * mask[b : b + 1, :].astype(F32)
        return weight * inflow[:, TILE * b : TILE * b + TILE]

    junc_first = INNER // wide
    junc_steps = JUNC // wide
    for k in range(3):
        split_into(pair, lambda b: basis[k, 8 * b : 8 * b + 8, :], pairs_all)
        for j in range(SHOWN):
            wanted = jnp.full((8, TILE), shown[j], I32)
            tile = jnp.zeros((8, TILE), F32)
            for b in range(BLOCKS):
                tile = jnp.where(wanted == b, basis[k, 8 * b : 8 * b + 8, :], tile)
            fwd_out[k, 8 * j : 8 * j + 8, :] = tile
        if k == 0:
            pl.semaphore_wait(barrier, len(partners))
        forward = pltpu.make_async_remote_copy(
            src_ref=fwd_out.at[k], dst_ref=fwd_in.at[k], send_sem=fwd_send.at[k], recv_sem=fwd_recv.at[k],
            device_id={"dom": lower}, device_id_type=MESH,
        )
        forward.start()
        moments = jnp.where(lane == k, total_of(k, right_side), moments)
        if k < 2:
            hcols = [head_cols(junc_first + step) for step in range(junc_steps)]
            tcols = [tail_cols(junc_first + step) for step in range(junc_steps)]
            back_out[...] = scatter([cond8[:, at] * gather(pair, at, pairs_all, k == 0) for at in hcols], tcols, pairs_shown)
            for j in range(SHOWN):
                back_src[k, 8 * j : 8 * j + 8, :] = tile_of(back_out, j, pairs_shown)
            backward = pltpu.make_async_remote_copy(
                src_ref=back_src.at[k], dst_ref=back_in.at[k], send_sem=back_send.at[k], recv_sem=back_recv.at[k],
                device_id={"dom": upper}, device_id_type=MESH,
            )
            backward.start()
            out[...] = jnp.zeros_like(out)

            def inner(step, carry):
                values, cols = [], []
                for i in range(UNROLL):
                    h, t = head_cols(UNROLL * step + i), tail_cols(UNROLL * step + i)
                    weight = cond8[:, h]
                    values += [weight * gather(pair, t, pairs_all, k == 0), weight * gather(pair, h, pairs_all, k == 0)]
                    cols += [h, t]
                out[...] += scatter(values, cols, pairs_all)
                return carry

            lax.fori_loop(0, INNER // wide // UNROLL, inner, 0)
            forward.wait()
            split_into(upper_pair, lambda j: fwd_in[k, 8 * j : 8 * j + 8, :], pairs_shown)
            out[...] += scatter([cond8[:, h] * gather(upper_pair, t, pairs_shown, k == 0) for h, t in zip(hcols, tcols)], hcols, pairs_all)
            backward.wait()
            for b in range(BLOCKS):
                acc = tile_of(out, b, pairs_all)
                for j in range(SHOWN):
                    acc = acc + jnp.where(jnp.full((8, TILE), shown[j], I32) == b, back_in[k, 8 * j : 8 * j + 8, :], 0.0)
                image = degree[b : b + 1, :] * basis[k, 8 * b : 8 * b + 8, :] - acc
                images[k, 8 * b : 8 * b + 8, :] = image
                residual[8 * b : 8 * b + 8, :] = residual[8 * b : 8 * b + 8, :] - image
            precondition(k + 1)
            moments = jnp.where(lane == 3 + k, total_of(k, lambda b: images[k, 8 * b : 8 * b + 8, :]), moments)
            moments = jnp.where(lane == 6 + k, total_of(k + 1, lambda b: images[k, 8 * b : 8 * b + 8, :]), moments)
        else:
            def quadratic(step, carry):
                for i in range(UNROLL):
                    h, t = head_cols(UNROLL * step + i), tail_cols(UNROLL * step + i)
                    carry = carry + cond8[:, h] * gather(pair, h, pairs_all, k == 0) * gather(pair, t, pairs_all, k == 0)
                return carry

            crossed = lax.fori_loop(0, INNER // wide // UNROLL, quadratic, jnp.zeros((8, wide), F32))
            ahead = [cond8[:, head_cols(junc_first + step)] * gather(pair, head_cols(junc_first + step), pairs_all, k == 0) for step in range(junc_steps)]
            forward.wait()
            split_into(upper_pair, lambda j: fwd_in[k, 8 * j : 8 * j + 8, :], pairs_shown)
            for step in range(junc_steps):
                crossed = crossed + ahead[step] * gather(upper_pair, tail_cols(junc_first + step), pairs_shown, k == 0)
            square = total_of(2, lambda b: degree[b : b + 1, :] * basis[2, 8 * b : 8 * b + 8, :])
            square = square - 2.0 * jnp.sum(crossed, axis=1, keepdims=True)
            moments = jnp.where(lane == 5, square, moments)
            moments = jnp.where(lane == 8, total_of(2, lambda b: images[0, 8 * b : 8 * b + 8, :]), moments)

    def exchange(buffer, send, recv, index, count, target):
        copies = []
        for o in range(1, count):
            other = lax.rem(index + o, count)
            copies.append(pltpu.make_async_remote_copy(
                src_ref=buffer.at[index], dst_ref=buffer.at[index], send_sem=send.at[o], recv_sem=recv.at[o],
                device_id=target(other), device_id_type=MESH,
            ))
        for copy in copies:
            copy.start()
        for copy in copies:
            copy.wait()
        acc = buffer[0]
        for o in range(1, count):
            acc = acc + buffer[o]
        return acc

    one_buf[seat] = moments
    moments = exchange(one_buf, one_send, one_recv, seat, planes, lambda other: {"dom": plane_place(other)})
    two_buf[column] = moments
    moments = exchange(two_buf, two_send, two_recv, column, depth_z, lambda other: {"dom": column_place(other)})

    def entry(index):
        return jnp.broadcast_to(moments[:, index : index + 1], (8, TILE))

    b0, b1, b2, g00, g11, g22, g01, g12, g02 = [entry(i) for i in range(9)]

    def safe_inverse(value, scale):
        good = value > 1e-6 * scale
        return jnp.where(good, 1.0 / jnp.where(good, value, 1.0), 0.0)

    i0 = safe_inverse(g00, g00)
    l10 = g01 * i0
    l20 = g02 * i0
    i1 = safe_inverse(g11 - l10 * g01, g11)
    c12 = g12 - l20 * g01
    l21 = c12 * i1
    i2 = safe_inverse(g22 - l20 * g02 - l21 * c12, g22)
    w1 = b1 - l10 * b0
    w2 = b2 - l20 * b0 - l21 * w1
    y2 = w2 * i2
    y1 = w1 * i1 - l21 * y2
    y0 = b0 * i0 - l10 * y1 - l20 * y2
    for b in range(BLOCKS):
        rows = slice(8 * b, 8 * b + 8)
        value = y0 * basis[0, rows, :] + y1 * basis[1, rows, :] + y2 * basis[2, rows, :]
        pressure[:, TILE * b : TILE * b + TILE] = value
        rep_buf[mine, b : b + 1, :] = jnp.sum(value, axis=0, keepdims=True)
    total = exchange(rep_buf, rep_send, rep_recv, mine, reps, lambda other: {"rep": other})
    mean[...] = total * (1.0 / SCEN_ALL)


def vmem(count):
    return [pl.BlockSpec(memory_space=pltpu.VMEM)] * count


def smem(count):
    return [pl.BlockSpec(memory_space=pltpu.SMEM)] * count


def setup_call(ends, cond, mask, shown, arrived):
    return pl.pallas_call(
        setup_kernel,
        out_shape=(jax.ShapeDtypeStruct((BLOCKS, TILE, TILE), BF16), jax.ShapeDtypeStruct((BLOCKS, TILE), F32)),
        in_specs=vmem(3) + smem(1) + vmem(1),
        out_specs=tuple(vmem(2)),
        scratch_shapes=[
            pltpu.VMEM((NODES, TILE), F32),
            pltpu.VMEM((1, INNER), F32),
            pltpu.VMEM((64, TILE), F32),
            pltpu.VMEM((4 * CHUNKS, TILE), F32),
            pltpu.VMEM((4 * CHUNKS, TILE), F32),
            pltpu.VMEM((72, TILE), I32),
            pltpu.VMEM((BLOCKS * PITCH, TILE), F32),
            pltpu.VMEM((8, TILE, TILE), F32),
            pltpu.VMEM((BLOCKS * PITCH, TILE), F32),
            pltpu.SMEM((72, TILE), I32),
            pltpu.SemaphoreType.DMA,
        ],
        name="inverses",
    )(ends, cond, mask, shown, arrived)


def per_device(sizes, inflow, mask, ends, live, shown, radius, length):
    parts, depth_z, planes, reps = sizes
    mask = mask.reshape(BLOCKS, TILE)
    dma = pltpu.SemaphoreType.DMA
    cond, arrived = pl.pallas_call(
        functools.partial(head_kernel, parts),
        out_shape=(jax.ShapeDtypeStruct((1, SEGS), F32), jax.ShapeDtypeStruct((SHOWN, TILE), F32)),
        in_specs=vmem(3) + smem(1),
        out_specs=tuple(vmem(2)),
        scratch_shapes=[pltpu.VMEM((SHOWN, TILE), F32), pltpu.VMEM((SHOWN, TILE), F32), dma, dma],
        compiler_params=pltpu.CompilerParams(collective_id=0, has_side_effects=True),
        name="conductances",
    )(ends, radius.reshape(1, SEGS), length.reshape(1, SEGS), live)
    inverse, degree = setup_call(ends, cond, mask, shown, arrived)
    rows = 8 * BLOCKS
    back = 8 * SHOWN
    pressure, mean = pl.pallas_call(
        functools.partial(solve_kernel, sizes),
        out_shape=(jax.ShapeDtypeStruct((8, NODES), F32), jax.ShapeDtypeStruct((BLOCKS, TILE), F32)),
        in_specs=vmem(6) + smem(1),
        out_specs=tuple(vmem(2)),
        scratch_shapes=[
            pltpu.VMEM((2 * TILE, 2 * SEGS), BF16),
            pltpu.VMEM((8, 2 * SEGS), I32),
            pltpu.VMEM((8, SEGS), F32),
            pltpu.VMEM((3, rows, TILE), F32),
            pltpu.VMEM((2, rows, TILE), F32),
            pltpu.VMEM((rows, TILE), F32),
            pltpu.VMEM((rows, 2 * TILE), BF16),
            pltpu.VMEM((back, 2 * TILE), BF16),
            pltpu.VMEM((rows, 2 * TILE), F32),
            pltpu.VMEM((back, 2 * TILE), F32),
            pltpu.VMEM((3, back, TILE), F32),
            pltpu.VMEM((3, back, TILE), F32),
            pltpu.VMEM((2, back, TILE), F32),
            pltpu.VMEM((2, back, TILE), F32),
            pltpu.VMEM((planes, 8, TILE), F32),
            pltpu.VMEM((depth_z, 8, TILE), F32),
            pltpu.VMEM((reps, BLOCKS, TILE), F32),
            dma((3,)), dma((3,)), dma((2,)), dma((2,)),
            dma((planes,)), dma((planes,)), dma((depth_z,)), dma((depth_z,)), dma((reps,)), dma((reps,)),
        ],
        compiler_params=pltpu.CompilerParams(collective_id=1, has_side_effects=True),
        name="gradients",
    )(inflow, mask, ends, cond, degree, inverse, shown)
    return pressure, mean.reshape(NODES)


def solution(mesh):
    in_specs = (P("rep", "dom"), P("dom"), P(None, "dom"), P("dom"), P("dom"), P("dom"), P("dom"))
    out_specs = (P("rep", "dom"), P("dom"))
    parts, reps = mesh.shape["dom"], mesh.shape["rep"]
    depth_z = 8 if parts == 64 else parts // 4
    sizes = (parts, depth_z, parts // depth_z, reps)
    return jax.shard_map(
        functools.partial(per_device, sizes), mesh=mesh, in_specs=in_specs, out_specs=out_specs, check_vma=False
    )
```

```python
import functools

import jax
import jax.numpy as jnp
from jax import lax
from jax.experimental import pallas as pl
from jax.experimental.pallas import tpu as pltpu
from jax.sharding import PartitionSpec as P

MESH = pl.DeviceIdType.MESH
F32 = jnp.float32
BF16 = jnp.bfloat16
I32 = jnp.int32

TILE = 128
BLOCKS = 32
NODES = 4096
SCEN_ALL = 32
JUNC = 1024
INNER = 6144
SEGS = 7168
SHOWN = 8
CHUNKS = 48
PANEL = 32
PITCH = 40
FOUR = 4
UNROLL = 8
SCANS = 4
FILLS = 8

leak_rate = 0.05
inflow_weight = 20.0


def dot_nt(a, b):
    return lax.dot_general(a, b, (((1,), (1,)), ((), ())), preferred_element_type=F32)


def dot_nn(a, b):
    return lax.dot_general(a, b, (((1,), (0,)), ((), ())), preferred_element_type=F32)


def dot_tn(a, b):
    return lax.dot_general(a, b, (((0,), (0,)), ((), ())), preferred_element_type=F32)


def parts2(x):
    hi = x.astype(BF16).astype(F32)
    return hi, x - hi


def parts3(x):
    hi = x.astype(BF16).astype(F32)
    rest = x - hi
    mid = rest.astype(BF16).astype(F32)
    return hi, mid, rest - mid


def one_hot_rows(row, count):
    ids = lax.broadcasted_iota(I32, (count, row.shape[1]), 0)
    return ids == row


def one_hot_lanes(row, count):
    ids = lax.broadcasted_iota(I32, (count, row.shape[1]), 0).astype(F32).astype(BF16)
    return jnp.where(ids == row.astype(F32).astype(BF16), jnp.ones((), BF16), jnp.zeros((), BF16))


def spread(mask, value):
    return jnp.where(mask, value, 0.0).astype(BF16)


def conductance(radius, seg_length):
    diameter = 2.0 * radius
    power = jnp.exp(0.645 * jnp.log(diameter))
    viscous = 220.0 * jnp.exp(-1.3 * diameter) + 3.2 - 2.44 * jnp.exp(-0.06 * power)
    scaled = diameter * 0.125
    scaled = scaled * scaled
    return scaled * scaled * (50.0 / seg_length) / viscous


def head_kernel(parts, ends, radius, length, live, cond_out, arrived, sent, landed, send_sem, recv_sem):
    place = lax.axis_index("dom")
    upper = lax.rem(place + 1, parts)
    lower = lax.rem(place + parts - 1, parts)
    barrier = pltpu.get_barrier_semaphore()
    for other in (upper, lower):
        pl.semaphore_signal(barrier, inc=1, device_id={"dom": other}, device_id_type=MESH)
    cond = conductance(radius[...], length[...])
    position = lax.broadcasted_iota(I32, (1, SEGS), 1)
    limit = jnp.where(position < INNER, jnp.full((1, SEGS), live[0], I32), jnp.full((1, SEGS), (parts - 1 - place) * SEGS, I32))
    cond = jnp.where(position < limit, cond, 0.0)
    high, low = parts2(cond)
    cond = high + low.astype(BF16).astype(F32)
    cond_out[...] = cond
    slot = ends[1:2, INNER:]
    junc = cond[:, INNER:]
    owner = one_hot_rows(slot >> 7, SHOWN)
    stack = jnp.concatenate([jnp.where(owner, part, 0.0) for part in parts2(junc)], axis=0).astype(BF16)
    lanes = spread(one_hot_rows(slot & 127, TILE), 1.0)
    sums = dot_nt(stack, lanes)
    sent[...] = sums[0:8] + sums[8:16]
    pl.semaphore_wait(barrier, 2)
    copy = pltpu.make_async_remote_copy(
        src_ref=sent, dst_ref=landed, send_sem=send_sem, recv_sem=recv_sem, device_id={"dom": upper}, device_id_type=MESH
    )
    copy.start()
    copy.wait()
    arrived[...] = landed[...]


def setup_kernel(
    ends, cond, mask, shown, arrived, inverse, degree_out, table, rank, degree, near, sums, counts, old_rows, turned_rows, small, counts_smem, sem
):
    degree[...] = jnp.zeros_like(degree)
    near[...] = jnp.zeros_like(near)
    width = 256
    before = lax.broadcasted_iota(I32, (width, width), 0) < lax.broadcasted_iota(I32, (width, width), 1)
    before = jnp.where(before, 1.0, 0.0).astype(BF16)

    def add_degree(nodes, values):
        stacks, lanes = [], []
        for node, value in zip(nodes, values):
            owner = one_hot_rows(node >> 7, BLOCKS)
            stacks.append(jnp.concatenate([jnp.where(owner, part, 0.0) for part in parts2(value)], axis=0).astype(BF16))
            lanes.append(one_hot_lanes(node & 127, TILE))
        degree[...] += dot_nt(jnp.concatenate(stacks, axis=1), jnp.concatenate(lanes, axis=1))

    def scan(step, carry):
        nodes, values, stacks, lanes = [], [], [], []
        for i in range(SCANS):
            cols = pl.ds(pl.multiple_of((SCANS * step + i) * width, width), width)
            head = ends[0:1, cols]
            tail = ends[1:2, cols]
            value = cond[:, cols]
            nodes += [head, tail]
            values += [value, value]
            bucket = jnp.where((head >> 7) == (tail >> 7), head >> 7, -1)
            member = one_hot_rows(bucket, BLOCKS)
            ahead = dot_nn(spread(member, 1.0), before)
            place = jnp.sum(jnp.where(member, ahead + carry, 0.0), axis=0, keepdims=True)
            rank[:, cols] = place
            carry = carry + jnp.sum(jnp.where(member, 1.0, 0.0), axis=1, keepdims=True)
            order = place.astype(I32)
            at_block = one_hot_rows(jnp.where(order < TILE, bucket, -1), BLOCKS)
            fields = ((head & 127).astype(F32), (tail & 127).astype(F32)) + parts2(value)
            stacks.append(jnp.concatenate([spread(at_block, field) for field in fields], axis=0))
            lanes.append(one_hot_lanes(order & 127, TILE))
        add_degree(nodes, values)
        near[...] += dot_nt(jnp.concatenate(stacks, axis=1), jnp.concatenate(lanes, axis=1))
        return carry

    total = lax.fori_loop(0, INNER // width // SCANS, scan, jnp.zeros((BLOCKS, 1), F32))
    add_degree([ends[0:1, INNER:]], [cond[:, INNER:]])
    deg = degree[0:32, :] + degree[32:64, :]
    block_id = lax.broadcasted_iota(I32, (BLOCKS, TILE), 0)
    for j in range(SHOWN):
        deg = deg + jnp.where(block_id == shown[j], arrived[j : j + 1, :], 0.0)
    deg = deg + (leak_rate + inflow_weight * mask[...].astype(F32))
    degree_out[...] = deg

    chunks = jnp.maximum(jnp.floor((jnp.broadcast_to(total, (BLOCKS, TILE)) - 1.0) * (1.0 / 128.0)), 0.0)
    below = lax.broadcasted_iota(I32, (BLOCKS, BLOCKS), 1) < lax.broadcasted_iota(I32, (BLOCKS, BLOCKS), 0)
    start = dot_nn(jnp.where(below, 1.0, 0.0).astype(BF16), chunks.astype(BF16))
    counts[0:32, :] = start.astype(I32)
    counts[32:64, :] = chunks.astype(I32)
    counts[64:72, :] = jnp.broadcast_to(jnp.max(chunks, axis=0, keepdims=True), (8, TILE)).astype(I32)
    to_scalar = pltpu.make_async_copy(counts, counts_smem, sem)
    to_scalar.start()
    start_column = start[:, 0:1]
    wide = 1024

    def compact(step, carry):
        cols = pl.ds(pl.multiple_of(step * wide, wide), wide)
        head = ends[0:1, cols]
        tail = ends[1:2, cols]
        inside = (head >> 7) == (tail >> 7)
        bucket = jnp.where(inside, head >> 7, -1)
        base = jnp.sum(jnp.where(one_hot_rows(bucket, BLOCKS), start_column, 0.0), axis=0, keepdims=True)
        order = rank[:, cols].astype(I32)
        chunk = jnp.where(inside & (order >= TILE), base.astype(I32) + (order >> 7) - 1, -1)
        at_chunk = one_hot_rows(chunk, CHUNKS)
        values = ((head & 127).astype(F32), (tail & 127).astype(F32)) + parts2(cond[:, cols])
        stack = jnp.concatenate([spread(at_chunk, value) for value in values], axis=0)
        lanes = one_hot_lanes(order & 127, TILE)
        sums[...] += dot_nt(stack, lanes)
        return carry

    row_id = lax.broadcasted_iota(I32, (TILE, TILE), 0)
    lane_id = lax.broadcasted_iota(I32, (TILE, TILE), 1)

    def chunk_of(source, row, pitch):
        head = source[pl.ds(row, 1), :].astype(I32)
        tail = source[pl.ds(row + pitch, 1), :].astype(I32)
        at_head = row_id == head
        at_tail = row_id == tail
        left = jnp.concatenate([spread(at_head, 1.0), spread(at_tail, 1.0)], axis=1)
        right = []
        for k in range(2):
            value = source[pl.ds(row + (2 + k) * pitch, 1), :]
            right.append(jnp.concatenate([spread(at_tail, value), spread(at_head, value)], axis=1))
        both = dot_nt(left, jnp.concatenate(right, axis=0))
        return both[:, 0:TILE] + both[:, TILE:]

    def fill(step, carry):
        filled = []
        for i in range(FILLS):
            block = step * FILLS + i
            off = chunk_of(near, block, BLOCKS)
            filled.append(jnp.where(row_id == lane_id, degree_out[pl.ds(block, 1), :], -off))
        for i in range(FILLS):
            table[pl.ds(pl.multiple_of((step * FILLS + i) * TILE, TILE), TILE), :] = filled[i]
        return carry

    lax.fori_loop(0, BLOCKS // FILLS, fill, 0)
    to_scalar.wait()

    def refill(block, carry):
        rows = pl.ds(pl.multiple_of(block * TILE, TILE), TILE)

        def more(index, inner):
            table[rows, :] = table[rows, :] - chunk_of(sums, counts_smem[block, 0] + index, CHUNKS)
            return inner

        lax.fori_loop(0, counts_smem[block + BLOCKS, 0], more, 0)
        return carry

    @pl.when(counts_smem[64, 0] > 0)
    def _():
        sums[...] = jnp.zeros_like(sums)
        lax.fori_loop(0, INNER // wide, compact, 0)
        lax.fori_loop(0, BLOCKS, refill, 0)

    panel_lane = lax.broadcasted_iota(I32, (PANEL, TILE), 1)
    panel_row = lax.broadcasted_iota(I32, (PANEL, TILE), 0)
    own_block = (row_id // PANEL) == (lane_id // PANEL)
    lane_block = panel_lane & (PANEL - 1)
    lane_group = panel_lane // PANEL

    def replicated(x, group):
        return jnp.take_along_axis(x, lane_block + group * PANEL, axis=1, mode="promise_in_bounds")

    def panel(index, carry):
        base = pl.multiple_of(index * PANEL, PANEL)
        for b in range(BLOCKS):
            old_rows[b * PITCH : b * PITCH + PANEL, :] = table[pl.ds(b * TILE + base, PANEL), :]
        for i in range(8):
            lines = [old_rows[pl.ds(8 * h + i, BLOCKS, stride=PITCH), :] for h in range(4)]
            turned_rows[i] = jnp.concatenate(lines, axis=0).T
        state = [turned_rows[i, pl.ds(base, PANEL), :] for i in range(8)]
        for first in range(0, PANEL, 4):
            coming = [replicated(state[(first + d) % 8], (first + d) // 8) for d in range(4)]
            for d in range(4):
                t = first + d
                at_row = panel_row == t
                now = coming[d]
                pivot = 1.0 / now[t : t + 1, :]
                new = jnp.where(at_row, pivot, now * pivot)
                for e in range(d + 1, 4):
                    x = coming[e]
                    coming[e] = jnp.where(at_row, 0.0, x) - x[t : t + 1, :] * new
                for i in range(8):
                    x = state[i]
                    rest = jnp.where(at_row, 0.0, x) - x[t : t + 1, :] * new
                    state[i] = jnp.where(lane_group == t // 8, new, rest) if i == t % 8 else rest
        for i in range(8):
            back = jnp.concatenate([state[i]] * 4, axis=0).T
            for h in range(4):
                small[pl.ds(8 * h + i, BLOCKS, stride=PITCH), :] = back[PANEL * h : PANEL * h + PANEL, :]
        unit = jnp.where(panel_lane == panel_row + base, 1.0, 0.0)
        in_panel = (panel_lane >= base) & (panel_lane < base + PANEL)
        keep = ((lane_id >= base) & (lane_id < base + PANEL)) | ((row_id >= base) & (row_id < base + PANEL))
        for g in range(BLOCKS // FOUR):
            starts = [PITCH * (g * FOUR + i) for i in range(FOUR)]
            diagonal = jnp.where(own_block, jnp.concatenate([small[at : at + PANEL, :] for at in starts], axis=0), 0.0)
            members = [jnp.where(in_panel, unit, old_rows[at : at + PANEL, :]) for at in starts]
            stack = jnp.concatenate(members, axis=0)
            dh, dm = [part.astype(BF16) for part in parts2(diagonal)]
            sh, sm = [part.astype(BF16) for part in parts2(stack)]
            def crossed(high, low):
                return jnp.concatenate([jnp.concatenate([high, low], axis=1), jnp.concatenate([low, high], axis=1)], axis=0)

            fresh = dot_nn(jnp.concatenate([dh, dm], axis=1), crossed(sh, sm))
            fresh = fresh[:, 0:TILE] + fresh[:, TILE:]
            turned = stack.T
            turned = jnp.where(row_id < base + PANEL, -turned, turned)
            parts = [part.astype(BF16) for part in parts2(turned)]
            fh, fm = [part.astype(BF16) for part in parts2(fresh)]
            none = jnp.zeros((TILE, TILE), BF16)
            left = [jnp.concatenate([jnp.where((lane_id // PANEL) == i, part, none) for part in parts], axis=1) for i in range(FOUR)]
            update = dot_nn(jnp.concatenate(left, axis=0), crossed(fh, fm))
            update = update[:, 0:TILE] + update[:, TILE:]
            for i in range(FOUR):
                rows = slice((g * FOUR + i) * TILE, (g * FOUR + i + 1) * TILE)
                table[rows, :] = jnp.where(keep, 0.0, table[rows, :]) - update[TILE * i : TILE * i + TILE, :]
        return carry

    lax.fori_loop(0, TILE // PANEL, panel, 0)

    for block in range(BLOCKS):
        inverse[block] = table[block * TILE : (block + 1) * TILE, :].astype(BF16)


def solve_kernel(
    sizes, inflow, mask, ends, cond, degree, inverse, shown, pressure, mean,
    table, owner8, cond8, basis, images, residual, pair, upper_pair, out, back_out, fwd_out, fwd_in, back_src, back_in,
    one_buf, two_buf, rep_buf,
    fwd_send, fwd_recv, back_send, back_recv, one_send, one_recv, two_send, two_recv, rep_send, rep_recv,
):
    parts, depth_z, planes, reps = sizes
    place = lax.axis_index("dom")
    mine = lax.axis_index("rep")
    upper = lax.rem(place + 1, parts)
    lower = lax.rem(place + parts - 1, parts)
    core = lax.rem(place, 2)
    column = lax.rem(place // 2, depth_z)
    line = place // (2 * depth_z)
    seat = line * 2 + core

    def plane_place(other):
        return ((other // 2) * depth_z + column) * 2 + lax.rem(other, 2)

    def column_place(other):
        return (line * depth_z + other) * 2 + core

    barrier = pltpu.get_barrier_semaphore()
    partners = [{"dom": upper}, {"dom": lower}]
    partners += [{"dom": plane_place(lax.rem(seat + o, planes))} for o in range(1, planes)]
    partners += [{"dom": column_place(lax.rem(column + o, depth_z))} for o in range(1, depth_z)]
    partners += [{"rep": lax.rem(mine + o, reps)} for o in range(1, reps)]
    for partner in partners:
        pl.semaphore_signal(barrier, inc=1, device_id=partner, device_id_type=MESH)

    wide = 256

    def make(step, carry):
        cols = pl.ds(pl.multiple_of(step * wide, wide), wide)
        value = jnp.broadcast_to(cond[:, cols], (8, wide))
        cond8[:, cols] = value
        for side in range(2):
            node = ends[side : side + 1, cols]
            into = pl.ds(pl.multiple_of(side * SEGS + step * wide, wide), wide)
            table[:, into] = one_hot_lanes(node & 255, 256)
            owner8[:, into] = jnp.broadcast_to(node >> 8, (8, wide))
        return carry

    lax.fori_loop(0, SEGS // wide, make, 0, unroll=4)

    def split_into(target, tile, pairs):
        rows = 8 * pairs
        for q in range(0, pairs, 2):
            highs, lows = [], []
            for half in range(2):
                parts = [parts2(tile(2 * (q + i) + half)) for i in range(2)]
                highs.append(jnp.concatenate([part[0] for part in parts], axis=0))
                lows.append(jnp.concatenate([part[1] for part in parts], axis=0))
            target[8 * q : 8 * q + 16, :] = jnp.concatenate(highs, axis=1).astype(BF16)
            target[rows + 8 * q : rows + 8 * q + 16, :] = jnp.concatenate(lows, axis=1).astype(BF16)

    def gather(source, cols, pairs, both):
        full = dot_nn(source[...] if both else source[0 : 8 * pairs, :], table[:, cols])
        owner = owner8[:, cols]
        result = jnp.zeros((8, wide), F32)
        for q in range(pairs):
            value = full[8 * q : 8 * q + 8, :]
            if both:
                value = value + full[8 * (q + pairs) : 8 * (q + pairs) + 8, :]
            result = jnp.where(owner == q, value, result)
        return result

    def scatter(values, cols, pairs):
        left, right = [], []
        for value, at in zip(values, cols):
            owner = owner8[:, at]
            left.append(jnp.concatenate([jnp.where(owner == q, part, 0.0) for part in parts2(value) for q in range(pairs)], axis=0).astype(BF16))
            right.append(table[:, at])
        return dot_nt(jnp.concatenate(left, axis=1), jnp.concatenate(right, axis=1))

    def tile_of(source, b, pairs):
        rows, lanes = 8 * (b // 2), slice(TILE * (b % 2), TILE * (b % 2) + TILE)
        return source[rows : rows + 8, lanes] + source[8 * pairs + rows : 8 * pairs + rows + 8, lanes]

    pairs_all = BLOCKS // 2
    pairs_shown = SHOWN // 2

    def head_cols(step):
        return pl.ds(pl.multiple_of(step * wide, wide), wide)

    def tail_cols(step):
        return pl.ds(pl.multiple_of(SEGS + step * wide, wide), wide)

    def precondition(k):
        for b in range(BLOCKS):
            field = residual[8 * b : 8 * b + 8, :].astype(BF16)
            value = dot_nn(field, inverse[b])
            if k == 1:
                value = value.astype(BF16).astype(F32)
            basis[k, 8 * b : 8 * b + 8, :] = value

    for b in range(BLOCKS):
        weight = inflow_weight * mask[b : b + 1, :].astype(F32)
        residual[8 * b : 8 * b + 8, :] = weight * inflow[:, TILE * b : TILE * b + TILE]
    precondition(0)

    lane = lax.broadcasted_iota(I32, (8, TILE), 1)
    moments = jnp.zeros((8, TILE), F32)

    def total_of(k, other):
        accs = [jnp.zeros((8, TILE), F32)] * 4
        for b in range(BLOCKS):
            accs[b % 4] = accs[b % 4] + basis[k, 8 * b : 8 * b + 8, :] * other(b)
        return jnp.sum((accs[0] + accs[1]) + (accs[2] + accs[3]), axis=1, keepdims=True)

    def right_side(b):
        weight = inflow_weight * mask[b : b + 1, :].astype(F32)
        return weight * inflow[:, TILE * b : TILE * b + TILE]

    junc_first = INNER // wide
    junc_steps = JUNC // wide
    for k in range(3):
        split_into(pair, lambda b: basis[k, 8 * b : 8 * b + 8, :], pairs_all)
        for j in range(SHOWN):
            wanted = jnp.full((8, TILE), shown[j], I32)
            tile = jnp.zeros((8, TILE), F32)
            for b in range(BLOCKS):
                tile = jnp.where(wanted == b, basis[k, 8 * b : 8 * b + 8, :], tile)
            fwd_out[k, 8 * j : 8 * j + 8, :] = tile
        if k == 0:
            pl.semaphore_wait(barrier, len(partners))
        forward = pltpu.make_async_remote_copy(
            src_ref=fwd_out.at[k], dst_ref=fwd_in.at[k], send_sem=fwd_send.at[k], recv_sem=fwd_recv.at[k],
            device_id={"dom": lower}, device_id_type=MESH,
        )
        forward.start()
        moments = jnp.where(lane == k, total_of(k, right_side), moments)
        if k < 2:
            hcols = [head_cols(junc_first + step) for step in range(junc_steps)]
            tcols = [tail_cols(junc_first + step) for step in range(junc_steps)]
            back_out[...] = scatter([cond8[:, at] * gather(pair, at, pairs_all, k == 0) for at in hcols], tcols, pairs_shown)
            for j in range(SHOWN):
                back_src[k, 8 * j : 8 * j + 8, :] = tile_of(back_out, j, pairs_shown)
            backward = pltpu.make_async_remote_copy(
                src_ref=back_src.at[k], dst_ref=back_in.at[k], send_sem=back_send.at[k], recv_sem=back_recv.at[k],
                device_id={"dom": upper}, device_id_type=MESH,
            )
            backward.start()
            out[...] = jnp.zeros_like(out)

            def inner(step, carry):
                values, cols = [], []
                for i in range(UNROLL):
                    h, t = head_cols(UNROLL * step + i), tail_cols(UNROLL * step + i)
                    weight = cond8[:, h]
                    values += [weight * gather(pair, t, pairs_all, k == 0), weight * gather(pair, h, pairs_all, k == 0)]
                    cols += [h, t]
                out[...] += scatter(values, cols, pairs_all)
                return carry

            lax.fori_loop(0, INNER // wide // UNROLL, inner, 0)
            forward.wait()
            split_into(upper_pair, lambda j: fwd_in[k, 8 * j : 8 * j + 8, :], pairs_shown)
            out[...] += scatter([cond8[:, h] * gather(upper_pair, t, pairs_shown, k == 0) for h, t in zip(hcols, tcols)], hcols, pairs_all)
            backward.wait()
            for b in range(BLOCKS):
                acc = tile_of(out, b, pairs_all)
                for j in range(SHOWN):
                    acc = acc + jnp.where(jnp.full((8, TILE), shown[j], I32) == b, back_in[k, 8 * j : 8 * j + 8, :], 0.0)
                image = degree[b : b + 1, :] * basis[k, 8 * b : 8 * b + 8, :] - acc
                images[k, 8 * b : 8 * b + 8, :] = image
                residual[8 * b : 8 * b + 8, :] = residual[8 * b : 8 * b + 8, :] - image
            precondition(k + 1)
            moments = jnp.where(lane == 3 + k, total_of(k, lambda b: images[k, 8 * b : 8 * b + 8, :]), moments)
            moments = jnp.where(lane == 6 + k, total_of(k + 1, lambda b: images[k, 8 * b : 8 * b + 8, :]), moments)
        else:
            def quadratic(step, carry):
                for i in range(UNROLL):
                    h, t = head_cols(UNROLL * step + i), tail_cols(UNROLL * step + i)
                    carry = carry + cond8[:, h] * gather(pair, h, pairs_all, k == 0) * gather(pair, t, pairs_all, k == 0)
                return carry

            crossed = lax.fori_loop(0, INNER // wide // UNROLL, quadratic, jnp.zeros((8, wide), F32))
            ahead = [cond8[:, head_cols(junc_first + step)] * gather(pair, head_cols(junc_first + step), pairs_all, k == 0) for step in range(junc_steps)]
            forward.wait()
            split_into(upper_pair, lambda j: fwd_in[k, 8 * j : 8 * j + 8, :], pairs_shown)
            for step in range(junc_steps):
                crossed = crossed + ahead[step] * gather(upper_pair, tail_cols(junc_first + step), pairs_shown, k == 0)
            square = total_of(2, lambda b: degree[b : b + 1, :] * basis[2, 8 * b : 8 * b + 8, :])
            square = square - 2.0 * jnp.sum(crossed, axis=1, keepdims=True)
            moments = jnp.where(lane == 5, square, moments)
            moments = jnp.where(lane == 8, total_of(2, lambda b: images[0, 8 * b : 8 * b + 8, :]), moments)

    def exchange(buffer, send, recv, index, count, target):
        copies = []
        for o in range(1, count):
            other = lax.rem(index + o, count)
            copies.append(pltpu.make_async_remote_copy(
                src_ref=buffer.at[index], dst_ref=buffer.at[index], send_sem=send.at[o], recv_sem=recv.at[o],
                device_id=target(other), device_id_type=MESH,
            ))
        for copy in copies:
            copy.start()
        for copy in copies:
            copy.wait()
        acc = buffer[0]
        for o in range(1, count):
            acc = acc + buffer[o]
        return acc

    one_buf[seat] = moments
    moments = exchange(one_buf, one_send, one_recv, seat, planes, lambda other: {"dom": plane_place(other)})
    two_buf[column] = moments
    moments = exchange(two_buf, two_send, two_recv, column, depth_z, lambda other: {"dom": column_place(other)})

    def entry(index):
        return jnp.broadcast_to(moments[:, index : index + 1], (8, TILE))

    b0, b1, b2, g00, g11, g22, g01, g12, g02 = [entry(i) for i in range(9)]

    def safe_inverse(value, scale):
        good = value > 1e-6 * scale
        return jnp.where(good, 1.0 / jnp.where(good, value, 1.0), 0.0)

    i0 = safe_inverse(g00, g00)
    l10 = g01 * i0
    l20 = g02 * i0
    i1 = safe_inverse(g11 - l10 * g01, g11)
    c12 = g12 - l20 * g01
    l21 = c12 * i1
    i2 = safe_inverse(g22 - l20 * g02 - l21 * c12, g22)
    w1 = b1 - l10 * b0
    w2 = b2 - l20 * b0 - l21 * w1
    y2 = w2 * i2
    y1 = w1 * i1 - l21 * y2
    y0 = b0 * i0 - l10 * y1 - l20 * y2
    for b in range(BLOCKS):
        rows = slice(8 * b, 8 * b + 8)
        value = y0 * basis[0, rows, :] + y1 * basis[1, rows, :] + y2 * basis[2, rows, :]
        pressure[:, TILE * b : TILE * b + TILE] = value
        rep_buf[mine, b : b + 1, :] = jnp.sum(value, axis=0, keepdims=True)
    total = exchange(rep_buf, rep_send, rep_recv, mine, reps, lambda other: {"rep": other})
    mean[...] = total * (1.0 / SCEN_ALL)


def vmem(count):
    return [pl.BlockSpec(memory_space=pltpu.VMEM)] * count


def smem(count):
    return [pl.BlockSpec(memory_space=pltpu.SMEM)] * count


def setup_call(ends, cond, mask, shown, arrived):
    return pl.pallas_call(
        setup_kernel,
        out_shape=(jax.ShapeDtypeStruct((BLOCKS, TILE, TILE), BF16), jax.ShapeDtypeStruct((BLOCKS, TILE), F32)),
        in_specs=vmem(3) + smem(1) + vmem(1),
        out_specs=tuple(vmem(2)),
        scratch_shapes=[
            pltpu.VMEM((NODES, TILE), F32),
            pltpu.VMEM((1, INNER), F32),
            pltpu.VMEM((64, TILE), F32),
            pltpu.VMEM((4 * BLOCKS, TILE), F32),
            pltpu.VMEM((4 * CHUNKS, TILE), F32),
            pltpu.VMEM((72, TILE), I32),
            pltpu.VMEM((BLOCKS * PITCH, TILE), F32),
            pltpu.VMEM((8, TILE, TILE), F32),
            pltpu.VMEM((BLOCKS * PITCH, TILE), F32),
            pltpu.SMEM((72, TILE), I32),
            pltpu.SemaphoreType.DMA,
        ],
        name="inverses",
    )(ends, cond, mask, shown, arrived)


def per_device(sizes, inflow, mask, ends, live, shown, radius, length):
    parts, depth_z, planes, reps = sizes
    mask = mask.reshape(BLOCKS, TILE)
    dma = pltpu.SemaphoreType.DMA
    cond, arrived = pl.pallas_call(
        functools.partial(head_kernel, parts),
        out_shape=(jax.ShapeDtypeStruct((1, SEGS), F32), jax.ShapeDtypeStruct((SHOWN, TILE), F32)),
        in_specs=vmem(3) + smem(1),
        out_specs=tuple(vmem(2)),
        scratch_shapes=[pltpu.VMEM((SHOWN, TILE), F32), pltpu.VMEM((SHOWN, TILE), F32), dma, dma],
        compiler_params=pltpu.CompilerParams(collective_id=0, has_side_effects=True),
        name="conductances",
    )(ends, radius.reshape(1, SEGS), length.reshape(1, SEGS), live)
    inverse, degree = setup_call(ends, cond, mask, shown, arrived)
    rows = 8 * BLOCKS
    back = 8 * SHOWN
    pressure, mean = pl.pallas_call(
        functools.partial(solve_kernel, sizes),
        out_shape=(jax.ShapeDtypeStruct((8, NODES), F32), jax.ShapeDtypeStruct((BLOCKS, TILE), F32)),
        in_specs=vmem(6) + smem(1),
        out_specs=tuple(vmem(2)),
        scratch_shapes=[
            pltpu.VMEM((2 * TILE, 2 * SEGS), BF16),
            pltpu.VMEM((8, 2 * SEGS), I32),
            pltpu.VMEM((8, SEGS), F32),
            pltpu.VMEM((3, rows, TILE), F32),
            pltpu.VMEM((2, rows, TILE), F32),
            pltpu.VMEM((rows, TILE), F32),
            pltpu.VMEM((rows, 2 * TILE), BF16),
            pltpu.VMEM((back, 2 * TILE), BF16),
            pltpu.VMEM((rows, 2 * TILE), F32),
            pltpu.VMEM((back, 2 * TILE), F32),
            pltpu.VMEM((3, back, TILE), F32),
            pltpu.VMEM((3, back, TILE), F32),
            pltpu.VMEM((2, back, TILE), F32),
            pltpu.VMEM((2, back, TILE), F32),
            pltpu.VMEM((planes, 8, TILE), F32),
            pltpu.VMEM((depth_z, 8, TILE), F32),
            pltpu.VMEM((reps, BLOCKS, TILE), F32),
            dma((3,)), dma((3,)), dma((2,)), dma((2,)),
            dma((planes,)), dma((planes,)), dma((depth_z,)), dma((depth_z,)), dma((reps,)), dma((reps,)),
        ],
        compiler_params=pltpu.CompilerParams(collective_id=1, has_side_effects=True),
        name="gradients",
    )(inflow, mask, ends, cond, degree, inverse, shown)
    return pressure, mean.reshape(NODES)


def solution(mesh):
    in_specs = (P("rep", "dom"), P("dom"), P(None, "dom"), P("dom"), P("dom"), P("dom"), P("dom"))
    out_specs = (P("rep", "dom"), P("dom"))
    parts, reps = mesh.shape["dom"], mesh.shape["rep"]
    depth_z = 8 if parts == 64 else parts // 4
    sizes = (parts, depth_z, parts // depth_z, reps)
    return jax.shard_map(
        functools.partial(per_device, sizes), mesh=mesh, in_specs=in_specs, out_specs=out_specs, check_vma=False
    )
```

```python
import functools

import jax
import jax.numpy as jnp
from jax import lax
from jax.experimental import pallas as pl
from jax.experimental.pallas import tpu as pltpu
from jax.sharding import PartitionSpec as P

MESH = pl.DeviceIdType.MESH
F32 = jnp.float32
BF16 = jnp.bfloat16
I32 = jnp.int32

TILE = 128
BLOCKS = 32
NODES = 4096
SCEN_ALL = 32
JUNC = 1024
INNER = 6144
SEGS = 7168
SHOWN = 8
CHUNKS = 48
PANEL = 32
PITCH = 40
FOUR = 4
UNROLL = 12
SCANS = 4
FILLS = 8

leak_rate = 0.05
inflow_weight = 20.0


def dot_nt(a, b):
    return lax.dot_general(a, b, (((1,), (1,)), ((), ())), preferred_element_type=F32)


def dot_nn(a, b):
    return lax.dot_general(a, b, (((1,), (0,)), ((), ())), preferred_element_type=F32)


def dot_tn(a, b):
    return lax.dot_general(a, b, (((0,), (0,)), ((), ())), preferred_element_type=F32)


def parts2(x):
    hi = x.astype(BF16).astype(F32)
    return hi, x - hi


def parts3(x):
    hi = x.astype(BF16).astype(F32)
    rest = x - hi
    mid = rest.astype(BF16).astype(F32)
    return hi, mid, rest - mid


def one_hot_rows(row, count):
    ids = lax.broadcasted_iota(I32, (count, row.shape[1]), 0)
    return ids == row


def one_hot_lanes(row, count):
    ids = lax.broadcasted_iota(I32, (count, row.shape[1]), 0).astype(F32).astype(BF16)
    return jnp.where(ids == row.astype(F32).astype(BF16), jnp.ones((), BF16), jnp.zeros((), BF16))


def spread(mask, value):
    return jnp.where(mask, value, 0.0).astype(BF16)


def conductance(radius, seg_length):
    diameter = 2.0 * radius
    power = jnp.exp(0.645 * jnp.log(diameter))
    viscous = 220.0 * jnp.exp(-1.3 * diameter) + 3.2 - 2.44 * jnp.exp(-0.06 * power)
    scaled = diameter * 0.125
    scaled = scaled * scaled
    return scaled * scaled * (50.0 / seg_length) / viscous


def head_kernel(parts, ends, radius, length, live, cond_out, arrived, sent, landed, send_sem, recv_sem):
    place = lax.axis_index("dom")
    upper = lax.rem(place + 1, parts)
    lower = lax.rem(place + parts - 1, parts)
    barrier = pltpu.get_barrier_semaphore()
    for other in (upper, lower):
        pl.semaphore_signal(barrier, inc=1, device_id={"dom": other}, device_id_type=MESH)
    cond = conductance(radius[...], length[...])
    position = lax.broadcasted_iota(I32, (1, SEGS), 1)
    limit = jnp.where(position < INNER, jnp.full((1, SEGS), live[0], I32), jnp.full((1, SEGS), (parts - 1 - place) * SEGS, I32))
    cond = jnp.where(position < limit, cond, 0.0)
    high, low = parts2(cond)
    cond = high + low.astype(BF16).astype(F32)
    cond_out[...] = cond
    slot = ends[1:2, INNER:]
    junc = cond[:, INNER:]
    owner = one_hot_rows(slot >> 7, SHOWN)
    stack = jnp.concatenate([jnp.where(owner, part, 0.0) for part in parts2(junc)], axis=0).astype(BF16)
    lanes = spread(one_hot_rows(slot & 127, TILE), 1.0)
    sums = dot_nt(stack, lanes)
    sent[...] = sums[0:8] + sums[8:16]
    pl.semaphore_wait(barrier, 2)
    copy = pltpu.make_async_remote_copy(
        src_ref=sent, dst_ref=landed, send_sem=send_sem, recv_sem=recv_sem, device_id={"dom": upper}, device_id_type=MESH
    )
    copy.start()
    copy.wait()
    arrived[...] = landed[...]


def setup_kernel(
    ends, cond, mask, shown, arrived, inverse, degree_out, table, rank, degree, near, sums, counts, old_rows, turned_rows, small, counts_smem, sem
):
    degree[...] = jnp.zeros_like(degree)
    near[...] = jnp.zeros_like(near)
    width = 256
    before = lax.broadcasted_iota(I32, (width, width), 0) < lax.broadcasted_iota(I32, (width, width), 1)
    before = jnp.where(before, 1.0, 0.0).astype(BF16)

    def add_degree(nodes, values):
        stacks, lanes = [], []
        for node, value in zip(nodes, values):
            owner = one_hot_rows(node >> 7, BLOCKS)
            stacks.append(jnp.concatenate([jnp.where(owner, part, 0.0) for part in parts2(value)], axis=0).astype(BF16))
            lanes.append(one_hot_lanes(node & 127, TILE))
        degree[...] += dot_nt(jnp.concatenate(stacks, axis=1), jnp.concatenate(lanes, axis=1))

    def scan(step, carry):
        nodes, values, stacks, lanes = [], [], [], []
        for i in range(SCANS):
            cols = pl.ds(pl.multiple_of((SCANS * step + i) * width, width), width)
            head = ends[0:1, cols]
            tail = ends[1:2, cols]
            value = cond[:, cols]
            nodes += [head, tail]
            values += [value, value]
            bucket = jnp.where((head >> 7) == (tail >> 7), head >> 7, -1)
            member = one_hot_rows(bucket, BLOCKS)
            ahead = dot_nn(spread(member, 1.0), before)
            place = jnp.sum(jnp.where(member, ahead + carry, 0.0), axis=0, keepdims=True)
            rank[:, cols] = place
            carry = carry + jnp.sum(jnp.where(member, 1.0, 0.0), axis=1, keepdims=True)
            order = place.astype(I32)
            at_block = one_hot_rows(jnp.where(order < TILE, bucket, -1), BLOCKS)
            fields = ((head & 127).astype(F32), (tail & 127).astype(F32)) + parts2(value)
            stacks.append(jnp.concatenate([spread(at_block, field) for field in fields], axis=0))
            lanes.append(one_hot_lanes(order & 127, TILE))
        add_degree(nodes, values)
        near[...] += dot_nt(jnp.concatenate(stacks, axis=1), jnp.concatenate(lanes, axis=1))
        return carry

    total = lax.fori_loop(0, INNER // width // SCANS, scan, jnp.zeros((BLOCKS, 1), F32))
    add_degree([ends[0:1, INNER:]], [cond[:, INNER:]])
    deg = degree[0:32, :] + degree[32:64, :]
    block_id = lax.broadcasted_iota(I32, (BLOCKS, TILE), 0)
    for j in range(SHOWN):
        deg = deg + jnp.where(block_id == shown[j], arrived[j : j + 1, :], 0.0)
    deg = deg + (leak_rate + inflow_weight * mask[...].astype(F32))
    degree_out[...] = deg

    chunks = jnp.maximum(jnp.floor((jnp.broadcast_to(total, (BLOCKS, TILE)) - 1.0) * (1.0 / 128.0)), 0.0)
    below = lax.broadcasted_iota(I32, (BLOCKS, BLOCKS), 1) < lax.broadcasted_iota(I32, (BLOCKS, BLOCKS), 0)
    start = dot_nn(jnp.where(below, 1.0, 0.0).astype(BF16), chunks.astype(BF16))
    counts[0:32, :] = start.astype(I32)
    counts[32:64, :] = chunks.astype(I32)
    counts[64:72, :] = jnp.broadcast_to(jnp.max(chunks, axis=0, keepdims=True), (8, TILE)).astype(I32)
    to_scalar = pltpu.make_async_copy(counts, counts_smem, sem)
    to_scalar.start()
    start_column = start[:, 0:1]
    wide = 1024

    def compact(step, carry):
        cols = pl.ds(pl.multiple_of(step * wide, wide), wide)
        head = ends[0:1, cols]
        tail = ends[1:2, cols]
        inside = (head >> 7) == (tail >> 7)
        bucket = jnp.where(inside, head >> 7, -1)
        base = jnp.sum(jnp.where(one_hot_rows(bucket, BLOCKS), start_column, 0.0), axis=0, keepdims=True)
        order = rank[:, cols].astype(I32)
        chunk = jnp.where(inside & (order >= TILE), base.astype(I32) + (order >> 7) - 1, -1)
        at_chunk = one_hot_rows(chunk, CHUNKS)
        values = ((head & 127).astype(F32), (tail & 127).astype(F32)) + parts2(cond[:, cols])
        stack = jnp.concatenate([spread(at_chunk, value) for value in values], axis=0)
        lanes = one_hot_lanes(order & 127, TILE)
        sums[...] += dot_nt(stack, lanes)
        return carry

    row_id = lax.broadcasted_iota(I32, (TILE, TILE), 0)
    lane_id = lax.broadcasted_iota(I32, (TILE, TILE), 1)

    def chunk_of(source, row, pitch):
        head = source[pl.ds(row, 1), :].astype(I32)
        tail = source[pl.ds(row + pitch, 1), :].astype(I32)
        at_head = row_id == head
        at_tail = row_id == tail
        left = jnp.concatenate([spread(at_head, 1.0), spread(at_tail, 1.0)], axis=1)
        right = []
        for k in range(2):
            value = source[pl.ds(row + (2 + k) * pitch, 1), :]
            right.append(jnp.concatenate([spread(at_tail, value), spread(at_head, value)], axis=1))
        both = dot_nt(left, jnp.concatenate(right, axis=0))
        return both[:, 0:TILE] + both[:, TILE:]

    def fill(step, carry):
        filled = []
        for i in range(FILLS):
            block = step * FILLS + i
            off = chunk_of(near, block, BLOCKS)
            filled.append(jnp.where(row_id == lane_id, degree_out[pl.ds(block, 1), :], -off))
        for i in range(FILLS):
            table[pl.ds(pl.multiple_of((step * FILLS + i) * TILE, TILE), TILE), :] = filled[i]
        return carry

    lax.fori_loop(0, BLOCKS // FILLS, fill, 0)
    to_scalar.wait()

    def refill(block, carry):
        rows = pl.ds(pl.multiple_of(block * TILE, TILE), TILE)

        def more(index, inner):
            table[rows, :] = table[rows, :] - chunk_of(sums, counts_smem[block, 0] + index, CHUNKS)
            return inner

        lax.fori_loop(0, counts_smem[block + BLOCKS, 0], more, 0)
        return carry

    @pl.when(counts_smem[64, 0] > 0)
    def _():
        sums[...] = jnp.zeros_like(sums)
        lax.fori_loop(0, INNER // wide, compact, 0)
        lax.fori_loop(0, BLOCKS, refill, 0)

    panel_lane = lax.broadcasted_iota(I32, (PANEL, TILE), 1)
    panel_row = lax.broadcasted_iota(I32, (PANEL, TILE), 0)
    own_block = (row_id // PANEL) == (lane_id // PANEL)
    lane_block = panel_lane & (PANEL - 1)
    lane_group = panel_lane // PANEL

    def replicated(x, group):
        return jnp.take_along_axis(x, lane_block + group * PANEL, axis=1, mode="promise_in_bounds")

    def panel(index, carry):
        base = pl.multiple_of(index * PANEL, PANEL)
        for b in range(BLOCKS):
            old_rows[b * PITCH : b * PITCH + PANEL, :] = table[pl.ds(b * TILE + base, PANEL), :]
        for i in range(8):
            lines = [old_rows[pl.ds(8 * h + i, BLOCKS, stride=PITCH), :] for h in range(4)]
            turned_rows[i] = jnp.concatenate(lines, axis=0).T
        state = [turned_rows[i, pl.ds(base, PANEL), :] for i in range(8)]
        for first in range(0, PANEL, 4):
            coming = [replicated(state[(first + d) % 8], (first + d) // 8) for d in range(4)]
            for d in range(4):
                t = first + d
                at_row = panel_row == t
                now = coming[d]
                pivot = 1.0 / now[t : t + 1, :]
                new = jnp.where(at_row, pivot, now * pivot)
                for e in range(d + 1, 4):
                    x = coming[e]
                    coming[e] = jnp.where(at_row, 0.0, x) - x[t : t + 1, :] * new
                for i in range(8):
                    x = state[i]
                    rest = jnp.where(at_row, 0.0, x) - x[t : t + 1, :] * new
                    state[i] = jnp.where(lane_group == t // 8, new, rest) if i == t % 8 else rest
        for i in range(8):
            back = jnp.concatenate([state[i]] * 4, axis=0).T
            for h in range(4):
                small[pl.ds(8 * h + i, BLOCKS, stride=PITCH), :] = back[PANEL * h : PANEL * h + PANEL, :]
        unit = jnp.where(panel_lane == panel_row + base, 1.0, 0.0)
        in_panel = (panel_lane >= base) & (panel_lane < base + PANEL)
        keep = ((lane_id >= base) & (lane_id < base + PANEL)) | ((row_id >= base) & (row_id < base + PANEL))
        for g in range(BLOCKS // FOUR):
            starts = [PITCH * (g * FOUR + i) for i in range(FOUR)]
            diagonal = jnp.where(own_block, jnp.concatenate([small[at : at + PANEL, :] for at in starts], axis=0), 0.0)
            members = [jnp.where(in_panel, unit, old_rows[at : at + PANEL, :]) for at in starts]
            stack = jnp.concatenate(members, axis=0)
            dh, dm = [part.astype(BF16) for part in parts2(diagonal)]
            sh, sm = [part.astype(BF16) for part in parts2(stack)]
            def crossed(high, low):
                return jnp.concatenate([jnp.concatenate([high, low], axis=1), jnp.concatenate([low, high], axis=1)], axis=0)

            fresh = dot_nn(jnp.concatenate([dh, dm], axis=1), crossed(sh, sm))
            fresh = fresh[:, 0:TILE] + fresh[:, TILE:]
            turned = stack.T
            turned = jnp.where(row_id < base + PANEL, -turned, turned)
            parts = [part.astype(BF16) for part in parts2(turned)]
            fh, fm = [part.astype(BF16) for part in parts2(fresh)]
            none = jnp.zeros((TILE, TILE), BF16)
            left = [jnp.concatenate([jnp.where((lane_id // PANEL) == i, part, none) for part in parts], axis=1) for i in range(FOUR)]
            update = dot_nn(jnp.concatenate(left, axis=0), crossed(fh, fm))
            update = update[:, 0:TILE] + update[:, TILE:]
            for i in range(FOUR):
                rows = slice((g * FOUR + i) * TILE, (g * FOUR + i + 1) * TILE)
                table[rows, :] = jnp.where(keep, 0.0, table[rows, :]) - update[TILE * i : TILE * i + TILE, :]
        return carry

    lax.fori_loop(0, TILE // PANEL, panel, 0)

    for block in range(BLOCKS):
        inverse[block] = table[block * TILE : (block + 1) * TILE, :].astype(BF16)


def solve_kernel(
    sizes, inflow, mask, ends, cond, degree, inverse, shown, pressure, mean,
    table, owner8, cond8, basis, images, residual, pair, upper_pair, out, back_out, fwd_out, fwd_in, back_src, back_in,
    one_buf, two_buf, rep_buf,
    fwd_send, fwd_recv, back_send, back_recv, one_send, one_recv, two_send, two_recv, rep_send, rep_recv,
):
    parts, depth_z, planes, reps = sizes
    place = lax.axis_index("dom")
    mine = lax.axis_index("rep")
    upper = lax.rem(place + 1, parts)
    lower = lax.rem(place + parts - 1, parts)
    core = lax.rem(place, 2)
    column = lax.rem(lax.div(place, 2), depth_z)
    line = lax.div(place, 2 * depth_z)
    seat = line * 2 + core

    def plane_place(other):
        return (lax.div(other, 2) * depth_z + column) * 2 + lax.rem(other, 2)

    def column_place(other):
        return (line * depth_z + other) * 2 + core

    barrier = pltpu.get_barrier_semaphore()
    partners = [{"dom": upper}, {"dom": lower}]
    partners += [{"dom": plane_place(lax.rem(seat + o, planes))} for o in range(1, planes)]
    partners += [{"dom": column_place(lax.rem(column + o, depth_z))} for o in range(1, depth_z)]
    partners += [{"rep": lax.rem(mine + o, reps)} for o in range(1, reps)]
    for partner in partners:
        pl.semaphore_signal(barrier, inc=1, device_id=partner, device_id_type=MESH)

    wide = 256

    def make(step, carry):
        cols = pl.ds(pl.multiple_of(step * wide, wide), wide)
        value = jnp.broadcast_to(cond[:, cols], (8, wide))
        cond8[:, cols] = value
        for side in range(2):
            node = ends[side : side + 1, cols]
            into = pl.ds(pl.multiple_of(side * SEGS + step * wide, wide), wide)
            table[:, into] = one_hot_lanes(node & 255, 256)
            owner8[:, into] = jnp.broadcast_to(node >> 8, (8, wide))
        return carry

    lax.fori_loop(0, SEGS // wide, make, 0, unroll=4)

    def split_into(target, tile, pairs):
        rows = 8 * pairs
        for q in range(0, pairs, 2):
            highs, lows = [], []
            for half in range(2):
                parts = [parts2(tile(2 * (q + i) + half)) for i in range(2)]
                highs.append(jnp.concatenate([part[0] for part in parts], axis=0))
                lows.append(jnp.concatenate([part[1] for part in parts], axis=0))
            target[8 * q : 8 * q + 16, :] = jnp.concatenate(highs, axis=1).astype(BF16)
            target[rows + 8 * q : rows + 8 * q + 16, :] = jnp.concatenate(lows, axis=1).astype(BF16)

    def gather(source, cols, pairs, both):
        full = dot_nn(source[...] if both else source[0 : 8 * pairs, :], table[:, cols])
        owner = owner8[:, cols]
        result = jnp.zeros((8, wide), F32)
        for q in range(pairs):
            value = full[8 * q : 8 * q + 8, :]
            if both:
                value = value + full[8 * (q + pairs) : 8 * (q + pairs) + 8, :]
            result = jnp.where(owner == q, value, result)
        return result

    def scatter(values, cols, pairs):
        left, right = [], []
        for value, at in zip(values, cols):
            owner = owner8[:, at]
            left.append(jnp.concatenate([jnp.where(owner == q, part, 0.0) for part in parts2(value) for q in range(pairs)], axis=0).astype(BF16))
            right.append(table[:, at])
        return dot_nt(jnp.concatenate(left, axis=1), jnp.concatenate(right, axis=1))

    def tile_of(source, b, pairs):
        rows, lanes = 8 * (b // 2), slice(TILE * (b % 2), TILE * (b % 2) + TILE)
        return source[rows : rows + 8, lanes] + source[8 * pairs + rows : 8 * pairs + rows + 8, lanes]

    pairs_all = BLOCKS // 2
    pairs_shown = SHOWN // 2

    def head_cols(step):
        return pl.ds(pl.multiple_of(step * wide, wide), wide)

    def tail_cols(step):
        return pl.ds(pl.multiple_of(SEGS + step * wide, wide), wide)

    def precondition(k):
        for b in range(BLOCKS):
            field = residual[8 * b : 8 * b + 8, :].astype(BF16)
            value = dot_nn(field, inverse[b])
            if k == 1:
                value = value.astype(BF16).astype(F32)
            basis[k, 8 * b : 8 * b + 8, :] = value

    for b in range(BLOCKS):
        weight = inflow_weight * mask[b : b + 1, :].astype(F32)
        residual[8 * b : 8 * b + 8, :] = weight * inflow[:, TILE * b : TILE * b + TILE]
    precondition(0)

    lane = lax.broadcasted_iota(I32, (8, TILE), 1)
    moments = jnp.zeros((8, TILE), F32)

    def total_of(k, other):
        accs = [jnp.zeros((8, TILE), F32)] * 4
        for b in range(BLOCKS):
            accs[b % 4] = accs[b % 4] + basis[k, 8 * b : 8 * b + 8, :] * other(b)
        return jnp.sum((accs[0] + accs[1]) + (accs[2] + accs[3]), axis=1, keepdims=True)

    def right_side(b):
        weight = inflow_weight * mask[b : b + 1, :].astype(F32)
        return weight * inflow[:, TILE * b : TILE * b + TILE]

    junc_first = INNER // wide
    junc_steps = JUNC // wide
    for k in range(3):
        split_into(pair, lambda b: basis[k, 8 * b : 8 * b + 8, :], pairs_all)
        for j in range(SHOWN):
            wanted = jnp.full((8, TILE), shown[j], I32)
            tile = jnp.zeros((8, TILE), F32)
            for b in range(BLOCKS):
                tile = jnp.where(wanted == b, basis[k, 8 * b : 8 * b + 8, :], tile)
            fwd_out[k, 8 * j : 8 * j + 8, :] = tile
        if k == 0:
            pl.semaphore_wait(barrier, len(partners))
        forward = pltpu.make_async_remote_copy(
            src_ref=fwd_out.at[k], dst_ref=fwd_in.at[k], send_sem=fwd_send.at[k], recv_sem=fwd_recv.at[k],
            device_id={"dom": lower}, device_id_type=MESH,
        )
        forward.start()
        moments = jnp.where(lane == k, total_of(k, right_side), moments)
        if k < 2:
            hcols = [head_cols(junc_first + step) for step in range(junc_steps)]
            tcols = [tail_cols(junc_first + step) for step in range(junc_steps)]
            back_out[...] = scatter([cond8[:, at] * gather(pair, at, pairs_all, k == 0) for at in hcols], tcols, pairs_shown)
            for j in range(SHOWN):
                back_src[k, 8 * j : 8 * j + 8, :] = tile_of(back_out, j, pairs_shown)
            backward = pltpu.make_async_remote_copy(
                src_ref=back_src.at[k], dst_ref=back_in.at[k], send_sem=back_send.at[k], recv_sem=back_recv.at[k],
                device_id={"dom": upper}, device_id_type=MESH,
            )
            backward.start()
            out[...] = jnp.zeros_like(out)

            def inner(step, carry):
                values, cols = [], []
                for i in range(UNROLL):
                    h, t = head_cols(UNROLL * step + i), tail_cols(UNROLL * step + i)
                    weight = cond8[:, h]
                    values += [weight * gather(pair, t, pairs_all, k == 0), weight * gather(pair, h, pairs_all, k == 0)]
                    cols += [h, t]
                out[...] += scatter(values, cols, pairs_all)
                return carry

            lax.fori_loop(0, INNER // wide // UNROLL, inner, 0)
            forward.wait()
            split_into(upper_pair, lambda j: fwd_in[k, 8 * j : 8 * j + 8, :], pairs_shown)
            out[...] += scatter([cond8[:, h] * gather(upper_pair, t, pairs_shown, k == 0) for h, t in zip(hcols, tcols)], hcols, pairs_all)
            backward.wait()
            for b in range(BLOCKS):
                acc = tile_of(out, b, pairs_all)
                for j in range(SHOWN):
                    acc = acc + jnp.where(jnp.full((8, TILE), shown[j], I32) == b, back_in[k, 8 * j : 8 * j + 8, :], 0.0)
                image = degree[b : b + 1, :] * basis[k, 8 * b : 8 * b + 8, :] - acc
                images[k, 8 * b : 8 * b + 8, :] = image
                residual[8 * b : 8 * b + 8, :] = residual[8 * b : 8 * b + 8, :] - image
            precondition(k + 1)
            moments = jnp.where(lane == 3 + k, total_of(k, lambda b: images[k, 8 * b : 8 * b + 8, :]), moments)
            moments = jnp.where(lane == 6 + k, total_of(k + 1, lambda b: images[k, 8 * b : 8 * b + 8, :]), moments)
        else:
            def quadratic(step, carry):
                for i in range(UNROLL):
                    h, t = head_cols(UNROLL * step + i), tail_cols(UNROLL * step + i)
                    carry = carry + cond8[:, h] * gather(pair, h, pairs_all, k == 0) * gather(pair, t, pairs_all, k == 0)
                return carry

            crossed = lax.fori_loop(0, INNER // wide // UNROLL, quadratic, jnp.zeros((8, wide), F32))
            ahead = [cond8[:, head_cols(junc_first + step)] * gather(pair, head_cols(junc_first + step), pairs_all, k == 0) for step in range(junc_steps)]
            forward.wait()
            split_into(upper_pair, lambda j: fwd_in[k, 8 * j : 8 * j + 8, :], pairs_shown)
            for step in range(junc_steps):
                crossed = crossed + ahead[step] * gather(upper_pair, tail_cols(junc_first + step), pairs_shown, k == 0)
            square = total_of(2, lambda b: degree[b : b + 1, :] * basis[2, 8 * b : 8 * b + 8, :])
            square = square - 2.0 * jnp.sum(crossed, axis=1, keepdims=True)
            moments = jnp.where(lane == 5, square, moments)
            moments = jnp.where(lane == 8, total_of(2, lambda b: images[0, 8 * b : 8 * b + 8, :]), moments)

    def exchange(buffer, send, recv, index, count, target):
        copies = []
        for o in range(1, count):
            other = lax.rem(index + o, count)
            copies.append(pltpu.make_async_remote_copy(
                src_ref=buffer.at[index], dst_ref=buffer.at[index], send_sem=send.at[o], recv_sem=recv.at[o],
                device_id=target(other), device_id_type=MESH,
            ))
        for copy in copies:
            copy.start()
        for copy in copies:
            copy.wait()
        acc = buffer[0]
        for o in range(1, count):
            acc = acc + buffer[o]
        return acc

    one_buf[seat] = moments
    moments = exchange(one_buf, one_send, one_recv, seat, planes, lambda other: {"dom": plane_place(other)})
    two_buf[column] = moments
    moments = exchange(two_buf, two_send, two_recv, column, depth_z, lambda other: {"dom": column_place(other)})

    def entry(index):
        return jnp.broadcast_to(moments[:, index : index + 1], (8, TILE))

    b0, b1, b2, g00, g11, g22, g01, g12, g02 = [entry(i) for i in range(9)]

    def safe_inverse(value, scale):
        good = value > 1e-6 * scale
        return jnp.where(good, 1.0 / jnp.where(good, value, 1.0), 0.0)

    i0 = safe_inverse(g00, g00)
    l10 = g01 * i0
    l20 = g02 * i0
    i1 = safe_inverse(g11 - l10 * g01, g11)
    c12 = g12 - l20 * g01
    l21 = c12 * i1
    i2 = safe_inverse(g22 - l20 * g02 - l21 * c12, g22)
    w1 = b1 - l10 * b0
    w2 = b2 - l20 * b0 - l21 * w1
    y2 = w2 * i2
    y1 = w1 * i1 - l21 * y2
    y0 = b0 * i0 - l10 * y1 - l20 * y2
    for b in range(BLOCKS):
        rows = slice(8 * b, 8 * b + 8)
        value = y0 * basis[0, rows, :] + y1 * basis[1, rows, :] + y2 * basis[2, rows, :]
        pressure[:, TILE * b : TILE * b + TILE] = value
        rep_buf[mine, b : b + 1, :] = jnp.sum(value, axis=0, keepdims=True)
    total = exchange(rep_buf, rep_send, rep_recv, mine, reps, lambda other: {"rep": other})
    mean[...] = total * (1.0 / SCEN_ALL)


def vmem(count):
    return [pl.BlockSpec(memory_space=pltpu.VMEM)] * count


def smem(count):
    return [pl.BlockSpec(memory_space=pltpu.SMEM)] * count


def setup_call(ends, cond, mask, shown, arrived):
    return pl.pallas_call(
        setup_kernel,
        out_shape=(jax.ShapeDtypeStruct((BLOCKS, TILE, TILE), BF16), jax.ShapeDtypeStruct((BLOCKS, TILE), F32)),
        in_specs=vmem(3) + smem(1) + vmem(1),
        out_specs=tuple(vmem(2)),
        scratch_shapes=[
            pltpu.VMEM((NODES, TILE), F32),
            pltpu.VMEM((1, INNER), F32),
            pltpu.VMEM((64, TILE), F32),
            pltpu.VMEM((4 * BLOCKS, TILE), F32),
            pltpu.VMEM((4 * CHUNKS, TILE), F32),
            pltpu.VMEM((72, TILE), I32),
            pltpu.VMEM((BLOCKS * PITCH, TILE), F32),
            pltpu.VMEM((8, TILE, TILE), F32),
            pltpu.VMEM((BLOCKS * PITCH, TILE), F32),
            pltpu.SMEM((72, TILE), I32),
            pltpu.SemaphoreType.DMA,
        ],
        name="inverses",
    )(ends, cond, mask, shown, arrived)


def per_device(sizes, inflow, mask, ends, live, shown, radius, length):
    parts, depth_z, planes, reps = sizes
    mask = mask.reshape(BLOCKS, TILE)
    dma = pltpu.SemaphoreType.DMA
    cond, arrived = pl.pallas_call(
        functools.partial(head_kernel, parts),
        out_shape=(jax.ShapeDtypeStruct((1, SEGS), F32), jax.ShapeDtypeStruct((SHOWN, TILE), F32)),
        in_specs=vmem(3) + smem(1),
        out_specs=tuple(vmem(2)),
        scratch_shapes=[pltpu.VMEM((SHOWN, TILE), F32), pltpu.VMEM((SHOWN, TILE), F32), dma, dma],
        compiler_params=pltpu.CompilerParams(collective_id=0, has_side_effects=True),
        name="conductances",
    )(ends, radius.reshape(1, SEGS), length.reshape(1, SEGS), live)
    inverse, degree = setup_call(ends, cond, mask, shown, arrived)
    rows = 8 * BLOCKS
    back = 8 * SHOWN
    pressure, mean = pl.pallas_call(
        functools.partial(solve_kernel, sizes),
        out_shape=(jax.ShapeDtypeStruct((8, NODES), F32), jax.ShapeDtypeStruct((BLOCKS, TILE), F32)),
        in_specs=vmem(6) + smem(1),
        out_specs=tuple(vmem(2)),
        scratch_shapes=[
            pltpu.VMEM((2 * TILE, 2 * SEGS), BF16),
            pltpu.VMEM((8, 2 * SEGS), I32),
            pltpu.VMEM((8, SEGS), F32),
            pltpu.VMEM((3, rows, TILE), F32),
            pltpu.VMEM((2, rows, TILE), F32),
            pltpu.VMEM((rows, TILE), F32),
            pltpu.VMEM((rows, 2 * TILE), BF16),
            pltpu.VMEM((back, 2 * TILE), BF16),
            pltpu.VMEM((rows, 2 * TILE), F32),
            pltpu.VMEM((back, 2 * TILE), F32),
            pltpu.VMEM((3, back, TILE), F32),
            pltpu.VMEM((3, back, TILE), F32),
            pltpu.VMEM((2, back, TILE), F32),
            pltpu.VMEM((2, back, TILE), F32),
            pltpu.VMEM((planes, 8, TILE), F32),
            pltpu.VMEM((depth_z, 8, TILE), F32),
            pltpu.VMEM((reps, BLOCKS, TILE), F32),
            dma((3,)), dma((3,)), dma((2,)), dma((2,)),
            dma((planes,)), dma((planes,)), dma((depth_z,)), dma((depth_z,)), dma((reps,)), dma((reps,)),
        ],
        compiler_params=pltpu.CompilerParams(collective_id=1, has_side_effects=True),
        name="gradients",
    )(inflow, mask, ends, cond, degree, inverse, shown)
    return pressure, mean.reshape(NODES)


def solution(mesh):
    in_specs = (P("rep", "dom"), P("dom"), P(None, "dom"), P("dom"), P("dom"), P("dom"), P("dom"))
    out_specs = (P("rep", "dom"), P("dom"))
    parts, reps = mesh.shape["dom"], mesh.shape["rep"]
    depth_z = 8 if parts == 64 else parts // 4
    sizes = (parts, depth_z, parts // depth_z, reps)
    return jax.shard_map(
        functools.partial(per_device, sizes), mesh=mesh, in_specs=in_specs, out_specs=out_specs, check_vma=False
    )
```
